32 devices in a mesh: seq: 8 (over z, x), head: 4 (over y, core).
Axes of the slice: x: 2, y: 2, z: 4, core: 2. Of those that a mesh axis runs over, the one named last changes fastest.
Arguments:
- queries: bfloat16 [2048, 2048], P('seq', 'head'), may hold values from -6 to 6
- keys: bfloat16 [2048, 1024], P('seq', 'head'), may hold values from -5 to 5
- values: bfloat16 [2048, 1024], P('seq', 'head'), may hold values from -6 to 6
- out_weight: bfloat16 [2048, 5376], P('head'), may hold values from -0.125 to 0.125
- out_grad: bfloat16 [2048, 5376], P(('seq', 'head')), may hold values from -6 to 6
Outputs:
- projected: bfloat16 [2048, 5376], P(('seq', 'head'))
- query_gradient: bfloat16 [2048, 2048], P('seq', 'head')
- key_gradient: bfloat16 [2048, 1024], P('seq', 'head')
- value_gradient: bfloat16 [2048, 1024], P('seq', 'head')
The draws below stay inside these ranges and needn't reach their ends.
All inputs are finite; a program needn't handle non-finite values.
Results may differ from the reference program's by a relative error of at most 0.018.
Values may be sent and summed in bfloat16 or wider, within the bound.
No kernel may reach another device: no remote copies, remote signals or barrier semaphores. Data moves between devices by JAX's collectives and lax.ppermute only.
A program may use at most 64 MiB of HBM per device.

```python
import jax
import jax.numpy as jnp
from jax import lax

D = 5376
QUERY_HEADS = 16
KEY_VALUE_HEADS = 8
HEAD_SIZE = 128
WIN = 1024
LOCAL_TOKENS = 256
TOKEN_COUNT = 2048
REACH = 4
N_HEAD = 4


def paired_draw(key):
    key_query = jax.random.fold_in(key, 101)
    key_random_keys = jax.random.fold_in(key, 202)
    query_vals = jnp.clip(jax.random.normal(key_query, (TOKEN_COUNT, QUERY_HEADS * HEAD_SIZE), jnp.float32), -6.0, 6.0)
    key_entries = jnp.clip(jax.random.normal(key_random_keys, (TOKEN_COUNT, KEY_VALUE_HEADS * HEAD_SIZE), jnp.float32), -5.0, 5.0)
    return (query_vals, key_entries)


def draw_queries(key, part):
    return paired_draw(key)[0].astype(jnp.bfloat16)


def draw_keys(key, part):
    return paired_draw(key)[1].astype(jnp.bfloat16)


def block_levels(key, extent, shards, least, high):
    def one(dim, parts):
        heights = jax.random.uniform(jax.random.fold_in(jax.random.fold_in(key, 6), dim), (parts,), jnp.float32, least / len(shards), high / len(shards))
        return jnp.repeat(jnp.exp(heights), extent[dim] // parts).reshape((-1,) + (1,) * (len(extent) - dim - 1))

    loudness = one(*shards[0])
    for cut in shards[1:]:
        loudness = loudness * one(*cut)
    return loudness


def bell_draw(stream_key, extent, width, limit, cuts=(), held_as=jnp.bfloat16):
    values = jax.random.normal(stream_key, extent, jnp.float32) * width
    if len(cuts) > 0:
        values = block_levels(stream_key, extent, cuts, -0.22, 0.18) * values
    return jnp.clip(values, min=-limit, max=limit).astype(held_as)


def setup_inputs(seed: int = 0) -> dict:
    arg_keys = jax.random.split(jax.random.key(seed), 6)
    return {
        "queries": draw_queries(jax.random.fold_in(arg_keys[5], 71), 0),
        "keys": draw_keys(jax.random.fold_in(arg_keys[5], 71), 0),
        "values": bell_draw(arg_keys[2], (TOKEN_COUNT, KEY_VALUE_HEADS * HEAD_SIZE), 1.0, 6.0, ((0, 8), (1, 4))),
        "out_weight": bell_draw(arg_keys[3], (QUERY_HEADS * HEAD_SIZE, D), (QUERY_HEADS * HEAD_SIZE) ** -0.5, 0.125, ((0, 4),)),
        "out_grad": bell_draw(arg_keys[4], (TOKEN_COUNT, D), 1.0, 6.0, ((0, 32),)),
    }


LOGIT_SCALE = 168.0 ** -0.5


def reference(queries, keys, values, out_weight, out_grad):
    window_behind = REACH * LOCAL_TOKENS
    window_rows = window_behind + LOCAL_TOKENS
    heads_per_group = QUERY_HEADS // KEY_VALUE_HEADS
    block_count = TOKEN_COUNT // LOCAL_TOKENS
    attended_gradient = jnp.dot(out_grad, out_weight.T, preferred_element_type=jnp.float32).astype(jnp.bfloat16)
    padding_rows = jnp.zeros((window_behind, KEY_VALUE_HEADS * HEAD_SIZE), keys.dtype)
    key_padded = jnp.concatenate([padding_rows, keys], 0)
    value_padded = jnp.concatenate([padding_rows, values], 0)

    def one_block(totals, block_index):
        key_total, value_total = totals
        leading_row = (block_index * LOCAL_TOKENS).astype(jnp.int32)
        query_block = lax.dynamic_slice_in_dim(queries, leading_row, LOCAL_TOKENS, 0).astype(jnp.float32).reshape(LOCAL_TOKENS, KEY_VALUE_HEADS, heads_per_group, HEAD_SIZE)
        key_block = lax.dynamic_slice_in_dim(key_padded, leading_row, window_rows, 0).astype(jnp.float32).reshape(window_rows, KEY_VALUE_HEADS, HEAD_SIZE)
        value_block = lax.dynamic_slice_in_dim(value_padded, leading_row, window_rows, 0).astype(jnp.float32).reshape(window_rows, KEY_VALUE_HEADS, HEAD_SIZE)
        gradient_block = lax.dynamic_slice_in_dim(attended_gradient, leading_row, LOCAL_TOKENS, 0).astype(jnp.float32).reshape(LOCAL_TOKENS, KEY_VALUE_HEADS, heads_per_group, HEAD_SIZE)
        logit_scores = jnp.einsum("pfbo,vfo->fbpv", query_block, key_block) * LOGIT_SCALE
        query_pos = leading_row + jnp.arange(LOCAL_TOKENS, dtype=jnp.int32)[:, None]
        key_pos = leading_row - window_behind + jnp.arange(window_rows, dtype=jnp.int32)[None, :]
        distance = query_pos - key_pos
        allowed = (distance >= 0) & (distance < WIN) & (key_pos >= 0)
        logit_scores = jnp.where(allowed, logit_scores, -jnp.inf)
        row_max = jnp.max(logit_scores, axis=-1, keepdims=True)
        log_total = row_max + jnp.log(jnp.sum(jnp.exp(logit_scores - row_max), axis=-1, keepdims=True))
        attention_prob = lax.optimization_barrier(jnp.exp(logit_scores - log_total).astype(jnp.bfloat16))
        prob_wide = attention_prob.astype(jnp.float32)
        attended_rows = jnp.einsum("ebml,leh->mebh", prob_wide, value_block).astype(jnp.bfloat16)
        attended_rows = lax.optimization_barrier(attended_rows)
        row_delta = jnp.sum(gradient_block * attended_rows.astype(jnp.float32), axis=-1).transpose(1, 2, 0)[..., None]
        prob_gradient = jnp.einsum("pfbo,vfo->fbpv", gradient_block, value_block)
        score_gradient = lax.optimization_barrier((prob_wide * (prob_gradient - row_delta)).astype(jnp.bfloat16))
        score_wide = score_gradient.astype(jnp.float32)
        query_gradient = (jnp.einsum("ebml,leh->mebh", score_wide, key_block) * LOGIT_SCALE).astype(jnp.bfloat16)
        key_portion = jnp.einsum("cqiz,icqf->zcf", score_wide, query_block) * LOGIT_SCALE
        value_portion = jnp.einsum("cqiz,icqf->zcf", prob_wide, gradient_block)
        key_total = lax.dynamic_update_slice_in_dim(key_total, lax.dynamic_slice_in_dim(key_total, leading_row, window_rows, 0) + key_portion, leading_row, 0)
        value_total = lax.dynamic_update_slice_in_dim(value_total, lax.dynamic_slice_in_dim(value_total, leading_row, window_rows, 0) + value_portion, leading_row, 0)
        return (key_total, value_total), (attended_rows.reshape(LOCAL_TOKENS, QUERY_HEADS * HEAD_SIZE), query_gradient.reshape(LOCAL_TOKENS, QUERY_HEADS * HEAD_SIZE))

    initial_total = jnp.zeros((TOKEN_COUNT + window_behind, KEY_VALUE_HEADS, HEAD_SIZE), jnp.float32)
    (key_total, value_total), (attended_rows, query_gradient) = lax.scan(one_block, (initial_total, initial_total), jnp.arange(block_count, dtype=jnp.int32))
    attended_rows = attended_rows.reshape(TOKEN_COUNT, QUERY_HEADS * HEAD_SIZE)
    query_gradient = query_gradient.reshape(TOKEN_COUNT, QUERY_HEADS * HEAD_SIZE)
    group_cols = QUERY_HEADS * HEAD_SIZE // N_HEAD
    summed = jnp.zeros((TOKEN_COUNT, D), jnp.float32)
    for group_index in range(N_HEAD):
        lower = group_index * group_cols
        partial_out = jnp.dot(attended_rows[:, lower:lower + group_cols], out_weight[lower:lower + group_cols], preferred_element_type=jnp.float32)
        partial_out = lax.optimization_barrier(partial_out.astype(jnp.bfloat16))
        summed = summed + partial_out.astype(jnp.float32)
    key_gradient = key_total[window_behind:].reshape(TOKEN_COUNT, KEY_VALUE_HEADS * HEAD_SIZE).astype(jnp.bfloat16)
    value_gradient = value_total[window_behind:].reshape(TOKEN_COUNT, KEY_VALUE_HEADS * HEAD_SIZE).astype(jnp.bfloat16)
    return (summed.astype(jnp.bfloat16), query_gradient, key_gradient, value_gradient)
```

```python
import jax
import jax.numpy as jnp
from jax import lax
from jax.experimental import pallas as pl
from jax.experimental.pallas import tpu as pltpu
from jax.sharding import PartitionSpec as P

HEAD_SIZE = 128
WIN = 1024
LOGIT_SCALE = 168.0 ** (-0.5)
LOG2E = 1.4426950408889634
NEG = -1e30
F32 = jnp.float32
BF16 = jnp.bfloat16
VMEM = pl.BlockSpec(memory_space=pltpu.VMEM)


def dot(a, b, ca, cb):
    return lax.dot_general(a, b, (((ca,), (cb,)), ((), ())), preferred_element_type=F32)


def shifted(value, steps):
    count = lax.axis_size("seq")
    first, last = (max(0, -steps), min(count, count - steps))
    return lax.ppermute(value, "seq", [(i, i + steps) for i in range(first, last)])


def swapped(value, axis, bit):
    count = lax.axis_size(axis)
    return lax.ppermute(value, axis, [(i, i ^ bit) for i in range(count)])


def to_parity(value, parity):
    count = lax.axis_size("seq")
    return lax.ppermute(value, "seq", [(i ^ 1, i) for i in range(parity, count, 2)])


def group_rows(group, head, size):
    return pl.ds(pl.multiple_of(jnp.bitwise_xor(group, head) * size, size), size)


def stacked(mat, kv_head):
    low = 2 * kv_head * HEAD_SIZE
    return jnp.concatenate([mat[:, low : low + HEAD_SIZE], mat[:, low + HEAD_SIZE : low + 2 * HEAD_SIZE]], 0)


def forward_kernel(q_ref, k_ref, v_ref, r1_ref, r2_ref, x1_ref, p0_ref, x2_ref, o_ref, p_ref):
    seq, head = lax.axis_index("seq"), lax.axis_index("head")
    odd = lax.rem(seq, 2) == 1
    tok = q_ref.shape[0]
    kv_heads = k_ref.shape[1] // HEAD_SIZE
    kv_cols = k_ref.shape[1]
    size = tok // 4
    q_rel = jnp.concatenate([q_ref[group_rows(g, head, size), :] for g in range(4)], 0)
    key_pos = lax.broadcasted_iota(jnp.int32, (tok, 2 * tok), 0)
    lane = lax.broadcasted_iota(jnp.int32, (tok, 2 * tok), 1)
    query_pos = jnp.bitwise_xor(jnp.bitwise_and(lane, tok - 1), head * size)
    causal = query_pos >= key_pos
    near = jnp.where(seq >= 2, 0.0, NEG).astype(F32)
    far = jnp.where(seq >= 4, 0.0, NEG).astype(F32)
    mixed = jnp.where(jnp.logical_or(odd, seq >= 4), 0.0, NEG).astype(F32)
    biases = [None, near, far, near, mixed]
    scale = LOGIT_SCALE * LOG2E
    for g in range(kv_heads):
        kc = slice(g * HEAD_SIZE, (g + 1) * HEAD_SIZE)
        vc = slice(kv_cols + g * HEAD_SIZE, kv_cols + (g + 1) * HEAD_SIZE)
        qg = stacked(q_rel, g)
        key_blocks = [k_ref[:, kc], r1_ref[:, kc], r2_ref[:, kc], x1_ref[:, kc], jnp.where(odd, p0_ref[:, kc], x2_ref[:, kc])]
        value_blocks = [v_ref[:, kc], r1_ref[:, vc], r2_ref[:, vc], x1_ref[:, vc], jnp.where(odd, p0_ref[:, vc], x2_ref[:, vc])]
        scores = [dot(kb, qg, 1, 1) for kb in key_blocks]
        scores[0] = jnp.where(causal, scores[0], NEG)
        scores[2] = jnp.where(causal, NEG, scores[2])
        tops = [jnp.max(sb, axis=0, keepdims=True) for sb in scores]
        tops = [t if b is None else t + b for t, b in zip(tops, biases)]
        top = tops[0]
        for t in tops[1:]:
            top = jnp.maximum(top, t)
        top = top * scale
        probs = [jnp.exp2(sb * scale - (top if b is None else top - b)) for sb, b in zip(scores, biases)]
        total = sum(jnp.sum(pb, axis=0, keepdims=True) for pb in probs)
        inv = 1.0 / total
        out = jnp.zeros((HEAD_SIZE, 2 * tok), F32)
        for b in range(5):
            pb = (probs[b] * inv).astype(BF16)
            p_ref[g, b] = pb
            out = out + dot(value_blocks[b], pb, 0, 0)
        out = out.T.astype(BF16)
        low = 2 * g * HEAD_SIZE
        o_ref[:, low : low + HEAD_SIZE] = out[:tok]
        o_ref[:, low + HEAD_SIZE : low + 2 * HEAD_SIZE] = out[tok:]


def backward_kernel(q_ref, k_ref, v_ref, r1_ref, r2_ref, x1_ref, p0_ref, x2_ref, p_ref, o_ref, d0_ref, d1_ref,
                    dq_ref, town_ref, t1_ref, t2_ref, tx_ref, tz_ref):
    seq, head = lax.axis_index("seq"), lax.axis_index("head")
    odd = lax.rem(seq, 2) == 1
    tok = q_ref.shape[0]
    kv_cols = k_ref.shape[1]
    kv_heads = kv_cols // HEAD_SIZE
    size = tok // 4
    q_rel = jnp.concatenate([q_ref[group_rows(g, head, size), :] for g in range(4)], 0)
    do_rel = jnp.concatenate([d0_ref[...], d1_ref[...]], 0)
    o_rel = o_ref[...]
    outs = [town_ref, t1_ref, t2_ref, tx_ref, tz_ref]
    for g in range(kv_heads):
        kc = slice(g * HEAD_SIZE, (g + 1) * HEAD_SIZE)
        vc = slice(kv_cols + g * HEAD_SIZE, kv_cols + (g + 1) * HEAD_SIZE)
        qg, dg, og = stacked(q_rel, g), stacked(do_rel, g), stacked(o_rel, g)
        key_blocks = [k_ref[:, kc], r1_ref[:, kc], r2_ref[:, kc], x1_ref[:, kc], jnp.where(odd, p0_ref[:, kc], x2_ref[:, kc])]
        value_blocks = [v_ref[:, kc], r1_ref[:, vc], r2_ref[:, vc], x1_ref[:, vc], jnp.where(odd, p0_ref[:, vc], x2_ref[:, vc])]
        delta = jnp.sum((dg.astype(F32) * og.astype(F32)).T, axis=0, keepdims=True)
        dq = jnp.zeros((HEAD_SIZE, 2 * tok), F32)
        for b in range(5):
            pb = p_ref[g, b]
            dp = dot(value_blocks[b], dg, 1, 1)
            ds = (pb.astype(F32) * (dp - delta)).astype(BF16)
            outs[b][:, vc] = dot(pb, dg, 1, 0).astype(outs[b].dtype)
            outs[b][:, kc] = (dot(ds, qg, 1, 0) * LOGIT_SCALE).astype(outs[b].dtype)
            dq = dq + dot(key_blocks[b], ds, 0, 0)
        dq = (dq * LOGIT_SCALE).T.astype(BF16)
        low = 2 * g * HEAD_SIZE
        for r in range(4):
            rows = group_rows(r, head, size)
            dq_ref[rows, low : low + HEAD_SIZE] = dq[r * size : (r + 1) * size]
            dq_ref[rows, low + HEAD_SIZE : low + 2 * HEAD_SIZE] = dq[tok + r * size : tok + (r + 1) * size]


def per_device(queries, keys, values, out_weight, out_grad):
    tok, q_cols = queries.shape
    kv_cols = keys.shape[1]
    kv_heads = kv_cols // HEAD_SIZE
    odd = lax.rem(lax.axis_index("seq"), 2) == 1
    params = pltpu.CompilerParams(vmem_limit_bytes=32 << 20)

    og_y = swapped(out_grad, "head", 2)
    own_kv = jnp.concatenate([keys, values], 1)
    r1 = shifted(own_kv, 2)
    p0 = to_parity(own_kv, 1)
    og_c = swapped(out_grad, "head", 1)
    r2 = shifted(r1, 2)
    x1 = swapped(r1, "seq", 1)
    x2 = to_parity(r2, 0)
    og_yc = swapped(og_y, "head", 1)

    attended, probs = pl.pallas_call(
        forward_kernel,
        out_shape=(
            jax.ShapeDtypeStruct((tok, q_cols), BF16),
            jax.ShapeDtypeStruct((kv_heads, 5, tok, 2 * tok), BF16),
        ),
        in_specs=[VMEM] * 8,
        out_specs=(VMEM, VMEM),
        compiler_params=params,
        name="attend",
    )(queries, keys, values, r1, r2, x1, p0, x2)

    half, size = tok // 2, tok // 4
    far_part = jnp.dot(attended[half:], out_weight, preferred_element_type=F32).astype(BF16)
    sent = swapped(far_part[size:], "head", 1)
    far_sum = (far_part[:size].astype(F32) + sent.astype(F32)).astype(BF16)
    near_part = jnp.dot(attended[:half], out_weight, preferred_element_type=F32).astype(BF16)
    from_y = swapped(far_sum, "head", 2)
    from_core = swapped(near_part[size:], "head", 1)
    projected = (near_part[:size].astype(F32) + from_core.astype(F32) + from_y.astype(F32)).astype(BF16)

    def back(rows):
        return dot(rows, out_weight, 1, 1).astype(BF16)

    near_grad = back(jnp.concatenate([out_grad, og_c], 0))
    far_grad = back(jnp.concatenate([og_y, og_yc], 0))

    block = jax.ShapeDtypeStruct((tok, 2 * kv_cols), BF16)
    query_gradient, t_own, t_1, t_2, t_x, t_z = pl.pallas_call(
        backward_kernel,
        out_shape=(
            jax.ShapeDtypeStruct((tok, q_cols), BF16),
            jax.ShapeDtypeStruct((tok, 2 * kv_cols), F32),
            block, block, block, block,
        ),
        in_specs=[VMEM] * 12,
        out_specs=(VMEM,) * 6,
        compiler_params=params,
        name="attend_grad",
    )(queries, keys, values, r1, r2, x1, p0, x2, probs, attended, near_grad, far_grad)

    def wide(a):
        return a.astype(F32)

    g = swapped(t_z, "seq", 1)
    zero = jnp.zeros_like(g)
    c1 = shifted((wide(t_2) + wide(jnp.where(odd, g, zero))).astype(BF16), -2)
    d1 = swapped(t_x, "seq", 1)
    e1 = shifted((wide(t_1) + wide(c1) + wide(d1)).astype(BF16), -2)
    own = (t_own + wide(e1) + wide(jnp.where(odd, zero, g))).astype(BF16)
    return (projected, query_gradient, own[:, :kv_cols], own[:, kv_cols:])


def solution(mesh):
    return jax.shard_map(
        per_device,
        mesh=mesh,
        in_specs=(
            P("seq", "head"),
            P("seq", "head"),
            P("seq", "head"),
            P("head", None),
            P(("seq", "head"), None),
        ),
        out_specs=(P(("seq", "head"), None), P("seq", "head"), P("seq", "head"), P("seq", "head")),
        check_vma=False,
    )
```

```python
import jax
import jax.numpy as jnp
from jax import lax
from jax.experimental import pallas as pl
from jax.experimental.pallas import tpu as pltpu
from jax.sharding import PartitionSpec as P

HEAD_SIZE = 128
WIN = 1024
LOGIT_SCALE = 168.0 ** (-0.5)
LOG2E = 1.4426950408889634
NEG = -1e30
F32 = jnp.float32
BF16 = jnp.bfloat16
SMALL = pl.CostEstimate(flops=1, bytes_accessed=1, transcendentals=0)
VMEM = pl.BlockSpec(memory_space=pltpu.VMEM)


def dot(a, b, ca, cb):
    return lax.dot_general(a, b, (((ca,), (cb,)), ((), ())), preferred_element_type=F32)


def shifted(value, steps):
    count = lax.axis_size("seq")
    first, last = (max(0, -steps), min(count, count - steps))
    return lax.ppermute(value, "seq", [(i, i + steps) for i in range(first, last)])


def swapped(value, axis, bit):
    count = lax.axis_size(axis)
    return lax.ppermute(value, axis, [(i, i ^ bit) for i in range(count)])


def to_parity(value, parity):
    count = lax.axis_size("seq")
    return lax.ppermute(value, "seq", [(i ^ 1, i) for i in range(parity, count, 2)])


def group_rows(group, head, size):
    return pl.ds(pl.multiple_of(jnp.bitwise_xor(group, head) * size, size), size)


def stacked(mat, kv_head):
    low = 2 * kv_head * HEAD_SIZE
    return jnp.concatenate([mat[:, low : low + HEAD_SIZE], mat[:, low + HEAD_SIZE : low + 2 * HEAD_SIZE]], 0)


def forward_kernel(q_ref, k_ref, v_ref, r1_ref, r2_ref, x1_ref, p0k_ref, p0v_ref, x2_ref, w_ref,
                   o_ref, p_ref, near_own_ref, near_core_ref, far_own_ref, far_core_ref):
    seq, head = lax.axis_index("seq"), lax.axis_index("head")
    odd = lax.rem(seq, 2) == 1
    tok = q_ref.shape[0]
    kv_heads = k_ref.shape[1] // HEAD_SIZE
    kv_cols = k_ref.shape[1]
    size = tok // 4
    q_rel = jnp.concatenate([q_ref[group_rows(g, head, size), :] for g in range(4)], 0)
    key_pos = lax.broadcasted_iota(jnp.int32, (tok, 2 * tok), 0)
    lane = lax.broadcasted_iota(jnp.int32, (tok, 2 * tok), 1)
    query_pos = jnp.bitwise_xor(jnp.bitwise_and(lane, tok - 1), head * size)
    causal = query_pos >= key_pos
    near = jnp.where(seq >= 2, 0.0, NEG).astype(F32)
    far = jnp.where(seq >= 4, 0.0, NEG).astype(F32)
    mixed = jnp.where(jnp.logical_or(odd, seq >= 4), 0.0, NEG).astype(F32)
    biases = [None, near, far, near, mixed]
    scale = LOGIT_SCALE * LOG2E
    for g in range(kv_heads):
        kc = slice(g * HEAD_SIZE, (g + 1) * HEAD_SIZE)
        vc = slice(kv_cols + g * HEAD_SIZE, kv_cols + (g + 1) * HEAD_SIZE)
        qg = stacked(q_rel, g)
        key_blocks = [k_ref[:, kc], r1_ref[:, kc], r2_ref[:, kc], x1_ref[:, kc], jnp.where(odd, p0k_ref[:, kc], x2_ref[:, kc])]
        value_blocks = [v_ref[:, kc], r1_ref[:, vc], r2_ref[:, vc], x1_ref[:, vc], jnp.where(odd, p0v_ref[:, kc], x2_ref[:, vc])]
        scores = [dot(kb, qg, 1, 1) for kb in key_blocks]
        scores[0] = jnp.where(causal, scores[0], NEG)
        scores[2] = jnp.where(causal, NEG, scores[2])
        tops = [jnp.max(sb, axis=0, keepdims=True) for sb in scores]
        tops = [t if b is None else t + b for t, b in zip(tops, biases)]
        top = tops[0]
        for t in tops[1:]:
            top = jnp.maximum(top, t)
        top = top * scale
        probs = [jnp.exp2(sb * scale - (top if b is None else top - b)) for sb, b in zip(scores, biases)]
        total = sum(jnp.sum(pb, axis=0, keepdims=True) for pb in probs)
        inv = 1.0 / total
        out = jnp.zeros((HEAD_SIZE, 2 * tok), F32)
        for b in range(5):
            pb = (probs[b] * inv).astype(BF16)
            p_ref[g, b] = pb
            out = out + dot(value_blocks[b], pb, 0, 0)
        out = out.T.astype(BF16)
        low = 2 * g * HEAD_SIZE
        o_ref[:, low : low + HEAD_SIZE] = out[:tok]
        o_ref[:, low + HEAD_SIZE : low + 2 * HEAD_SIZE] = out[tok:]
    project(o_ref[...], w_ref, (near_own_ref, near_core_ref, far_own_ref, far_core_ref))


def project(rows, w_ref, part_refs):
    size = part_refs[0].shape[0]
    cols = w_ref.shape[1]
    step = cols // 7 if cols % (7 * HEAD_SIZE) == 0 else cols
    for low in range(0, cols, step):
        part = dot(rows, w_ref[:, low : low + step], 1, 0).astype(BF16)
        for i, ref in enumerate(part_refs):
            ref[:, low : low + step] = part[i * size : (i + 1) * size]


def back_kernel(own_ref, core_ref, y_ref, yc_ref, w_ref, d_ref):
    rows = jnp.concatenate([own_ref[...], core_ref[...], y_ref[...], yc_ref[...]], 0)
    d_ref[...] = dot(rows, w_ref[...], 1, 1).astype(BF16)


def backward_kernel(q_ref, k_ref, v_ref, r1_ref, r2_ref, x1_ref, p0k_ref, p0v_ref, x2_ref, p_ref, o_ref, d_ref,
                    dq_ref, town_ref, t1_ref, t2_ref, tx_ref, tz_ref):
    seq, head = lax.axis_index("seq"), lax.axis_index("head")
    odd = lax.rem(seq, 2) == 1
    tok = q_ref.shape[0]
    kv_cols = k_ref.shape[1]
    kv_heads = kv_cols // HEAD_SIZE
    size = tok // 4
    q_rel = jnp.concatenate([q_ref[group_rows(g, head, size), :] for g in range(4)], 0)
    do_rel = d_ref[...]
    o_rel = o_ref[...]
    outs = [town_ref, t1_ref, t2_ref, tx_ref, tz_ref]
    for g in range(kv_heads):
        kc = slice(g * HEAD_SIZE, (g + 1) * HEAD_SIZE)
        vc = slice(kv_cols + g * HEAD_SIZE, kv_cols + (g + 1) * HEAD_SIZE)
        qg, dg, og = stacked(q_rel, g), stacked(do_rel, g), stacked(o_rel, g)
        key_blocks = [k_ref[:, kc], r1_ref[:, kc], r2_ref[:, kc], x1_ref[:, kc], jnp.where(odd, p0k_ref[:, kc], x2_ref[:, kc])]
        value_blocks = [v_ref[:, kc], r1_ref[:, vc], r2_ref[:, vc], x1_ref[:, vc], jnp.where(odd, p0v_ref[:, kc], x2_ref[:, vc])]
        delta = jnp.sum((dg.astype(F32) * og.astype(F32)).T, axis=0, keepdims=True)
        dq = jnp.zeros((HEAD_SIZE, 2 * tok), F32)
        for b in range(5):
            pb = p_ref[g, b]
            dp = dot(value_blocks[b], dg, 1, 1)
            ds = (pb.astype(F32) * (dp - delta)).astype(BF16)
            outs[b][:, vc] = dot(pb, dg, 1, 0).astype(outs[b].dtype)
            outs[b][:, kc] = (dot(ds, qg, 1, 0) * LOGIT_SCALE).astype(outs[b].dtype)
            dq = dq + dot(key_blocks[b], ds, 0, 0)
        dq = (dq * LOGIT_SCALE).T.astype(BF16)
        low = 2 * g * HEAD_SIZE
        for r in range(4):
            rows = group_rows(r, head, size)
            dq_ref[rows, low : low + HEAD_SIZE] = dq[r * size : (r + 1) * size]
            dq_ref[rows, low + HEAD_SIZE : low + 2 * HEAD_SIZE] = dq[tok + r * size : tok + (r + 1) * size]


def per_device(queries, keys, values, out_weight, out_grad):
    tok, q_cols = queries.shape
    kv_cols = keys.shape[1]
    kv_heads = kv_cols // HEAD_SIZE
    odd = lax.rem(lax.axis_index("seq"), 2) == 1
    params = pltpu.CompilerParams(vmem_limit_bytes=16 << 20)

    def wide(a):
        return a.astype(F32)

    def gate(value, *others):
        return lax.optimization_barrier((value, *others))[0]

    r1_parts = [shifted(keys, 2), shifted(values, 2)]
    p0_parts = [to_parity(keys, 1), to_parity(values, 1)]
    og_y = swapped(out_grad, "head", 2)
    og_c = swapped(out_grad, "head", 1)
    r1 = jnp.concatenate(r1_parts, 1)
    r1 = gate(r1, *p0_parts)
    r2 = shifted(r1, 2)
    x1 = swapped(r1, "seq", 1)
    x2 = to_parity(gate(r2, x1), 0)
    og_yc = swapped(gate(og_y, r2, x1), "head", 1)
    half, size = tok // 2, tok // 4
    rows = jax.ShapeDtypeStruct((size, out_weight.shape[1]), BF16)
    attended_grad = pl.pallas_call(
        back_kernel,
        out_shape=jax.ShapeDtypeStruct((tok, q_cols), BF16),
        in_specs=[VMEM] * 5,
        out_specs=VMEM,
        compiler_params=params,
        cost_estimate=SMALL,
        name="turn_back",
    )(out_grad, og_c, og_y, og_yc, out_weight)

    attended, probs, near_own, near_core, far_own, far_core = pl.pallas_call(
        forward_kernel,
        out_shape=(
            jax.ShapeDtypeStruct((tok, q_cols), BF16),
            jax.ShapeDtypeStruct((kv_heads, 5, tok, 2 * tok), BF16),
            rows, rows, rows, rows,
        ),
        in_specs=[VMEM] * 10,
        out_specs=(VMEM,) * 6,
        compiler_params=params,
        cost_estimate=SMALL,
        name="attend",
    )(gate(queries, attended_grad), keys, values, r1, r2, x1, *p0_parts, x2, out_weight)
    sent = swapped(far_core, "head", 1)
    cuts = (0, size * 3 // 8, size * 3 // 4, size)
    far_sums = [(wide(far_own[i:j]) + wide(sent[i:j])).astype(BF16) for i, j in zip(cuts, cuts[1:])]
    from_y = [swapped(part, "head", 2) for part in far_sums]

    block = jax.ShapeDtypeStruct((tok, 2 * kv_cols), BF16)
    query_gradient, t_own, t_1, t_2, t_x, t_z = pl.pallas_call(
        backward_kernel,
        out_shape=(
            jax.ShapeDtypeStruct((tok, q_cols), BF16),
            jax.ShapeDtypeStruct((tok, 2 * kv_cols), F32),
            block, block, block, block,
        ),
        in_specs=[VMEM] * 12,
        out_specs=(VMEM,) * 6,
        compiler_params=params,
        cost_estimate=SMALL,
        name="attend_grad",
    )(queries, keys, values, r1, r2, x1, *p0_parts, x2, probs, attended, attended_grad)

    g = swapped(gate(t_z, *far_sums), "seq", 1)
    d1 = swapped(gate(t_x, g), "seq", 1)
    zero = jnp.zeros_like(g)
    c1 = shifted(gate((wide(t_2) + wide(jnp.where(odd, g, zero))).astype(BF16), from_y[0]), -2)
    from_core = swapped(gate(near_core, g), "head", 1)
    e1 = shifted(gate((wide(t_1) + wide(c1) + wide(d1)).astype(BF16), from_y[1]), -2)
    kept = jnp.where(odd, zero, g)

    def total(cols):
        return (t_own[:, cols] + wide(e1[:, cols]) + wide(kept[:, cols])).astype(BF16)

    projected = (wide(near_own) + wide(from_core) + wide(jnp.concatenate(from_y, 0))).astype(BF16)
    return (projected, query_gradient, total(slice(0, kv_cols)), total(slice(kv_cols, 2 * kv_cols)))


def solution(mesh):
    return jax.shard_map(
        per_device,
        mesh=mesh,
        in_specs=(
            P("seq", "head"),
            P("seq", "head"),
            P("seq", "head"),
            P("head", None),
            P(("seq", "head"), None),
        ),
        out_specs=(P(("seq", "head"), None), P("seq", "head"), P("seq", "head"), P("seq", "head")),
        check_vma=False,
    )
```

```python
import jax
import jax.numpy as jnp
from jax import lax
from jax.experimental import pallas as pl
from jax.experimental.pallas import tpu as pltpu
from jax.sharding import PartitionSpec as P

HEAD_SIZE = 128
WIN = 1024
LOGIT_SCALE = 168.0 ** (-0.5)
LOG2E = 1.4426950408889634
NEG = -1e30
FAR = 4
F32 = jnp.float32
BF16 = jnp.bfloat16
SMALL = pl.CostEstimate(flops=1, bytes_accessed=1, transcendentals=0)
VMEM = pl.BlockSpec(memory_space=pltpu.VMEM)


def dot(a, b, ca, cb):
    return lax.dot_general(a, b, (((ca,), (cb,)), ((), ())), preferred_element_type=F32)


def shifted(value, steps):
    count = lax.axis_size("seq")
    first, last = (max(0, -steps), min(count, count - steps))
    return lax.ppermute(value, "seq", [(i, i + steps) for i in range(first, last)])


def swapped(value, axis, bit):
    count = lax.axis_size(axis)
    return lax.ppermute(value, axis, [(i, i ^ bit) for i in range(count)])


def far_swapped(lower, upper):
    count = lax.axis_size("seq")
    side = lax.rem(lax.div(lax.axis_index("seq"), FAR), 2)
    rounds = []
    for r in range(2):
        pairs = [(i, i + FAR) for i in range(count - FAR) if (i // FAR) % 2 == r]
        if pairs:
            pairs = pairs + [(j, i) for i, j in pairs]
            rounds.append(lax.ppermute(lower() if lower is upper else jnp.where(side == r, lower(), upper()), "seq", pairs))
    if len(rounds) == 1:
        return rounds[0], rounds[0]
    return jnp.where(side == 1, rounds[0], rounds[1]), jnp.where(side == 0, rounds[0], rounds[1])


def group_rows(group, head, size):
    return pl.ds(pl.multiple_of(jnp.bitwise_xor(group, head) * size, size), size)


def own_order(ref, head):
    size = ref.shape[0] // 4
    return jnp.concatenate([ref[group_rows(g, head, size), :] for g in range(4)], 0)


def stacked(mat, kv_head):
    low = 2 * kv_head * HEAD_SIZE
    return jnp.concatenate([mat[:, low : low + HEAD_SIZE], mat[:, low + HEAD_SIZE : low + 2 * HEAD_SIZE]], 0)


def causal_mask(tok, head):
    key_pos = lax.broadcasted_iota(jnp.int32, (tok, 2 * tok), 0)
    lane = lax.broadcasted_iota(jnp.int32, (tok, 2 * tok), 1)
    query_pos = jnp.bitwise_xor(jnp.bitwise_and(lane, tok - 1), head * (tok // 4))
    return query_pos >= key_pos


def columns(kv_cols, kv_head):
    low = kv_head * HEAD_SIZE
    return slice(low, low + HEAD_SIZE), slice(kv_cols + low, kv_cols + low + HEAD_SIZE)


def window(kv_ref, r1_ref, r2_ref, x1_ref, p0_ref, x2_ref, odd, cols):
    return [kv_ref[:, cols], r1_ref[:, cols], r2_ref[:, cols], x1_ref[:, cols], jnp.where(odd, p0_ref[:, cols], x2_ref[:, cols])]


def join_kernel(k_ref, v_ref, q_ref, kv_ref, sent_ref):
    lower = lax.rem(lax.div(lax.axis_index("seq"), FAR), 2) == 0
    kv = jnp.concatenate([k_ref[...], v_ref[...]], 1)
    kv_ref[...] = kv
    sent_ref[...] = jnp.where(lower, kv, q_ref[...])


def forward_kernel(q_ref, kv_ref, r1_ref, r2_ref, x1_ref, p0_ref, x2_ref, d_ref, w_ref,
                   p_ref, stat_ref, near_own_ref, near_core_ref, far_own_ref, far_core_ref, o_ref):
    seq, head = lax.axis_index("seq"), lax.axis_index("head")
    odd = lax.rem(seq, 2) == 1
    tok = q_ref.shape[0]
    kv_cols = kv_ref.shape[1] // 2
    q_rel = own_order(q_ref, head)
    causal = causal_mask(tok, head)
    near = jnp.where(seq >= 2, 0.0, NEG).astype(F32)
    far = jnp.where(seq >= 4, 0.0, NEG).astype(F32)
    mixed = jnp.where(jnp.logical_or(odd, seq >= 4), 0.0, NEG).astype(F32)
    biases = [None, near, far, near, mixed]
    scale = LOGIT_SCALE * LOG2E
    stats = []
    for g in range(kv_cols // HEAD_SIZE):
        kc, vc = columns(kv_cols, g)
        qg = stacked(q_rel, g)
        blocks = (kv_ref, r1_ref, r2_ref, x1_ref, p0_ref, x2_ref)
        key_blocks, value_blocks = window(*blocks, odd, kc), window(*blocks, odd, vc)
        scores = [dot(kb, qg, 1, 1) for kb in key_blocks]
        scores[0] = jnp.where(causal, scores[0], NEG)
        scores[2] = jnp.where(causal, NEG, scores[2])
        tops = [jnp.max(sb, axis=0, keepdims=True) for sb in scores]
        tops = [t if b is None else t + b for t, b in zip(tops, biases)]
        top = tops[0]
        for t in tops[1:]:
            top = jnp.maximum(top, t)
        top = top * scale
        probs = [jnp.exp2(sb * scale - (top if b is None else top - b)) for sb, b in zip(scores, biases)]
        total = sum(jnp.sum(pb, axis=0, keepdims=True) for pb in probs)
        inv = 1.0 / total
        out = jnp.zeros((HEAD_SIZE, 2 * tok), F32)
        for b in range(5):
            pb = (probs[b] * inv).astype(BF16)
            p_ref[g, b] = pb
            out = out + dot(value_blocks[b], pb, 0, 0)
        out = out.astype(BF16)
        grad = stacked(d_ref[...], g)
        delta = jnp.sum(grad.astype(F32).T * out.astype(F32), axis=0, keepdims=True)
        stats += [top + jnp.log2(total), delta]
        out = out.astype(F32).T.astype(BF16)
        low = 2 * g * HEAD_SIZE
        o_ref[:, low : low + HEAD_SIZE] = out[:tok]
        o_ref[:, low + HEAD_SIZE : low + 2 * HEAD_SIZE] = out[tok:]
    spare = stat_ref.shape[0] - len(stats)
    stat_ref[...] = jnp.concatenate(stats + [jnp.zeros((spare, 2 * tok), F32)], 0)
    project(o_ref[...], w_ref, (near_own_ref, near_core_ref, far_own_ref, far_core_ref))


def project(rows, w_ref, part_refs):
    size = part_refs[0].shape[0]
    cols = w_ref.shape[1]
    step = cols // 7 if cols % (7 * HEAD_SIZE) == 0 else cols
    for low in range(0, cols, step):
        part = dot(rows, w_ref[:, low : low + step], 1, 0).astype(BF16)
        for i, ref in enumerate(part_refs):
            ref[:, low : low + step] = part[i * size : (i + 1) * size]


def back_kernel(own_ref, core_ref, y_ref, yc_ref, w_ref, d_ref):
    rows = jnp.concatenate([own_ref[...], core_ref[...], y_ref[...], yc_ref[...]], 0)
    d_ref[...] = dot(rows, w_ref[...], 1, 1).astype(BF16)


def backward_kernel(q_ref, kv_ref, r1_ref, r2_ref, x1_ref, p0_ref, x2_ref, p_ref, stat_ref, d_ref,
                    dq_ref, town_ref, t1_ref, tx_ref, tz_ref):
    seq, head = lax.axis_index("seq"), lax.axis_index("head")
    odd = lax.rem(seq, 2) == 1
    tok = q_ref.shape[0]
    kv_cols = kv_ref.shape[1] // 2
    size = tok // 4
    q_rel = own_order(q_ref, head)
    outs = [town_ref, t1_ref, None, tx_ref, tz_ref]
    for g in range(kv_cols // HEAD_SIZE):
        kc, vc = columns(kv_cols, g)
        qg, dg = stacked(q_rel, g), stacked(d_ref[...], g)
        blocks = (kv_ref, r1_ref, r2_ref, x1_ref, p0_ref, x2_ref)
        key_blocks, value_blocks = window(*blocks, odd, kc), window(*blocks, odd, vc)
        delta = stat_ref[2 * g + 1 : 2 * g + 2, :]
        dq = jnp.zeros((HEAD_SIZE, 2 * tok), F32)
        for b in range(5):
            pb = p_ref[g, b]
            dp = dot(value_blocks[b], dg, 1, 1)
            ds = (pb.astype(F32) * (dp - delta)).astype(BF16)
            if outs[b] is not None:
                outs[b][:, vc] = dot(pb, dg, 1, 0).astype(outs[b].dtype)
                outs[b][:, kc] = (dot(ds, qg, 1, 0) * LOGIT_SCALE).astype(outs[b].dtype)
            dq = dq + dot(key_blocks[b], ds, 0, 0)
        dq = (dq * LOGIT_SCALE).T.astype(BF16)
        low = 2 * g * HEAD_SIZE
        for r in range(4):
            rows = group_rows(r, head, size)
            dq_ref[rows, low : low + HEAD_SIZE] = dq[r * size : (r + 1) * size]
            dq_ref[rows, low + HEAD_SIZE : low + 2 * HEAD_SIZE] = dq[tok + r * size : tok + (r + 1) * size]


def far_kernel(kv_ref, qf_ref, df_ref, sf_ref, qx_ref, dx_ref, sx_ref, t_ref):
    seq, head = lax.axis_index("seq"), lax.axis_index("head")
    count = lax.axis_size("seq")
    tok = kv_ref.shape[0]
    kv_cols = kv_ref.shape[1] // 2
    straight = jnp.logical_and(jnp.logical_not(causal_mask(tok, head)), seq + FAR < count)
    across = jnp.logical_and(lax.rem(seq, 2) == 1, seq + FAR - 1 < count)
    sources = ((qf_ref, df_ref, sf_ref, straight), (qx_ref, dx_ref, sx_ref, across))
    sources = [(own_order(q, head), d[...], st, keep) for q, d, st, keep in sources]
    scale = LOGIT_SCALE * LOG2E
    for g in range(kv_cols // HEAD_SIZE):
        kc, vc = columns(kv_cols, g)
        key, value = kv_ref[:, kc], kv_ref[:, vc]
        dk = jnp.zeros((tok, HEAD_SIZE), F32)
        dv = jnp.zeros((tok, HEAD_SIZE), F32)
        for q_rel, d_rel, st, keep in sources:
            qg, dg = stacked(q_rel, g), stacked(d_rel, g)
            prob = jnp.exp2(dot(key, qg, 1, 1) * scale - st[2 * g : 2 * g + 1, :])
            prob = jnp.where(keep, prob, 0.0).astype(BF16)
            dp = dot(value, dg, 1, 1)
            ds = (prob.astype(F32) * (dp - st[2 * g + 1 : 2 * g + 2, :])).astype(BF16)
            dv = dv + dot(prob, dg, 1, 0)
            dk = dk + dot(ds, qg, 1, 0)
        t_ref[:, kc] = dk * LOGIT_SCALE
        t_ref[:, vc] = dv


def per_device(queries, keys, values, out_weight, out_grad):
    tok, q_cols = queries.shape
    kv_cols = keys.shape[1]
    kv_heads = kv_cols // HEAD_SIZE
    odd = lax.rem(lax.axis_index("seq"), 2) == 1
    half, size = tok // 2, tok // 4
    rows = jax.ShapeDtypeStruct((size, out_weight.shape[1]), BF16)
    block = jax.ShapeDtypeStruct((tok, 2 * kv_cols), BF16)
    wide_block = jax.ShapeDtypeStruct((tok, 2 * kv_cols), F32)

    def call(kernel, name, outs, scratch, *operands):
        return pl.pallas_call(
            kernel,
            out_shape=outs,
            in_specs=[VMEM] * len(operands),
            out_specs=jax.tree.map(lambda _: VMEM, outs),
            scratch_shapes=scratch,
            compiler_params=pltpu.CompilerParams(vmem_limit_bytes=16 << 20),
            cost_estimate=SMALL,
            name=name,
        )(*operands)

    def wide(a):
        return a.astype(F32)

    def gate(value, *others):
        return lax.optimization_barrier((value, *others))[0]

    og_y = swapped(out_grad, "head", 2)
    kv, far_sent = call(join_kernel, "join", (block, block), [], keys, values, queries)
    r1 = shifted(kv, 2)
    r2, q_far = far_swapped(lambda: kv, lambda: queries) if lax.axis_size("seq") > 2 * FAR else (far_swapped(*[lambda: far_sent] * 2))
    p0 = swapped(kv, "seq", 1)
    og_c = swapped(out_grad, "head", 1)
    x1 = swapped(gate(r1, p0), "seq", 1)
    x2 = swapped(r2 if r2 is q_far else jnp.where(odd, r2, q_far), "seq", 1)
    og_yc = swapped(gate(og_y, x1, r2), "head", 1)
    grad = call(back_kernel, "turn_back", jax.ShapeDtypeStruct((tok, q_cols), BF16), [], out_grad, og_c, og_y, og_yc, out_weight)

    def down(value):
        return far_swapped(*[lambda: value] * 2)[1]

    grad_far = down(grad)
    probs, stats, near_own, near_core, far_own, far_core = call(
        forward_kernel,
        "attend",
        (
            jax.ShapeDtypeStruct((kv_heads, 5, tok, 2 * tok), BF16),
            jax.ShapeDtypeStruct((8 * pl.cdiv(2 * kv_heads, 8), 2 * tok), F32),
            rows, rows, rows, rows,
        ),
        [pltpu.VMEM((tok, q_cols), BF16)],
        queries, kv, r1, r2, x1, p0, x2, grad, out_weight,
    )
    sent = swapped(far_core, "head", 1)
    stats_far = down(stats)
    far_sum = (wide(far_own) + wide(sent)).astype(BF16)
    from_y = swapped(far_sum, "head", 2)
    stats_x = swapped(stats_far, "seq", 1)
    grad_x = swapped(gate(grad_far, stats_x), "seq", 1)

    query_gradient, t_own, t_1, t_x, t_z = call(
        backward_kernel,
        "attend_grad",
        (jax.ShapeDtypeStruct((tok, q_cols), BF16), wide_block, block, block, block),
        [],
        queries, kv, r1, r2, x1, p0, x2, probs, stats, grad,
    )
    d1 = swapped(gate(t_x, far_sum), "seq", 1)
    e1 = shifted((wide(t_1) + wide(d1)).astype(BF16), -2)
    g = swapped(gate(t_z, d1), "seq", 1)
    from_core = swapped(gate(near_core, d1), "head", 1)
    t_far = call(far_kernel, "far_grad", wide_block, [], gate(kv, from_y), q_far, grad_far, stats_far, x2, grad_x, stats_x)

    def total(cols):
        kept = jnp.where(odd, 0.0, wide(g[:, cols]))
        return (t_own[:, cols] + t_far[:, cols] + wide(e1[:, cols]) + kept).astype(BF16)

    projected = (wide(near_own) + wide(from_core) + wide(from_y)).astype(BF16)
    return (projected, query_gradient, total(slice(0, kv_cols)), total(slice(kv_cols, 2 * kv_cols)))


def solution(mesh):
    return jax.shard_map(
        per_device,
        mesh=mesh,
        in_specs=(
            P("seq", "head"),
            P("seq", "head"),
            P("seq", "head"),
            P("head", None),
            P(("seq", "head"), None),
        ),
        out_specs=(P(("seq", "head"), None), P("seq", "head"), P("seq", "head"), P("seq", "head")),
        check_vma=False,
    )
```

```python
import jax
import jax.numpy as jnp
from jax import lax
from jax.experimental import pallas as pl
from jax.experimental.pallas import tpu as pltpu
from jax.sharding import PartitionSpec as P

HEAD_SIZE = 128
WIN = 1024
LOGIT_SCALE = 168.0 ** (-0.5)
LOG2E = 1.4426950408889634
NEG = -1e30
FAR = 4
F32 = jnp.float32
BF16 = jnp.bfloat16
SMALL = pl.CostEstimate(flops=1, bytes_accessed=1, transcendentals=0)
MEDIUM = pl.CostEstimate(flops=50 * 10**8, bytes_accessed=1, transcendentals=0)
LARGE = pl.CostEstimate(flops=10**10, bytes_accessed=1, transcendentals=0)
VMEM = pl.BlockSpec(memory_space=pltpu.VMEM)


def dot(a, b, ca, cb):
    return lax.dot_general(a, b, (((ca,), (cb,)), ((), ())), preferred_element_type=F32)


def shifted(value, steps):
    count = lax.axis_size("seq")
    first, last = (max(0, -steps), min(count, count - steps))
    return lax.ppermute(value, "seq", [(i, i + steps) for i in range(first, last)])


def swapped(value, axis, bit):
    count = lax.axis_size(axis)
    return lax.ppermute(value, axis, [(i, i ^ bit) for i in range(count)])


def far_swapped(lower, upper):
    count = lax.axis_size("seq")
    side = lax.rem(lax.div(lax.axis_index("seq"), FAR), 2)
    rounds = []
    for r in range(2):
        pairs = [(i, i + FAR) for i in range(count - FAR) if (i // FAR) % 2 == r]
        if pairs:
            pairs = pairs + [(j, i) for i, j in pairs]
            rounds.append(lax.ppermute(lower() if lower is upper else jnp.where(side == r, lower(), upper()), "seq", pairs))
    if len(rounds) == 1:
        return rounds[0], rounds[0]
    return jnp.where(side == 1, rounds[0], rounds[1]), jnp.where(side == 0, rounds[0], rounds[1])


def group_rows(group, head, size):
    return pl.ds(pl.multiple_of(jnp.bitwise_xor(group, head) * size, size), size)


def own_order(ref, head):
    size = ref.shape[0] // 4
    return jnp.concatenate([ref[group_rows(g, head, size), :] for g in range(4)], 0)


def stacked(mat, kv_head):
    low = 2 * kv_head * HEAD_SIZE
    return jnp.concatenate([mat[:, low : low + HEAD_SIZE], mat[:, low + HEAD_SIZE : low + 2 * HEAD_SIZE]], 0)


def causal_mask(tok, head):
    key_pos = lax.broadcasted_iota(jnp.int32, (tok, 2 * tok), 0)
    lane = lax.broadcasted_iota(jnp.int32, (tok, 2 * tok), 1)
    query_pos = jnp.bitwise_xor(jnp.bitwise_and(lane, tok - 1), head * (tok // 4))
    return query_pos >= key_pos


def columns(kv_cols, kv_head):
    low = kv_head * HEAD_SIZE
    return slice(low, low + HEAD_SIZE), slice(kv_cols + low, kv_cols + low + HEAD_SIZE)


def window(kv_ref, r1_ref, r2_ref, x1_ref, p0_ref, x2_ref, odd, cols):
    return [kv_ref[:, cols], r1_ref[:, cols], r2_ref[:, cols], x1_ref[:, cols], jnp.where(odd, p0_ref[:, cols], x2_ref[:, cols])]


def join_kernel(k_ref, v_ref, q_ref, kv_ref, sent_ref):
    lower = lax.rem(lax.div(lax.axis_index("seq"), FAR), 2) == 0
    kv = jnp.concatenate([k_ref[...], v_ref[...]], 1)
    kv_ref[...] = kv
    sent_ref[...] = jnp.where(lower, kv, q_ref[...])


def forward_kernel(q_ref, kv_ref, r1_ref, r2_ref, x1_ref, p0_ref, x2_ref, d_ref, w_ref,
                   p_ref, stat_ref, near_own_ref, near_core_ref, far_own_ref, far_core_ref, o_ref):
    seq, head = lax.axis_index("seq"), lax.axis_index("head")
    odd = lax.rem(seq, 2) == 1
    tok = q_ref.shape[0]
    kv_cols = kv_ref.shape[1] // 2
    q_rel = own_order(q_ref, head)
    causal = causal_mask(tok, head)
    near = jnp.where(seq >= 2, 0.0, NEG).astype(F32)
    far = jnp.where(seq >= 4, 0.0, NEG).astype(F32)
    mixed = jnp.where(jnp.logical_or(odd, seq >= 4), 0.0, NEG).astype(F32)
    biases = [None, near, far, near, mixed]
    scale = LOGIT_SCALE * LOG2E
    stats = []
    for g in range(kv_cols // HEAD_SIZE):
        kc, vc = columns(kv_cols, g)
        qg = stacked(q_rel, g)
        blocks = (kv_ref, r1_ref, r2_ref, x1_ref, p0_ref, x2_ref)
        key_blocks, value_blocks = window(*blocks, odd, kc), window(*blocks, odd, vc)
        scores = [dot(kb, qg, 1, 1) for kb in key_blocks]
        scores[0] = jnp.where(causal, scores[0], NEG)
        scores[2] = jnp.where(causal, NEG, scores[2])
        tops = [jnp.max(sb, axis=0, keepdims=True) for sb in scores]
        tops = [t if b is None else t + b for t, b in zip(tops, biases)]
        top = tops[0]
        for t in tops[1:]:
            top = jnp.maximum(top, t)
        top = top * scale
        probs = [jnp.exp2(sb * scale - (top if b is None else top - b)) for sb, b in zip(scores, biases)]
        total = sum(jnp.sum(pb, axis=0, keepdims=True) for pb in probs)
        inv = 1.0 / total
        out = jnp.zeros((HEAD_SIZE, 2 * tok), F32)
        for b in range(5):
            pb = (probs[b] * inv).astype(BF16)
            p_ref[g, b] = pb
            out = out + dot(value_blocks[b], pb, 0, 0)
        out = out.astype(BF16)
        grad = stacked(d_ref[...], g)
        delta = jnp.sum(grad.astype(F32).T * out.astype(F32), axis=0, keepdims=True)
        stats += [top + jnp.log2(total), delta]
        out = out.astype(F32).T.astype(BF16)
        low = 2 * g * HEAD_SIZE
        o_ref[:, low : low + HEAD_SIZE] = out[:tok]
        o_ref[:, low + HEAD_SIZE : low + 2 * HEAD_SIZE] = out[tok:]
    spare = stat_ref.shape[0] - len(stats)
    stat_ref[...] = jnp.concatenate(stats + [jnp.zeros((spare, 2 * tok), F32)], 0)
    project(o_ref[...], w_ref, (near_own_ref, near_core_ref, far_own_ref, far_core_ref))


def project(rows, w_ref, part_refs):
    size = part_refs[0].shape[0]
    cols = w_ref.shape[1]
    step = cols // 7 if cols % (7 * HEAD_SIZE) == 0 else cols
    for low in range(0, cols, step):
        part = dot(rows, w_ref[:, low : low + step], 1, 0).astype(BF16)
        for i, ref in enumerate(part_refs):
            ref[:, low : low + step] = part[i * size : (i + 1) * size]


def back_kernel(own_ref, core_ref, y_ref, yc_ref, w_ref, d_ref):
    rows = jnp.concatenate([own_ref[...], core_ref[...], y_ref[...], yc_ref[...]], 0)
    d_ref[...] = dot(rows, w_ref[...], 1, 1).astype(BF16)


def backward_kernel(q_ref, kv_ref, r1_ref, r2_ref, x1_ref, p0_ref, x2_ref, p_ref, stat_ref, d_ref,
                    dq_ref, town_ref, t1_ref, tx_ref, tz_ref):
    seq, head = lax.axis_index("seq"), lax.axis_index("head")
    odd = lax.rem(seq, 2) == 1
    tok = q_ref.shape[0]
    kv_cols = kv_ref.shape[1] // 2
    size = tok // 4
    q_rel = own_order(q_ref, head)
    outs = [town_ref, t1_ref, None, tx_ref, tz_ref]
    for g in range(kv_cols // HEAD_SIZE):
        kc, vc = columns(kv_cols, g)
        qg, dg = stacked(q_rel, g), stacked(d_ref[...], g)
        blocks = (kv_ref, r1_ref, r2_ref, x1_ref, p0_ref, x2_ref)
        key_blocks, value_blocks = window(*blocks, odd, kc), window(*blocks, odd, vc)
        delta = stat_ref[2 * g + 1 : 2 * g + 2, :]
        dq = jnp.zeros((HEAD_SIZE, 2 * tok), F32)
        for b in range(5):
            pb = p_ref[g, b]
            dp = dot(value_blocks[b], dg, 1, 1)
            ds = (pb.astype(F32) * (dp - delta)).astype(BF16)
            if outs[b] is not None:
                outs[b][:, vc] = dot(pb, dg, 1, 0).astype(outs[b].dtype)
                outs[b][:, kc] = (dot(ds, qg, 1, 0) * LOGIT_SCALE).astype(outs[b].dtype)
            dq = dq + dot(key_blocks[b], ds, 0, 0)
        dq = (dq * LOGIT_SCALE).T.astype(BF16)
        low = 2 * g * HEAD_SIZE
        for r in range(4):
            rows = group_rows(r, head, size)
            dq_ref[rows, low : low + HEAD_SIZE] = dq[r * size : (r + 1) * size]
            dq_ref[rows, low + HEAD_SIZE : low + 2 * HEAD_SIZE] = dq[tok + r * size : tok + (r + 1) * size]


def far_kernel(kv_ref, qf_ref, df_ref, sf_ref, qx_ref, dx_ref, sx_ref, t_ref):
    seq, head = lax.axis_index("seq"), lax.axis_index("head")
    count = lax.axis_size("seq")
    tok = kv_ref.shape[0]
    kv_cols = kv_ref.shape[1] // 2
    straight = jnp.logical_and(jnp.logical_not(causal_mask(tok, head)), seq + FAR < count)
    across = jnp.logical_and(lax.rem(seq, 2) == 1, seq + FAR - 1 < count)
    sources = ((qf_ref, df_ref, sf_ref, straight), (qx_ref, dx_ref, sx_ref, across))
    sources = [(own_order(q, head), d[...], st, keep) for q, d, st, keep in sources]
    scale = LOGIT_SCALE * LOG2E
    for g in range(kv_cols // HEAD_SIZE):
        kc, vc = columns(kv_cols, g)
        key, value = kv_ref[:, kc], kv_ref[:, vc]
        dk = jnp.zeros((tok, HEAD_SIZE), F32)
        dv = jnp.zeros((tok, HEAD_SIZE), F32)
        for q_rel, d_rel, st, keep in sources:
            qg, dg = stacked(q_rel, g), stacked(d_rel, g)
            prob = jnp.exp2(dot(key, qg, 1, 1) * scale - st[2 * g : 2 * g + 1, :])
            prob = jnp.where(keep, prob, 0.0).astype(BF16)
            dp = dot(value, dg, 1, 1)
            ds = (prob.astype(F32) * (dp - st[2 * g + 1 : 2 * g + 2, :])).astype(BF16)
            dv = dv + dot(prob, dg, 1, 0)
            dk = dk + dot(ds, qg, 1, 0)
        t_ref[:, kc] = dk * LOGIT_SCALE
        t_ref[:, vc] = dv


def sum_kernel(*refs):
    total = refs[0][...].astype(F32)
    for ref in refs[1:-1]:
        total = total + ref[...].astype(F32)
    refs[-1][...] = total.astype(refs[-1].dtype)


def finish_kernel(own_ref, far_ref, hop_ref, pair_ref, dk_ref, dv_ref):
    odd = lax.rem(lax.axis_index("seq"), 2) == 1
    total = own_ref[...] + far_ref[...] + hop_ref[...].astype(F32) + jnp.where(odd, 0.0, pair_ref[...].astype(F32))
    kv_cols = dk_ref.shape[1]
    dk_ref[...] = total[:, :kv_cols].astype(BF16)
    dv_ref[...] = total[:, kv_cols:].astype(BF16)


def per_device(queries, keys, values, out_weight, out_grad):
    tok, q_cols = queries.shape
    kv_cols = keys.shape[1]
    kv_heads = kv_cols // HEAD_SIZE
    odd = lax.rem(lax.axis_index("seq"), 2) == 1
    size = tok // 4
    rows = jax.ShapeDtypeStruct((size, out_weight.shape[1]), BF16)
    block = jax.ShapeDtypeStruct((tok, 2 * kv_cols), BF16)
    wide_block = jax.ShapeDtypeStruct((tok, 2 * kv_cols), F32)

    def call(kernel, name, outs, scratch, *operands, cost=SMALL):
        return pl.pallas_call(
            kernel,
            out_shape=outs,
            in_specs=[VMEM] * len(operands),
            out_specs=jax.tree.map(lambda _: VMEM, outs),
            scratch_shapes=scratch,
            compiler_params=pltpu.CompilerParams(vmem_limit_bytes=16 << 20),
            cost_estimate=cost,
            name=name,
        )(*operands)

    def gate(value, *others):
        return lax.optimization_barrier((value, *others))[0]

    og_y = swapped(out_grad, "head", 2)
    kv, far_sent = call(join_kernel, "join", (block, block), [], keys, values, queries)
    r1 = shifted(kv, 2)
    r2, q_far = far_swapped(lambda: kv, lambda: queries) if lax.axis_size("seq") > 2 * FAR else (far_swapped(*[lambda: far_sent] * 2))
    p0 = swapped(kv, "seq", 1)
    og_c = swapped(out_grad, "head", 1)
    x1 = swapped(gate(r1, p0), "seq", 1)
    x2 = swapped(r2 if r2 is q_far else jnp.where(odd, r2, q_far), "seq", 1)
    og_yc = swapped(gate(og_y, x1, r2), "head", 1)
    grad = call(back_kernel, "turn_back", jax.ShapeDtypeStruct((tok, q_cols), BF16), [], out_grad, og_c, og_y, og_yc, out_weight)

    def down(value):
        return far_swapped(*[lambda: value] * 2)[1]

    grad_far = [down(grad[:, : q_cols // 2]), down(grad[:, q_cols // 2 :])]
    probs, stats, near_own, near_core, far_own, far_core = call(
        forward_kernel,
        "attend",
        (
            jax.ShapeDtypeStruct((kv_heads, 5, tok, 2 * tok), BF16),
            jax.ShapeDtypeStruct((8 * pl.cdiv(2 * kv_heads, 8), 2 * tok), F32),
            rows, rows, rows, rows,
        ),
        [pltpu.VMEM((tok, q_cols), BF16)],
        queries, kv, r1, r2, x1, p0, x2, grad, out_weight,
    )
    sent = swapped(far_core, "head", 1)
    stats_far = down(stats)
    far_sum = call(sum_kernel, "far_sum", rows, [], far_own, sent)
    from_y = swapped(far_sum, "head", 2)
    stats_x = swapped(gate(stats_far, grad_far[1]), "seq", 1)
    first_far, grad_far = grad_far[0], jnp.concatenate(grad_far, 1)
    grad_x = swapped(grad_far, "seq", 1)

    query_gradient, t_own, t_1, t_x, t_z = call(
        backward_kernel,
        "attend_grad",
        (jax.ShapeDtypeStruct((tok, q_cols), BF16), wide_block, block, block, block),
        [],
        queries, kv, r1, r2, x1, p0, x2, probs, stats, gate(grad, first_far),
        cost=LARGE,
    )
    d1 = gate(swapped(gate(t_x, far_sum, stats_far), "seq", 1), stats_x)
    e1 = shifted(call(sum_kernel, "hop_sum", block, [], t_1, d1), -2)
    g = swapped(gate(t_z, d1), "seq", 1)
    from_core = swapped(gate(near_core, d1), "head", 1)
    t_far = call(far_kernel, "far_grad", wide_block, [], kv, q_far, grad_far, stats_far, x2, grad_x, stats_x, cost=MEDIUM)

    narrow = jax.ShapeDtypeStruct(keys.shape, BF16)
    key_gradient, value_gradient = call(finish_kernel, "finish", (narrow, narrow), [], t_own, t_far, e1, g)
    projected = call(sum_kernel, "projected", rows, [], near_own, from_core, from_y, cost=LARGE)
    return (projected, query_gradient, key_gradient, value_gradient)


def solution(mesh):
    return jax.shard_map(
        per_device,
        mesh=mesh,
        in_specs=(
            P("seq", "head"),
            P("seq", "head"),
            P("seq", "head"),
            P("head", None),
            P(("seq", "head"), None),
        ),
        out_specs=(P(("seq", "head"), None), P("seq", "head"), P("seq", "head"), P("seq", "head")),
        check_vma=False,
    )
```

```python
import jax
import jax.numpy as jnp
from jax import lax
from jax.experimental import pallas as pl
from jax.experimental.pallas import tpu as pltpu
from jax.sharding import PartitionSpec as P

HEAD_SIZE = 128
WIN = 1024
LOGIT_SCALE = 168.0 ** (-0.5)
LOG2E = 1.4426950408889634
NEG = -1e30
PACK = 16
FAR = 4
F32 = jnp.float32
BF16 = jnp.bfloat16
SMALL = pl.CostEstimate(flops=1, bytes_accessed=1, transcendentals=0)
MEDIUM = pl.CostEstimate(flops=35 * 10**8, bytes_accessed=1, transcendentals=0)
LARGE = pl.CostEstimate(flops=10**10, bytes_accessed=1, transcendentals=0)
VMEM = pl.BlockSpec(memory_space=pltpu.VMEM)


def dot(a, b, ca, cb):
    return lax.dot_general(a, b, (((ca,), (cb,)), ((), ())), preferred_element_type=F32)


def shifted(value, steps):
    count = lax.axis_size("seq")
    first, last = (max(0, -steps), min(count, count - steps))
    return lax.ppermute(value, "seq", [(i, i + steps) for i in range(first, last)])


def swapped(value, axis, bit):
    count = lax.axis_size(axis)
    return lax.ppermute(value, axis, [(i, i ^ bit) for i in range(count)])


def far_swapped(lower, upper):
    count = lax.axis_size("seq")
    side = lax.rem(lax.div(lax.axis_index("seq"), FAR), 2)
    rounds = []
    for r in range(2):
        pairs = [(i, i + FAR) for i in range(count - FAR) if (i // FAR) % 2 == r]
        if pairs:
            pairs = pairs + [(j, i) for i, j in pairs]
            rounds.append(lax.ppermute(lower() if lower is upper else jnp.where(side == r, lower(), upper()), "seq", pairs))
    if len(rounds) == 1:
        return rounds[0], rounds[0]
    return jnp.where(side == 1, rounds[0], rounds[1]), jnp.where(side == 0, rounds[0], rounds[1])


def group_rows(group, head, size):
    return pl.ds(pl.multiple_of(jnp.bitwise_xor(group, head) * size, size), size)


def own_order(ref, head):
    size = ref.shape[0] // 4
    return jnp.concatenate([ref[group_rows(g, head, size), :] for g in range(4)], 0)


def stacked(mat, kv_head):
    low = 2 * kv_head * HEAD_SIZE
    return jnp.concatenate([mat[:, low : low + HEAD_SIZE], mat[:, low + HEAD_SIZE : low + 2 * HEAD_SIZE]], 0)


def causal_mask(tok, head):
    key_pos = lax.broadcasted_iota(jnp.int32, (tok, 2 * tok), 0)
    lane = lax.broadcasted_iota(jnp.int32, (tok, 2 * tok), 1)
    query_pos = jnp.bitwise_xor(jnp.bitwise_and(lane, tok - 1), head * (tok // 4))
    return query_pos >= key_pos


def columns(kv_cols, kv_head):
    low = kv_head * HEAD_SIZE
    return slice(low, low + HEAD_SIZE), slice(kv_cols + low, kv_cols + low + HEAD_SIZE)


def window(kv_ref, r1_ref, r2_ref, x1_ref, p0_ref, x2_ref, odd, cols):
    return [kv_ref[:, cols], r1_ref[:, cols], r2_ref[:, cols], x1_ref[:, cols], jnp.where(odd, p0_ref[:, cols], x2_ref[:, cols])]


def join_kernel(k_ref, v_ref, q_ref, kv_ref, sent_ref):
    lower = lax.rem(lax.div(lax.axis_index("seq"), FAR), 2) == 0
    kv = jnp.concatenate([k_ref[...], v_ref[...]], 1)
    kv_ref[...] = kv
    sent_ref[...] = jnp.where(lower, kv, q_ref[...])


def forward_kernel(q_ref, kv_ref, r1_ref, r2_ref, x1_ref, p0_ref, x2_ref, dn_ref, df_ref, w_ref,
                   p_ref, stat_ref, second_ref, near_own_ref, near_core_ref, far_own_ref, far_core_ref, o_ref):
    seq, head = lax.axis_index("seq"), lax.axis_index("head")
    odd = lax.rem(seq, 2) == 1
    tok = q_ref.shape[0]
    kv_cols = kv_ref.shape[1] // 2
    q_rel = own_order(q_ref, head)
    d_rel = jnp.concatenate([dn_ref[...], df_ref[...]], 0)
    causal = causal_mask(tok, head)
    near = jnp.where(seq >= 2, 0.0, NEG).astype(F32)
    far = jnp.where(seq >= 4, 0.0, NEG).astype(F32)
    mixed = jnp.where(jnp.logical_or(odd, seq >= 4), 0.0, NEG).astype(F32)
    biases = [None, near, far, near, mixed]
    scale = LOGIT_SCALE * LOG2E
    stats = []
    for g in range(kv_cols // HEAD_SIZE):
        kc, vc = columns(kv_cols, g)
        qg = stacked(q_rel, g)
        blocks = (kv_ref, r1_ref, r2_ref, x1_ref, p0_ref, x2_ref)
        key_blocks, value_blocks = window(*blocks, odd, kc), window(*blocks, odd, vc)
        scores = [dot(kb, qg, 1, 1) for kb in key_blocks]
        scores[0] = jnp.where(causal, scores[0], NEG)
        scores[2] = jnp.where(causal, NEG, scores[2])
        tops = [jnp.max(sb, axis=0, keepdims=True) for sb in scores]
        tops = [t if b is None else t + b for t, b in zip(tops, biases)]
        top = tops[0]
        for t in tops[1:]:
            top = jnp.maximum(top, t)
        top = top * scale
        probs = [jnp.exp2(sb * scale - (top if b is None else top - b)) for sb, b in zip(scores, biases)]
        total = sum(jnp.sum(pb, axis=0, keepdims=True) for pb in probs)
        inv = 1.0 / total
        out = jnp.zeros((HEAD_SIZE, 2 * tok), F32)
        for b in range(5):
            pb = (probs[b] * inv).astype(BF16)
            p_ref[g, b] = pb
            out = out + dot(value_blocks[b], pb, 0, 0)
        out = out.astype(BF16)
        grad = stacked(d_rel, g)
        delta = jnp.sum(grad.astype(F32).T * out.astype(F32), axis=0, keepdims=True)
        stats += [top + jnp.log2(total), delta]
        out = out.astype(F32).T.astype(BF16)
        low = 2 * g * HEAD_SIZE
        o_ref[:, low : low + HEAD_SIZE] = out[:tok]
        o_ref[:, low + HEAD_SIZE : low + 2 * HEAD_SIZE] = out[tok:]
    spare = jnp.zeros((stat_ref.shape[0] - len(stats), 2 * tok), F32)
    stat_ref[...] = jnp.concatenate(stats + [spare], 0)
    half = d_rel.shape[1] // 2
    packed = jnp.concatenate([st[:, :tok] for st in stats] + [st[:, tok:] for st in stats], 0)
    packed = jnp.concatenate([packed, jnp.zeros((PACK - packed.shape[0], tok), F32)], 0)
    second_ref[:tok, :] = d_rel[:, half:]
    for part in range(3):
        rounded = packed.astype(BF16)
        second_ref[tok + part * PACK : tok + (part + 1) * PACK, :] = rounded
        packed = packed - rounded.astype(F32)
    project(o_ref[...], w_ref, (near_own_ref, near_core_ref, far_own_ref, far_core_ref))


def project(rows, w_ref, part_refs):
    size = part_refs[0].shape[0]
    cols = w_ref.shape[1]
    step = cols // 7 if cols % (7 * HEAD_SIZE) == 0 else cols
    for low in range(0, cols, step):
        part = dot(rows, w_ref[:, low : low + step], 1, 0).astype(BF16)
        for i, ref in enumerate(part_refs):
            ref[:, low : low + step] = part[i * size : (i + 1) * size]


def near_back_kernel(own_ref, core_ref, w_ref, d_ref):
    rows = jnp.concatenate([own_ref[...], core_ref[...]], 0)
    d_ref[...] = dot(rows, w_ref[...], 1, 1).astype(BF16)


def far_back_kernel(y_ref, yc_ref, w_ref, near_ref, d_ref, first_ref):
    rows = jnp.concatenate([y_ref[...], yc_ref[...]], 0)
    grad = dot(rows, w_ref[...], 1, 1).astype(BF16)
    d_ref[...] = grad
    cols = first_ref.shape[1]
    first_ref[...] = jnp.concatenate([near_ref[:, :cols], grad[:, :cols]], 0)


def backward_kernel(q_ref, kv_ref, r1_ref, r2_ref, x1_ref, p0_ref, x2_ref, p_ref, stat_ref, dn_ref, df_ref,
                    dq_ref, town_ref, t1_ref, tx_ref, tz_ref):
    seq, head = lax.axis_index("seq"), lax.axis_index("head")
    odd = lax.rem(seq, 2) == 1
    tok = q_ref.shape[0]
    kv_cols = kv_ref.shape[1] // 2
    size = tok // 4
    q_rel = own_order(q_ref, head)
    d_rel = jnp.concatenate([dn_ref[...], df_ref[...]], 0)
    outs = [town_ref, t1_ref, None, tx_ref, tz_ref]
    for g in range(kv_cols // HEAD_SIZE):
        kc, vc = columns(kv_cols, g)
        qg, dg = stacked(q_rel, g), stacked(d_rel, g)
        blocks = (kv_ref, r1_ref, r2_ref, x1_ref, p0_ref, x2_ref)
        key_blocks, value_blocks = window(*blocks, odd, kc), window(*blocks, odd, vc)
        delta = stat_ref[2 * g + 1 : 2 * g + 2, :]
        dq = jnp.zeros((HEAD_SIZE, 2 * tok), F32)
        for b in range(5):
            pb = p_ref[g, b]
            dp = dot(value_blocks[b], dg, 1, 1)
            ds = (pb.astype(F32) * (dp - delta)).astype(BF16)
            if outs[b] is not None:
                outs[b][:, vc] = dot(pb, dg, 1, 0).astype(outs[b].dtype)
                outs[b][:, kc] = (dot(ds, qg, 1, 0) * LOGIT_SCALE).astype(outs[b].dtype)
            dq = dq + dot(key_blocks[b], ds, 0, 0)
        dq = (dq * LOGIT_SCALE).T.astype(BF16)
        low = 2 * g * HEAD_SIZE
        for r in range(4):
            rows = group_rows(r, head, size)
            dq_ref[rows, low : low + HEAD_SIZE] = dq[r * size : (r + 1) * size]
            dq_ref[rows, low + HEAD_SIZE : low + 2 * HEAD_SIZE] = dq[tok + r * size : tok + (r + 1) * size]


def unpacked(second_ref, tok, kv_heads):
    parts = [second_ref[tok + i * PACK : tok + (i + 1) * PACK, :tok].astype(F32) for i in range(3)]
    packed = parts[0] + (parts[1] + parts[2])
    count = 2 * kv_heads
    return [jnp.concatenate([packed[i : i + 1], packed[count + i : count + i + 1]], 1) for i in range(count)]


def pair_kernel(t_ref, a_ref, b_ref, out_ref):
    tok, half = a_ref.shape
    odd = lax.rem(lax.axis_index("seq"), 2) == 1
    out_ref[:tok, :] = jnp.where(odd, t_ref[...], jnp.concatenate([a_ref[...], b_ref[:tok, :]], 1))
    out_ref[tok:, :half] = b_ref[tok:, :]
    out_ref[tok:, half:] = jnp.zeros((b_ref.shape[0] - tok, half), BF16)


def far_kernel(kv_ref, qf_ref, af_ref, bf_ref, qx_ref, px_ref, t_ref):
    seq, head = lax.axis_index("seq"), lax.axis_index("head")
    count = lax.axis_size("seq")
    tok = kv_ref.shape[0]
    kv_cols = kv_ref.shape[1] // 2
    kv_heads = kv_cols // HEAD_SIZE
    straight = jnp.logical_and(jnp.logical_not(causal_mask(tok, head)), seq + FAR < count)
    across = jnp.logical_and(lax.rem(seq, 2) == 1, seq + FAR - 1 < count)
    sources = [
        (own_order(qf_ref, head), jnp.concatenate([af_ref[...], bf_ref[:tok, :]], 1), unpacked(bf_ref, tok, kv_heads), straight),
        (own_order(qx_ref, head), px_ref[:tok, :], unpacked(px_ref, tok, kv_heads), across),
    ]
    scale = LOGIT_SCALE * LOG2E
    for g in range(kv_heads):
        kc, vc = columns(kv_cols, g)
        key, value = kv_ref[:, kc], kv_ref[:, vc]
        dk = jnp.zeros((tok, HEAD_SIZE), F32)
        dv = jnp.zeros((tok, HEAD_SIZE), F32)
        for q_rel, d_rel, stats, keep in sources:
            qg, dg = stacked(q_rel, g), stacked(d_rel, g)
            prob = jnp.exp2(dot(key, qg, 1, 1) * scale - stats[2 * g])
            prob = jnp.where(keep, prob, 0.0).astype(BF16)
            dp = dot(value, dg, 1, 1)
            ds = jnp.where(keep, prob.astype(F32) * (dp - stats[2 * g + 1]), 0.0).astype(BF16)
            dv = dv + dot(prob, dg, 1, 0)
            dk = dk + dot(ds, qg, 1, 0)
        t_ref[:, kc] = dk * LOGIT_SCALE
        t_ref[:, vc] = dv


def sum_kernel(*refs):
    total = refs[0][...].astype(F32)
    for ref in refs[1:-1]:
        total = total + ref[...].astype(F32)
    refs[-1][...] = total.astype(refs[-1].dtype)


def finish_kernel(own_ref, far_ref, hop_ref, pair_ref, dk_ref, dv_ref):
    odd = lax.rem(lax.axis_index("seq"), 2) == 1
    total = own_ref[...] + far_ref[...] + hop_ref[...].astype(F32) + jnp.where(odd, 0.0, pair_ref[: own_ref.shape[0], :].astype(F32))
    kv_cols = dk_ref.shape[1]
    dk_ref[...] = total[:, :kv_cols].astype(BF16)
    dv_ref[...] = total[:, kv_cols:].astype(BF16)


def per_device(queries, keys, values, out_weight, out_grad):
    tok, q_cols = queries.shape
    kv_cols = keys.shape[1]
    kv_heads = kv_cols // HEAD_SIZE
    odd = lax.rem(lax.axis_index("seq"), 2) == 1
    size = tok // 4
    rows = jax.ShapeDtypeStruct((size, out_weight.shape[1]), BF16)
    block = jax.ShapeDtypeStruct((tok, 2 * kv_cols), BF16)
    wide_block = jax.ShapeDtypeStruct((tok, 2 * kv_cols), F32)

    def call(kernel, name, outs, scratch, *operands, cost=SMALL):
        return pl.pallas_call(
            kernel,
            out_shape=outs,
            in_specs=[VMEM] * len(operands),
            out_specs=jax.tree.map(lambda _: VMEM, outs),
            scratch_shapes=scratch,
            compiler_params=pltpu.CompilerParams(vmem_limit_bytes=16 << 20),
            cost_estimate=cost,
            name=name,
        )(*operands)

    def gate(value, *others):
        return lax.optimization_barrier((value, *others))[0]

    og_y = swapped(out_grad, "head", 2)
    kv, far_sent = call(join_kernel, "join", (block, block), [], keys, values, queries)
    r1 = shifted(kv, 2)
    r2, q_far = far_swapped(lambda: kv, lambda: queries) if lax.axis_size("seq") > 2 * FAR else (far_swapped(*[lambda: far_sent] * 2))
    p0 = swapped(kv, "seq", 1)
    og_c = swapped(out_grad, "head", 1)
    half_grad = jax.ShapeDtypeStruct((tok // 2, q_cols), BF16)
    grad_near = call(near_back_kernel, "near_back", half_grad, [], out_grad, og_c, out_weight, cost=SMALL)
    x1 = swapped(gate(r1, p0), "seq", 1)
    x2 = swapped(r2 if r2 is q_far else jnp.where(odd, r2, q_far), "seq", 1)
    og_yc = swapped(gate(og_y, r1, r2, p0, grad_near), "head", 1)
    first = jax.ShapeDtypeStruct((tok, q_cols // 2), BF16)
    second = jax.ShapeDtypeStruct((tok + 3 * PACK, q_cols // 2), BF16)
    grad_far, sent_first = call(far_back_kernel, "far_back", (half_grad, first), [], gate(og_y, x1), og_yc, out_weight, grad_near,
                                cost=LARGE)

    def down(value):
        return far_swapped(*[lambda: value] * 2)[1]

    far_first = down(sent_first)
    probs, stats, sent_second, near_own, near_core, far_own, far_core = call(
        forward_kernel,
        "attend",
        (
            jax.ShapeDtypeStruct((kv_heads, 5, tok, 2 * tok), BF16),
            jax.ShapeDtypeStruct((8 * pl.cdiv(2 * kv_heads, 8), 2 * tok), F32),
            second, rows, rows, rows, rows,
        ),
        [pltpu.VMEM((tok, q_cols), BF16)],
        queries, kv, r1, r2, x1, p0, x2, grad_near, grad_far, out_weight,
    )
    sent = swapped(far_core, "head", 1)
    far_second = down(sent_second)
    far_sum = call(sum_kernel, "far_sum", rows, [], far_own, sent)
    from_y = swapped(far_sum, "head", 2)

    query_gradient, t_own, t_1, t_x, t_z = call(
        backward_kernel,
        "attend_grad",
        (jax.ShapeDtypeStruct((tok, q_cols), BF16), wide_block, block, block, block),
        [],
        queries, kv, r1, r2, x1, p0, x2, probs, stats, grad_near, gate(grad_far, far_first),
        cost=LARGE,
    )
    d1 = swapped(gate(t_x, far_sum), "seq", 1)
    e1 = shifted(call(sum_kernel, "hop_sum", block, [], t_1, d1), -2)
    pair = jax.ShapeDtypeStruct((second.shape[0], q_cols), BF16)
    pair = swapped(call(pair_kernel, "pair", pair, [], t_z, far_first, far_second), "seq", 1)
    from_core = swapped(gate(near_core, d1), "head", 1)
    t_far = call(far_kernel, "far_grad", wide_block, [],
                 kv, q_far, far_first, far_second, x2, pair, cost=MEDIUM)

    narrow = jax.ShapeDtypeStruct(keys.shape, BF16)
    key_gradient, value_gradient = call(finish_kernel, "finish", (narrow, narrow), [], t_own, t_far, e1, pair)
    projected = call(sum_kernel, "projected", rows, [], near_own, from_core, from_y, cost=LARGE)
    return (projected, query_gradient, key_gradient, value_gradient)


def solution(mesh):
    return jax.shard_map(
        per_device,
        mesh=mesh,
        in_specs=(
            P("seq", "head"),
            P("seq", "head"),
            P("seq", "head"),
            P("head", None),
            P(("seq", "head"), None),
        ),
        out_specs=(P(("seq", "head"), None), P("seq", "head"), P("seq", "head"), P("seq", "head")),
        check_vma=False,
    )
```

```python
import functools

import jax
import jax.numpy as jnp
from jax import lax
from jax.experimental import pallas as pl
from jax.experimental.pallas import tpu as pltpu
from jax.sharding import PartitionSpec as P

HEAD_SIZE = 128
WIN = 1024
LOGIT_SCALE = 168.0 ** (-0.5)
LOG2E = 1.4426950408889634
NEG = -1e30
PACK = 16
FAR = 4
F32 = jnp.float32
BF16 = jnp.bfloat16
SMALL = pl.CostEstimate(flops=1, bytes_accessed=1, transcendentals=0)
MEDIUM = pl.CostEstimate(flops=1 * 10**8, bytes_accessed=1, transcendentals=0)
LARGE = pl.CostEstimate(flops=10**10, bytes_accessed=1, transcendentals=0)
VMEM = pl.BlockSpec(memory_space=pltpu.VMEM)


def dot(a, b, ca, cb):
    return lax.dot_general(a, b, (((ca,), (cb,)), ((), ())), preferred_element_type=F32)


def shifted(value, steps):
    count = lax.axis_size("seq")
    first, last = (max(0, -steps), min(count, count - steps))
    return lax.ppermute(value, "seq", [(i, i + steps) for i in range(first, last)])


def swapped(value, axis, bit):
    count = lax.axis_size(axis)
    return lax.ppermute(value, axis, [(i, i ^ bit) for i in range(count)])


def far_swapped(lower, upper):
    count = lax.axis_size("seq")
    side = lax.rem(lax.div(lax.axis_index("seq"), FAR), 2)
    rounds = []
    for r in range(2):
        pairs = [(i, i + FAR) for i in range(count - FAR) if (i // FAR) % 2 == r]
        if pairs:
            pairs = pairs + [(j, i) for i, j in pairs]
            rounds.append(lax.ppermute(lower() if lower is upper else jnp.where(side == r, lower(), upper()), "seq", pairs))
    if len(rounds) == 1:
        return rounds[0], rounds[0]
    return jnp.where(side == 1, rounds[0], rounds[1]), jnp.where(side == 0, rounds[0], rounds[1])


def group_rows(group, head, size):
    return pl.ds(pl.multiple_of(jnp.bitwise_xor(group, head) * size, size), size)


def own_order(ref, head):
    size = ref.shape[0] // 4
    return jnp.concatenate([ref[group_rows(g, head, size), :] for g in range(4)], 0)


def stacked(mat, kv_head):
    low = 2 * kv_head * HEAD_SIZE
    return jnp.concatenate([mat[:, low : low + HEAD_SIZE], mat[:, low + HEAD_SIZE : low + 2 * HEAD_SIZE]], 0)


def causal_mask(tok, head):
    key_pos = lax.broadcasted_iota(jnp.int32, (tok, 2 * tok), 0)
    lane = lax.broadcasted_iota(jnp.int32, (tok, 2 * tok), 1)
    query_pos = jnp.bitwise_xor(jnp.bitwise_and(lane, tok - 1), head * (tok // 4))
    return query_pos >= key_pos


def columns(kv_cols, kv_head):
    low = kv_head * HEAD_SIZE
    return slice(low, low + HEAD_SIZE), slice(kv_cols + low, kv_cols + low + HEAD_SIZE)


def window(kv_ref, r1_ref, r2_ref, x1_ref, p0_ref, x2_ref, odd, cols):
    return [kv_ref[:, cols], r1_ref[:, cols], r2_ref[:, cols], x1_ref[:, cols], jnp.where(odd, p0_ref[:, cols], x2_ref[:, cols])]


def join_kernel(k_ref, v_ref, kv_ref):
    cols = k_ref.shape[1]
    kv_ref[:, :cols] = k_ref[...]
    kv_ref[:, cols:] = v_ref[...]


def either_kernel(first, a_ref, b_ref, out_ref):
    out_ref[...] = jnp.where(first(lax.axis_index("seq")), a_ref[...], b_ref[...])


def is_odd(seq):
    return lax.rem(seq, 2) == 1


def is_lower(seq):
    return lax.rem(lax.div(seq, FAR), 2) == 0


def forward_kernel(q_ref, kv_ref, r1_ref, r2_ref, x1_ref, p0_ref, x2_ref, dn_ref, df_ref,
                   o_ref, p_ref, stat_ref, second_ref):
    seq, head = lax.axis_index("seq"), lax.axis_index("head")
    odd = lax.rem(seq, 2) == 1
    tok = q_ref.shape[0]
    kv_cols = kv_ref.shape[1] // 2
    q_rel = own_order(q_ref, head)
    d_rel = jnp.concatenate([dn_ref[...], df_ref[...]], 0)
    causal = causal_mask(tok, head)
    near = jnp.where(seq >= 2, 0.0, NEG).astype(F32)
    far = jnp.where(seq >= 4, 0.0, NEG).astype(F32)
    mixed = jnp.where(jnp.logical_or(odd, seq >= 4), 0.0, NEG).astype(F32)
    biases = [None, near, far, near, mixed]
    scale = LOGIT_SCALE * LOG2E
    stats = []
    for g in range(kv_cols // HEAD_SIZE):
        kc, vc = columns(kv_cols, g)
        qg = stacked(q_rel, g)
        blocks = (kv_ref, r1_ref, r2_ref, x1_ref, p0_ref, x2_ref)
        key_blocks, value_blocks = window(*blocks, odd, kc), window(*blocks, odd, vc)
        scores = [dot(kb, qg, 1, 1) for kb in key_blocks]
        scores[0] = jnp.where(causal, scores[0], NEG)
        scores[2] = jnp.where(causal, NEG, scores[2])
        tops = [jnp.max(sb, axis=0, keepdims=True) for sb in scores]
        tops = [t if b is None else t + b for t, b in zip(tops, biases)]
        top = tops[0]
        for t in tops[1:]:
            top = jnp.maximum(top, t)
        top = top * scale
        probs = [jnp.exp2(sb * scale - (top if b is None else top - b)) for sb, b in zip(scores, biases)]
        total = sum(jnp.sum(pb, axis=0, keepdims=True) for pb in probs)
        inv = 1.0 / total
        out = jnp.zeros((HEAD_SIZE, 2 * tok), F32)
        for b in range(5):
            pb = (probs[b] * inv).astype(BF16)
            p_ref[g, b] = pb
            out = out + dot(value_blocks[b], pb, 0, 0)
        out = out.astype(BF16)
        grad = stacked(d_rel, g)
        delta = jnp.sum(grad.astype(F32).T * out.astype(F32), axis=0, keepdims=True)
        stats += [top + jnp.log2(total), delta]
        out = out.astype(F32).T.astype(BF16)
        low = 2 * g * HEAD_SIZE
        o_ref[:, low : low + HEAD_SIZE] = out[:tok]
        o_ref[:, low + HEAD_SIZE : low + 2 * HEAD_SIZE] = out[tok:]
    spare = jnp.zeros((stat_ref.shape[0] - len(stats), 2 * tok), F32)
    stat_ref[...] = jnp.concatenate(stats + [spare], 0)
    half = d_rel.shape[1] // 2
    packed = jnp.concatenate([st[:, :tok] for st in stats] + [st[:, tok:] for st in stats], 0)
    packed = jnp.concatenate([packed, jnp.zeros((PACK - packed.shape[0], tok), F32)], 0)
    second_ref[:tok, :] = d_rel[:, half:]
    for part in range(3):
        rounded = packed.astype(BF16)
        second_ref[tok + part * PACK : tok + (part + 1) * PACK, :] = rounded
        packed = packed - rounded.astype(F32)


def project_kernel(o_ref, w_ref, *part_refs):
    size = part_refs[0].shape[0]
    cols = w_ref.shape[1]
    step = cols // 7 if cols % (7 * HEAD_SIZE) == 0 else cols
    for low in range(0, cols, step):
        part = dot(o_ref[...], w_ref[:, low : low + step], 1, 0).astype(BF16)
        for i, ref in enumerate(part_refs):
            ref[:, low : low + step] = part[i * size : (i + 1) * size]


def near_back_kernel(own_ref, core_ref, w_ref, d_ref):
    rows = jnp.concatenate([own_ref[...], core_ref[...]], 0)
    d_ref[...] = dot(rows, w_ref[...], 1, 1).astype(BF16)


def far_back_kernel(y_ref, yc_ref, w_ref, near_ref, d_ref, first_ref):
    rows = jnp.concatenate([y_ref[...], yc_ref[...]], 0)
    grad = dot(rows, w_ref[...], 1, 1).astype(BF16)
    d_ref[...] = grad
    cols = first_ref.shape[1]
    first_ref[...] = jnp.concatenate([near_ref[:, :cols], grad[:, :cols]], 0)


def across_kernel(q_ref, x1_ref, p_ref, stat_ref, dn_ref, df_ref, tx_ref):
    tok = q_ref.shape[0]
    kv_cols = x1_ref.shape[1] // 2
    q_rel = own_order(q_ref, lax.axis_index("head"))
    d_rel = jnp.concatenate([dn_ref[...], df_ref[...]], 0)
    for g in range(kv_cols // HEAD_SIZE):
        kc, vc = columns(kv_cols, g)
        qg, dg = stacked(q_rel, g), stacked(d_rel, g)
        pb = p_ref[g, 3]
        dp = dot(x1_ref[:, vc], dg, 1, 1)
        ds = (pb.astype(F32) * (dp - stat_ref[2 * g + 1 : 2 * g + 2, :])).astype(BF16)
        tx_ref[:, vc] = dot(pb, dg, 1, 0).astype(BF16)
        tx_ref[:, kc] = (dot(ds, qg, 1, 0) * LOGIT_SCALE).astype(BF16)


def backward_kernel(q_ref, kv_ref, r1_ref, r2_ref, x1_ref, p0_ref, x2_ref, p_ref, stat_ref, dn_ref, df_ref,
                    dq_ref, town_ref, t1_ref, tz_ref):
    seq, head = lax.axis_index("seq"), lax.axis_index("head")
    odd = lax.rem(seq, 2) == 1
    tok = q_ref.shape[0]
    kv_cols = kv_ref.shape[1] // 2
    size = tok // 4
    q_rel = own_order(q_ref, head)
    d_rel = jnp.concatenate([dn_ref[...], df_ref[...]], 0)
    outs = [town_ref, t1_ref, None, None, tz_ref]
    for g in range(kv_cols // HEAD_SIZE):
        kc, vc = columns(kv_cols, g)
        qg, dg = stacked(q_rel, g), stacked(d_rel, g)
        blocks = (kv_ref, r1_ref, r2_ref, x1_ref, p0_ref, x2_ref)
        key_blocks, value_blocks = window(*blocks, odd, kc), window(*blocks, odd, vc)
        delta = stat_ref[2 * g + 1 : 2 * g + 2, :]
        dq = jnp.zeros((HEAD_SIZE, 2 * tok), F32)
        for b in range(5):
            pb = p_ref[g, b]
            dp = dot(value_blocks[b], dg, 1, 1)
            ds = (pb.astype(F32) * (dp - delta)).astype(BF16)
            if outs[b] is not None:
                outs[b][:, vc] = dot(pb, dg, 1, 0).astype(outs[b].dtype)
                outs[b][:, kc] = (dot(ds, qg, 1, 0) * LOGIT_SCALE).astype(outs[b].dtype)
            dq = dq + dot(key_blocks[b], ds, 0, 0)
        dq = (dq * LOGIT_SCALE).T.astype(BF16)
        low = 2 * g * HEAD_SIZE
        for r in range(4):
            rows = group_rows(r, head, size)
            dq_ref[rows, low : low + HEAD_SIZE] = dq[r * size : (r + 1) * size]
            dq_ref[rows, low + HEAD_SIZE : low + 2 * HEAD_SIZE] = dq[tok + r * size : tok + (r + 1) * size]


def unpacked(second_ref, tok, kv_heads):
    parts = [second_ref[tok + i * PACK : tok + (i + 1) * PACK, :tok].astype(F32) for i in range(3)]
    packed = parts[0] + (parts[1] + parts[2])
    count = 2 * kv_heads
    return [jnp.concatenate([packed[i : i + 1], packed[count + i : count + i + 1]], 1) for i in range(count)]


def pair_kernel(t_ref, a_ref, b_ref, out_ref):
    tok, half = a_ref.shape
    odd = lax.rem(lax.axis_index("seq"), 2) == 1
    out_ref[:tok, :] = jnp.where(odd, t_ref[...], jnp.concatenate([a_ref[...], b_ref[:tok, :]], 1))
    out_ref[tok:, :half] = b_ref[tok:, :]
    out_ref[tok:, half:] = jnp.zeros((b_ref.shape[0] - tok, half), BF16)


def far_kernel(kv_ref, qf_ref, af_ref, bf_ref, qx_ref, px_ref, t_ref):
    seq, head = lax.axis_index("seq"), lax.axis_index("head")
    count = lax.axis_size("seq")
    tok = kv_ref.shape[0]
    kv_cols = kv_ref.shape[1] // 2
    kv_heads = kv_cols // HEAD_SIZE
    straight = jnp.logical_and(jnp.logical_not(causal_mask(tok, head)), seq + FAR < count)
    across = jnp.logical_and(lax.rem(seq, 2) == 1, seq + FAR - 1 < count)
    sources = [
        (own_order(qf_ref, head), jnp.concatenate([af_ref[...], bf_ref[:tok, :]], 1), unpacked(bf_ref, tok, kv_heads), straight),
        (own_order(qx_ref, head), px_ref[:tok, :], unpacked(px_ref, tok, kv_heads), across),
    ]
    scale = LOGIT_SCALE * LOG2E
    for g in range(kv_heads):
        kc, vc = columns(kv_cols, g)
        key, value = kv_ref[:, kc], kv_ref[:, vc]
        dk = jnp.zeros((tok, HEAD_SIZE), F32)
        dv = jnp.zeros((tok, HEAD_SIZE), F32)
        for q_rel, d_rel, stats, keep in sources:
            qg, dg = stacked(q_rel, g), stacked(d_rel, g)
            prob = jnp.exp2(dot(key, qg, 1, 1) * scale - stats[2 * g])
            prob = jnp.where(keep, prob, 0.0).astype(BF16)
            dp = dot(value, dg, 1, 1)
            ds = jnp.where(keep, prob.astype(F32) * (dp - stats[2 * g + 1]), 0.0).astype(BF16)
            dv = dv + dot(prob, dg, 1, 0)
            dk = dk + dot(ds, qg, 1, 0)
        t_ref[:, kc] = dk * LOGIT_SCALE
        t_ref[:, vc] = dv


def sum_kernel(*refs):
    total = refs[0][...].astype(F32)
    for ref in refs[1:-1]:
        total = total + ref[...].astype(F32)
    refs[-1][...] = total.astype(refs[-1].dtype)


def finish_kernel(own_ref, far_ref, hop_ref, pair_ref, dk_ref, dv_ref):
    odd = lax.rem(lax.axis_index("seq"), 2) == 1
    total = own_ref[...] + far_ref[...] + hop_ref[...].astype(F32) + jnp.where(odd, 0.0, pair_ref[: own_ref.shape[0], :].astype(F32))
    kv_cols = dk_ref.shape[1]
    dk_ref[...] = total[:, :kv_cols].astype(BF16)
    dv_ref[...] = total[:, kv_cols:].astype(BF16)


def per_device(queries, keys, values, out_weight, out_grad):
    tok, q_cols = queries.shape
    kv_cols = keys.shape[1]
    kv_heads = kv_cols // HEAD_SIZE
    size = tok // 4
    rows = jax.ShapeDtypeStruct((size, out_weight.shape[1]), BF16)
    block = jax.ShapeDtypeStruct((tok, 2 * kv_cols), BF16)
    wide_block = jax.ShapeDtypeStruct((tok, 2 * kv_cols), F32)

    def call(kernel, name, outs, scratch, *operands, cost=SMALL):
        return pl.pallas_call(
            kernel,
            out_shape=outs,
            in_specs=[VMEM] * len(operands),
            out_specs=jax.tree.map(lambda _: VMEM, outs),
            scratch_shapes=scratch,
            compiler_params=pltpu.CompilerParams(vmem_limit_bytes=16 << 20),
            cost_estimate=cost,
            name=name,
        )(*operands)

    def gate(value, *others):
        return lax.optimization_barrier((value, *others))[0]

    og_y = swapped(out_grad, "head", 2)
    kv = call(join_kernel, "join", block, [], keys, values)
    far_sent = call(functools.partial(either_kernel, is_lower), "far_sent", block, [], kv, queries)
    r1 = shifted(kv, 2)
    r2, q_far = far_swapped(lambda: kv, lambda: queries) if lax.axis_size("seq") > 2 * FAR else (far_swapped(*[lambda: far_sent] * 2))
    p0 = swapped(kv, "seq", 1)
    og_c = swapped(out_grad, "head", 1)
    half_grad = jax.ShapeDtypeStruct((tok // 2, q_cols), BF16)
    grad_near = call(near_back_kernel, "near_back", half_grad, [], out_grad, og_c, out_weight, cost=SMALL)
    x1 = swapped(gate(r1, p0), "seq", 1)
    x2 = swapped(call(functools.partial(either_kernel, is_odd), "pick", block, [], r2, q_far, cost=LARGE), "seq", 1)
    og_yc = swapped(gate(og_y, r1, r2, p0, grad_near), "head", 1)
    first = jax.ShapeDtypeStruct((tok, q_cols // 2), BF16)
    second = jax.ShapeDtypeStruct((tok + 3 * PACK, q_cols // 2), BF16)
    grad_far, sent_first = call(far_back_kernel, "far_back", (half_grad, first), [], gate(og_y, x1), og_yc, out_weight, grad_near,
                                cost=LARGE)

    def down(value):
        return far_swapped(*[lambda: value] * 2)[1]

    far_first = down(sent_first)
    attended, probs, stats, sent_second = call(
        forward_kernel,
        "attend",
        (
            jax.ShapeDtypeStruct((tok, q_cols), BF16),
            jax.ShapeDtypeStruct((kv_heads, 5, tok, 2 * tok), BF16),
            jax.ShapeDtypeStruct((8 * pl.cdiv(2 * kv_heads, 8), 2 * tok), F32),
            second,
        ),
        [],
        queries, kv, r1, r2, x1, p0, x2, grad_near, grad_far,
    )
    t_x = call(across_kernel, "across_grad", block, [], queries, x1, probs, stats, grad_near, grad_far)
    d1 = swapped(t_x, "seq", 1)
    far_second = down(sent_second)
    near_own, near_core, far_own, far_core = call(
        project_kernel, "project", (rows,) * 4, [], gate(attended, t_x), out_weight
    )
    sent = swapped(gate(far_core, far_first), "head", 1)
    far_sum = call(sum_kernel, "far_sum", rows, [], far_own, sent)
    from_y = swapped(far_sum, "head", 2)

    query_gradient, t_own, t_1, t_z = call(
        backward_kernel,
        "attend_grad",
        (jax.ShapeDtypeStruct((tok, q_cols), BF16), wide_block, block, block),
        [],
        queries, kv, r1, r2, x1, p0, x2, probs, stats, grad_near, gate(grad_far, far_first),
        cost=LARGE,
    )
    e1 = shifted(call(sum_kernel, "hop_sum", block, [], t_1, d1), -2)
    pair = jax.ShapeDtypeStruct((second.shape[0], q_cols), BF16)
    pair = swapped(call(pair_kernel, "pair", pair, [], t_z, far_first, far_second), "seq", 1)
    from_core = swapped(gate(near_core, far_sum), "head", 1)
    t_far = call(far_kernel, "far_grad", wide_block, [],
                 kv, q_far, far_first, far_second, x2, pair, cost=MEDIUM)

    narrow = jax.ShapeDtypeStruct(keys.shape, BF16)
    key_gradient, value_gradient = call(finish_kernel, "finish", (narrow, narrow), [], t_own, t_far, e1, pair)
    projected = call(sum_kernel, "projected", rows, [], near_own, from_core, from_y, cost=LARGE)
    return (projected, query_gradient, key_gradient, value_gradient)


def solution(mesh):
    return jax.shard_map(
        per_device,
        mesh=mesh,
        in_specs=(
            P("seq", "head"),
            P("seq", "head"),
            P("seq", "head"),
            P("head", None),
            P(("seq", "head"), None),
        ),
        out_specs=(P(("seq", "head"), None), P("seq", "head"), P("seq", "head"), P("seq", "head")),
        check_vma=False,
    )
```

```python
import functools

import jax
import jax.numpy as jnp
from jax import lax
from jax.experimental import pallas as pl
from jax.experimental.pallas import tpu as pltpu
from jax.sharding import PartitionSpec as P

HEAD_SIZE = 128
WIN = 1024
LOGIT_SCALE = 168.0 ** (-0.5)
LOG2E = 1.4426950408889634
NEG = -1e30
PACK = 16
FAR = 4
F32 = jnp.float32
BF16 = jnp.bfloat16
SMALL = pl.CostEstimate(flops=1, bytes_accessed=1, transcendentals=0)
MEDIUM = pl.CostEstimate(flops=1 * 10**8, bytes_accessed=1, transcendentals=0)
LARGE = pl.CostEstimate(flops=10**10, bytes_accessed=1, transcendentals=0)
VMEM = pl.BlockSpec(memory_space=pltpu.VMEM)


def dot(a, b, ca, cb):
    return lax.dot_general(a, b, (((ca,), (cb,)), ((), ())), preferred_element_type=F32)


def shifted(value, steps):
    count = lax.axis_size("seq")
    first, last = (max(0, -steps), min(count, count - steps))
    return lax.ppermute(value, "seq", [(i, i + steps) for i in range(first, last)])


def swapped(value, axis, bit):
    count = lax.axis_size(axis)
    return lax.ppermute(value, axis, [(i, i ^ bit) for i in range(count)])


def far_swapped(lower, upper):
    count = lax.axis_size("seq")
    side = lax.rem(lax.div(lax.axis_index("seq"), FAR), 2)
    rounds = []
    for r in range(2):
        pairs = [(i, i + FAR) for i in range(count - FAR) if (i // FAR) % 2 == r]
        if pairs:
            pairs = pairs + [(j, i) for i, j in pairs]
            rounds.append(lax.ppermute(lower() if lower is upper else jnp.where(side == r, lower(), upper()), "seq", pairs))
    if len(rounds) == 1:
        return rounds[0], rounds[0]
    return jnp.where(side == 1, rounds[0], rounds[1]), jnp.where(side == 0, rounds[0], rounds[1])


def group_rows(group, head, size):
    return pl.ds(pl.multiple_of(jnp.bitwise_xor(group, head) * size, size), size)


def own_order(ref, head):
    size = ref.shape[0] // 4
    return jnp.concatenate([ref[group_rows(g, head, size), :] for g in range(4)], 0)


def stacked(mat, kv_head):
    low = 2 * kv_head * HEAD_SIZE
    return jnp.concatenate([mat[:, low : low + HEAD_SIZE], mat[:, low + HEAD_SIZE : low + 2 * HEAD_SIZE]], 0)


def causal_mask(tok, head):
    key_pos = lax.broadcasted_iota(jnp.int32, (tok, 2 * tok), 0)
    lane = lax.broadcasted_iota(jnp.int32, (tok, 2 * tok), 1)
    query_pos = jnp.bitwise_xor(jnp.bitwise_and(lane, tok - 1), head * (tok // 4))
    return query_pos >= key_pos


def columns(kv_cols, kv_head):
    low = kv_head * HEAD_SIZE
    return slice(low, low + HEAD_SIZE), slice(kv_cols + low, kv_cols + low + HEAD_SIZE)


def window(kv_ref, r1_ref, r2_ref, x1_ref, p0_ref, x2_ref, odd, cols):
    return [kv_ref[:, cols], r1_ref[:, cols], r2_ref[:, cols], x1_ref[:, cols], jnp.where(odd, p0_ref[:, cols], x2_ref[:, cols])]


def join_kernel(k_ref, v_ref, kv_ref):
    cols = k_ref.shape[1]
    kv_ref[:, :cols] = k_ref[...]
    kv_ref[:, cols:] = v_ref[...]


def either_kernel(first, a_ref, b_ref, out_ref):
    out_ref[...] = jnp.where(first(lax.axis_index("seq")), a_ref[...], b_ref[...])


def is_odd(seq):
    return lax.rem(seq, 2) == 1


def is_lower(seq):
    return lax.rem(lax.div(seq, FAR), 2) == 0


def forward_kernel(q_ref, kv_ref, r1_ref, r2_ref, x1_ref, p0_ref, x2_ref, dn_ref, df_ref,
                   o_ref, p_ref, stat_ref, second_ref):
    seq, head = lax.axis_index("seq"), lax.axis_index("head")
    odd = lax.rem(seq, 2) == 1
    tok = q_ref.shape[0]
    kv_cols = kv_ref.shape[1] // 2
    q_rel = own_order(q_ref, head)
    d_rel = jnp.concatenate([dn_ref[...], df_ref[...]], 0)
    causal = causal_mask(tok, head)
    near = jnp.where(seq >= 2, 0.0, NEG).astype(F32)
    far = jnp.where(seq >= 4, 0.0, NEG).astype(F32)
    mixed = jnp.where(jnp.logical_or(odd, seq >= 4), 0.0, NEG).astype(F32)
    biases = [None, near, far, near, mixed]
    scale = LOGIT_SCALE * LOG2E
    stats = []
    for g in range(kv_cols // HEAD_SIZE):
        kc, vc = columns(kv_cols, g)
        qg = stacked(q_rel, g)
        blocks = (kv_ref, r1_ref, r2_ref, x1_ref, p0_ref, x2_ref)
        key_blocks, value_blocks = window(*blocks, odd, kc), window(*blocks, odd, vc)
        scores = [dot(kb, qg, 1, 1) for kb in key_blocks]
        scores[0] = jnp.where(causal, scores[0], NEG)
        scores[2] = jnp.where(causal, NEG, scores[2])
        tops = [jnp.max(sb, axis=0, keepdims=True) for sb in scores]
        tops = [t if b is None else t + b for t, b in zip(tops, biases)]
        top = tops[0]
        for t in tops[1:]:
            top = jnp.maximum(top, t)
        top = top * scale
        probs = [jnp.exp2(sb * scale - (top if b is None else top - b)) for sb, b in zip(scores, biases)]
        total = sum(jnp.sum(pb, axis=0, keepdims=True) for pb in probs)
        inv = 1.0 / total
        out = jnp.zeros((HEAD_SIZE, 2 * tok), F32)
        for b in range(5):
            pb = (probs[b] * inv).astype(BF16)
            p_ref[g, b] = pb
            out = out + dot(value_blocks[b], pb, 0, 0)
        out = out.astype(BF16)
        grad = stacked(d_rel, g)
        delta = jnp.sum(grad.astype(F32).T * out.astype(F32), axis=0, keepdims=True)
        stats += [top + jnp.log2(total), delta]
        out = out.astype(F32).T.astype(BF16)
        low = 2 * g * HEAD_SIZE
        o_ref[:, low : low + HEAD_SIZE] = out[:tok]
        o_ref[:, low + HEAD_SIZE : low + 2 * HEAD_SIZE] = out[tok:]
    spare = jnp.zeros((stat_ref.shape[0] - len(stats), 2 * tok), F32)
    stat_ref[...] = jnp.concatenate(stats + [spare], 0)
    half = d_rel.shape[1] // 2
    packed = jnp.concatenate([st[:, :tok] for st in stats] + [st[:, tok:] for st in stats], 0)
    packed = jnp.concatenate([packed, jnp.zeros((PACK - packed.shape[0], tok), F32)], 0)
    second_ref[:tok, :] = d_rel[:, half:]
    for part in range(3):
        rounded = packed.astype(BF16)
        second_ref[tok + part * PACK : tok + (part + 1) * PACK, :] = rounded
        packed = packed - rounded.astype(F32)


def project_kernel(o_ref, w_ref, *part_refs):
    size = part_refs[0].shape[0]
    cols = w_ref.shape[1]
    step = cols // 7 if cols % (7 * HEAD_SIZE) == 0 else cols
    for low in range(0, cols, step):
        part = dot(o_ref[...], w_ref[:, low : low + step], 1, 0).astype(BF16)
        for i, ref in enumerate(part_refs):
            ref[:, low : low + step] = part[i * size : (i + 1) * size]


def near_back_kernel(own_ref, core_ref, w_ref, d_ref):
    rows = jnp.concatenate([own_ref[...], core_ref[...]], 0)
    d_ref[...] = dot(rows, w_ref[...], 1, 1).astype(BF16)


def far_back_kernel(y_ref, yc_ref, w_ref, near_ref, d_ref, first_ref):
    rows = jnp.concatenate([y_ref[...], yc_ref[...]], 0)
    grad = dot(rows, w_ref[...], 1, 1).astype(BF16)
    d_ref[...] = grad
    cols = first_ref.shape[1]
    first_ref[...] = jnp.concatenate([near_ref[:, :cols], grad[:, :cols]], 0)


def across_kernel(q_ref, x1_ref, p_ref, stat_ref, dn_ref, df_ref, tx_ref):
    tok = q_ref.shape[0]
    kv_cols = x1_ref.shape[1] // 2
    q_rel = own_order(q_ref, lax.axis_index("head"))
    d_rel = jnp.concatenate([dn_ref[...], df_ref[...]], 0)
    for g in range(kv_cols // HEAD_SIZE):
        kc, vc = columns(kv_cols, g)
        qg, dg = stacked(q_rel, g), stacked(d_rel, g)
        pb = p_ref[g, 3]
        dp = dot(x1_ref[:, vc], dg, 1, 1)
        ds = (pb.astype(F32) * (dp - stat_ref[2 * g + 1 : 2 * g + 2, :])).astype(BF16)
        tx_ref[:, vc] = dot(pb, dg, 1, 0).astype(BF16)
        tx_ref[:, kc] = (dot(ds, qg, 1, 0) * LOGIT_SCALE).astype(BF16)


def backward_kernel(q_ref, kv_ref, r1_ref, r2_ref, x1_ref, p0_ref, x2_ref, p_ref, stat_ref, dn_ref, df_ref,
                    dq_ref, town_ref, t1_ref, tz_ref):
    seq, head = lax.axis_index("seq"), lax.axis_index("head")
    odd = lax.rem(seq, 2) == 1
    tok = q_ref.shape[0]
    kv_cols = kv_ref.shape[1] // 2
    size = tok // 4
    q_rel = own_order(q_ref, head)
    d_rel = jnp.concatenate([dn_ref[...], df_ref[...]], 0)
    outs = [town_ref, t1_ref, None, None, tz_ref]
    for g in range(kv_cols // HEAD_SIZE):
        kc, vc = columns(kv_cols, g)
        qg, dg = stacked(q_rel, g), stacked(d_rel, g)
        blocks = (kv_ref, r1_ref, r2_ref, x1_ref, p0_ref, x2_ref)
        key_blocks, value_blocks = window(*blocks, odd, kc), window(*blocks, odd, vc)
        delta = stat_ref[2 * g + 1 : 2 * g + 2, :]
        dq = jnp.zeros((HEAD_SIZE, 2 * tok), F32)
        for b in range(5):
            pb = p_ref[g, b]
            dp = dot(value_blocks[b], dg, 1, 1)
            ds = (pb.astype(F32) * (dp - delta)).astype(BF16)
            if outs[b] is not None:
                outs[b][:, vc] = dot(pb, dg, 1, 0).astype(outs[b].dtype)
                outs[b][:, kc] = (dot(ds, qg, 1, 0) * LOGIT_SCALE).astype(outs[b].dtype)
            dq = dq + dot(key_blocks[b], ds, 0, 0)
        dq = (dq * LOGIT_SCALE).T.astype(BF16)
        low = 2 * g * HEAD_SIZE
        for r in range(4):
            rows = group_rows(r, head, size)
            dq_ref[rows, low : low + HEAD_SIZE] = dq[r * size : (r + 1) * size]
            dq_ref[rows, low + HEAD_SIZE : low + 2 * HEAD_SIZE] = dq[tok + r * size : tok + (r + 1) * size]


def unpacked(second_ref, tok, kv_heads):
    parts = [second_ref[tok + i * PACK : tok + (i + 1) * PACK, :tok].astype(F32) for i in range(3)]
    packed = parts[0] + (parts[1] + parts[2])
    count = 2 * kv_heads
    return [jnp.concatenate([packed[i : i + 1], packed[count + i : count + i + 1]], 1) for i in range(count)]


def pair_kernel(t_ref, a_ref, b_ref, out_ref):
    tok, half = a_ref.shape
    odd = lax.rem(lax.axis_index("seq"), 2) == 1
    out_ref[:tok, :] = jnp.where(odd, t_ref[...], jnp.concatenate([a_ref[...], b_ref[:tok, :]], 1))
    out_ref[tok:, :half] = b_ref[tok:, :]
    out_ref[tok:, half:] = jnp.zeros((b_ref.shape[0] - tok, half), BF16)


def far_kernel(kv_ref, qf_ref, af_ref, bf_ref, qx_ref, px_ref, t_ref):
    seq, head = lax.axis_index("seq"), lax.axis_index("head")
    count = lax.axis_size("seq")
    tok = kv_ref.shape[0]
    kv_cols = kv_ref.shape[1] // 2
    kv_heads = kv_cols // HEAD_SIZE
    straight = jnp.logical_and(jnp.logical_not(causal_mask(tok, head)), seq + FAR < count)
    across = jnp.logical_and(lax.rem(seq, 2) == 1, seq + FAR - 1 < count)
    sources = [
        (own_order(qf_ref, head), jnp.concatenate([af_ref[...], bf_ref[:tok, :]], 1), unpacked(bf_ref, tok, kv_heads), straight),
        (own_order(qx_ref, head), px_ref[:tok, :], unpacked(px_ref, tok, kv_heads), across),
    ]
    scale = LOGIT_SCALE * LOG2E
    for g in range(kv_heads):
        kc, vc = columns(kv_cols, g)
        key, value = kv_ref[:, kc], kv_ref[:, vc]
        dk = jnp.zeros((tok, HEAD_SIZE), F32)
        dv = jnp.zeros((tok, HEAD_SIZE), F32)
        for q_rel, d_rel, stats, keep in sources:
            qg, dg = stacked(q_rel, g), stacked(d_rel, g)
            prob = jnp.exp2(dot(key, qg, 1, 1) * scale - stats[2 * g])
            prob = jnp.where(keep, prob, 0.0).astype(BF16)
            dp = dot(value, dg, 1, 1)
            ds = jnp.where(keep, prob.astype(F32) * (dp - stats[2 * g + 1]), 0.0).astype(BF16)
            dv = dv + dot(prob, dg, 1, 0)
            dk = dk + dot(ds, qg, 1, 0)
        t_ref[:, kc] = dk * LOGIT_SCALE
        t_ref[:, vc] = dv


def sum_kernel(*refs):
    total = refs[0][...].astype(F32)
    for ref in refs[1:-1]:
        total = total + ref[...].astype(F32)
    refs[-1][...] = total.astype(refs[-1].dtype)


def finish_kernel(own_ref, far_ref, hop_ref, pair_ref, dk_ref, dv_ref):
    odd = lax.rem(lax.axis_index("seq"), 2) == 1
    total = own_ref[...] + far_ref[...] + hop_ref[...].astype(F32) + jnp.where(odd, 0.0, pair_ref[: own_ref.shape[0], :].astype(F32))
    kv_cols = dk_ref.shape[1]
    dk_ref[...] = total[:, :kv_cols].astype(BF16)
    dv_ref[...] = total[:, kv_cols:].astype(BF16)


def per_device(queries, keys, values, out_weight, out_grad):
    tok, q_cols = queries.shape
    kv_cols = keys.shape[1]
    kv_heads = kv_cols // HEAD_SIZE
    size = tok // 4
    rows = jax.ShapeDtypeStruct((size, out_weight.shape[1]), BF16)
    block = jax.ShapeDtypeStruct((tok, 2 * kv_cols), BF16)
    wide_block = jax.ShapeDtypeStruct((tok, 2 * kv_cols), F32)

    def call(kernel, name, outs, scratch, *operands, cost=SMALL):
        return pl.pallas_call(
            kernel,
            out_shape=outs,
            in_specs=[VMEM] * len(operands),
            out_specs=jax.tree.map(lambda _: VMEM, outs),
            scratch_shapes=scratch,
            compiler_params=pltpu.CompilerParams(vmem_limit_bytes=16 << 20),
            cost_estimate=cost,
            name=name,
        )(*operands)

    def gate(value, *others):
        return lax.optimization_barrier((value, *others))[0]

    og_y = swapped(out_grad, "head", 2)
    kv = call(join_kernel, "join", block, [], keys, values)
    far_sent = call(functools.partial(either_kernel, is_lower), "far_sent", block, [], kv, queries)
    r1 = shifted(kv, 2)
    r2, q_far = far_swapped(lambda: kv, lambda: queries) if lax.axis_size("seq") > 2 * FAR else (far_swapped(*[lambda: far_sent] * 2))
    p0 = swapped(kv, "seq", 1)
    og_c = swapped(out_grad, "head", 1)
    half_grad = jax.ShapeDtypeStruct((tok // 2, q_cols), BF16)
    grad_near = call(near_back_kernel, "near_back", half_grad, [], out_grad, og_c, out_weight, cost=LARGE)
    x1 = swapped(gate(r1, p0, grad_near), "seq", 1)
    x2 = swapped(call(functools.partial(either_kernel, is_odd), "pick", block, [], r2, q_far, cost=LARGE), "seq", 1)
    og_yc = swapped(gate(og_y, r2, grad_near), "head", 1)
    first = jax.ShapeDtypeStruct((tok, q_cols // 2), BF16)
    second = jax.ShapeDtypeStruct((tok + 3 * PACK, q_cols // 2), BF16)
    grad_far, sent_first = call(far_back_kernel, "far_back", (half_grad, first), [], gate(og_y, x1), og_yc, out_weight, grad_near,
                                cost=LARGE)

    def down(value):
        return far_swapped(*[lambda: value] * 2)[1]

    far_first = down(sent_first)
    attended, probs, stats, sent_second = call(
        forward_kernel,
        "attend",
        (
            jax.ShapeDtypeStruct((tok, q_cols), BF16),
            jax.ShapeDtypeStruct((kv_heads, 5, tok, 2 * tok), BF16),
            jax.ShapeDtypeStruct((8 * pl.cdiv(2 * kv_heads, 8), 2 * tok), F32),
            second,
        ),
        [],
        queries, kv, r1, r2, x1, p0, x2, grad_near, grad_far,
    )
    t_x = call(across_kernel, "across_grad", block, [], queries, x1, probs, stats, grad_near, grad_far)
    d1 = swapped(t_x, "seq", 1)
    far_second = down(sent_second)
    near_own, near_core, far_own, far_core = call(
        project_kernel, "project", (rows,) * 4, [], gate(attended, t_x), out_weight
    )
    sent = swapped(gate(far_core, far_first), "head", 1)
    far_sum = call(sum_kernel, "far_sum", rows, [], far_own, sent)
    from_y = swapped(far_sum, "head", 2)

    query_gradient, t_own, t_1, t_z = call(
        backward_kernel,
        "attend_grad",
        (jax.ShapeDtypeStruct((tok, q_cols), BF16), wide_block, block, block),
        [],
        queries, kv, r1, r2, x1, p0, x2, probs, stats, grad_near, gate(grad_far, far_first),
        cost=LARGE,
    )
    e1 = shifted(call(sum_kernel, "hop_sum", block, [], t_1, d1), -2)
    pair = jax.ShapeDtypeStruct((second.shape[0], q_cols), BF16)
    pair = swapped(call(pair_kernel, "pair", pair, [], t_z, far_first, far_second), "seq", 1)
    from_core = swapped(gate(near_core, far_sum), "head", 1)
    t_far = call(far_kernel, "far_grad", wide_block, [],
                 kv, q_far, far_first, far_second, x2, pair, cost=MEDIUM)

    narrow = jax.ShapeDtypeStruct(keys.shape, BF16)
    key_gradient, value_gradient = call(finish_kernel, "finish", (narrow, narrow), [], t_own, t_far, e1, pair)
    projected = call(sum_kernel, "projected", rows, [], near_own, from_core, from_y, cost=LARGE)
    return (projected, query_gradient, key_gradient, value_gradient)


def solution(mesh):
    return jax.shard_map(
        per_device,
        mesh=mesh,
        in_specs=(
            P("seq", "head"),
            P("seq", "head"),
            P("seq", "head"),
            P("head", None),
            P(("seq", "head"), None),
        ),
        out_specs=(P(("seq", "head"), None), P("seq", "head"), P("seq", "head"), P("seq", "head")),
        check_vma=False,
    )
```

```python
import functools

import jax
import jax.numpy as jnp
from jax import lax
from jax.experimental import pallas as pl
from jax.experimental.pallas import tpu as pltpu
from jax.sharding import PartitionSpec as P

HEAD_SIZE = 128
WIN = 1024
LOGIT_SCALE = 168.0 ** (-0.5)
LOG2E = 1.4426950408889634
NEG = -1e30
PACK = 16
FAR = 4
F32 = jnp.float32
BF16 = jnp.bfloat16
SMALL = pl.CostEstimate(flops=1, bytes_accessed=1, transcendentals=0)
MEDIUM = pl.CostEstimate(flops=1 * 10**8, bytes_accessed=1, transcendentals=0)
LARGE = pl.CostEstimate(flops=10**10, bytes_accessed=1, transcendentals=0)
VMEM = pl.BlockSpec(memory_space=pltpu.VMEM)


def dot(a, b, ca, cb):
    return lax.dot_general(a, b, (((ca,), (cb,)), ((), ())), preferred_element_type=F32)


def shifted(value, steps):
    count = lax.axis_size("seq")
    first, last = (max(0, -steps), min(count, count - steps))
    return lax.ppermute(value, "seq", [(i, i + steps) for i in range(first, last)])


def swapped(value, axis, bit):
    count = lax.axis_size(axis)
    return lax.ppermute(value, axis, [(i, i ^ bit) for i in range(count)])


def far_swapped(lower, upper):
    count = lax.axis_size("seq")
    side = lax.rem(lax.div(lax.axis_index("seq"), FAR), 2)
    rounds = []
    for r in range(2):
        pairs = [(i, i + FAR) for i in range(count - FAR) if (i // FAR) % 2 == r]
        if pairs:
            pairs = pairs + [(j, i) for i, j in pairs]
            rounds.append(lax.ppermute(lower() if lower is upper else jnp.where(side == r, lower(), upper()), "seq", pairs))
    if len(rounds) == 1:
        return rounds[0], rounds[0]
    return jnp.where(side == 1, rounds[0], rounds[1]), jnp.where(side == 0, rounds[0], rounds[1])


def group_rows(group, head, size):
    return pl.ds(pl.multiple_of(jnp.bitwise_xor(group, head) * size, size), size)


def own_order(ref, head):
    size = ref.shape[0] // 4
    return jnp.concatenate([ref[group_rows(g, head, size), :] for g in range(4)], 0)


def stacked(mat, kv_head):
    low = 2 * kv_head * HEAD_SIZE
    return jnp.concatenate([mat[:, low : low + HEAD_SIZE], mat[:, low + HEAD_SIZE : low + 2 * HEAD_SIZE]], 0)


def causal_mask(tok, head):
    key_pos = lax.broadcasted_iota(jnp.int32, (tok, 2 * tok), 0)
    lane = lax.broadcasted_iota(jnp.int32, (tok, 2 * tok), 1)
    query_pos = jnp.bitwise_xor(jnp.bitwise_and(lane, tok - 1), head * (tok // 4))
    return query_pos >= key_pos


def columns(kv_cols, kv_head):
    low = kv_head * HEAD_SIZE
    return slice(low, low + HEAD_SIZE), slice(kv_cols + low, kv_cols + low + HEAD_SIZE)


def window(kv_ref, r1_ref, r2_ref, x1_ref, p0_ref, x2_ref, odd, cols):
    return [kv_ref[:, cols], r1_ref[:, cols], r2_ref[:, cols], x1_ref[:, cols], jnp.where(odd, p0_ref[:, cols], x2_ref[:, cols])]


def join_kernel(k_ref, v_ref, kv_ref):
    cols = k_ref.shape[1]
    kv_ref[:, :cols] = k_ref[...]
    kv_ref[:, cols:] = v_ref[...]


def either_kernel(first, a_ref, b_ref, out_ref):
    out_ref[...] = jnp.where(first(lax.axis_index("seq")), a_ref[...], b_ref[...])


def is_odd(seq):
    return lax.rem(seq, 2) == 1


def is_lower(seq):
    return lax.rem(lax.div(seq, FAR), 2) == 0


def early_kernel(q_ref, kv_ref, r1_ref, r2_ref, x1_ref, e_ref, m_ref, part_ref):
    seq, head = lax.axis_index("seq"), lax.axis_index("head")
    tok = q_ref.shape[0]
    kv_cols = kv_ref.shape[1] // 2
    q_rel = own_order(q_ref, head)
    causal = causal_mask(tok, head)
    near = jnp.where(seq >= 2, 0.0, NEG).astype(F32)
    far = jnp.where(seq >= FAR, 0.0, NEG).astype(F32)
    biases = [None, near, far, near]
    scale = LOGIT_SCALE * LOG2E
    marks = []
    for g in range(kv_cols // HEAD_SIZE):
        kc, vc = columns(kv_cols, g)
        qg = stacked(q_rel, g)
        blocks = (kv_ref, r1_ref, r2_ref, x1_ref)
        scores = [dot(ref[:, kc], qg, 1, 1) for ref in blocks]
        scores[0] = jnp.where(causal, scores[0], NEG)
        scores[2] = jnp.where(causal, NEG, scores[2])
        tops = [jnp.max(sb, axis=0, keepdims=True) for sb in scores]
        tops = [t if b is None else t + b for t, b in zip(tops, biases)]
        top = jnp.maximum(jnp.maximum(tops[0], tops[1]), jnp.maximum(tops[2], tops[3])) * scale
        total = jnp.zeros_like(top)
        part = jnp.zeros((HEAD_SIZE, 2 * tok), F32)
        for b, bias in enumerate(biases):
            eb = jnp.exp2(scores[b] * scale - (top if bias is None else top - bias))
            e_ref[g, b] = eb
            total = total + jnp.sum(eb, axis=0, keepdims=True)
            part = part + dot(blocks[b][:, vc], eb.astype(BF16), 0, 0)
        part_ref[g] = part
        marks += [top, total]
    spare = jnp.zeros((m_ref.shape[0] - len(marks), 2 * tok), F32)
    m_ref[...] = jnp.concatenate(marks + [spare], 0)


def forward_kernel(q_ref, p0_ref, x2_ref, e_ref, m_ref, part_ref, dn_ref, df_ref,
                   o_ref, p_ref, stat_ref, second_ref):
    seq, head = lax.axis_index("seq"), lax.axis_index("head")
    odd = lax.rem(seq, 2) == 1
    tok = q_ref.shape[0]
    kv_cols = p0_ref.shape[1] // 2
    q_rel = own_order(q_ref, head)
    d_rel = jnp.concatenate([dn_ref[...], df_ref[...]], 0)
    bias = jnp.where(jnp.logical_or(odd, seq >= FAR), 0.0, NEG).astype(F32)
    scale = LOGIT_SCALE * LOG2E
    stats = []
    for g in range(kv_cols // HEAD_SIZE):
        kc, vc = columns(kv_cols, g)
        score = dot(jnp.where(odd, p0_ref[:, kc], x2_ref[:, kc]), stacked(q_rel, g), 1, 1)
        top_early = m_ref[2 * g : 2 * g + 1, :]
        top = jnp.maximum(top_early, (jnp.max(score, axis=0, keepdims=True) + bias) * scale)
        last = jnp.exp2(score * scale - (top - bias))
        shrink = jnp.exp2(top_early - top)
        total = m_ref[2 * g + 1 : 2 * g + 2, :] * shrink + jnp.sum(last, axis=0, keepdims=True)
        inv = 1.0 / total
        shrink = shrink * inv
        last = (last * inv).astype(BF16)
        p_ref[g, 4] = last
        out = part_ref[g] * shrink + dot(jnp.where(odd, p0_ref[:, vc], x2_ref[:, vc]), last, 0, 0)
        for b in range(4):
            p_ref[g, b] = (e_ref[g, b] * shrink).astype(BF16)
        out = out.astype(BF16)
        grad = stacked(d_rel, g)
        delta = jnp.sum(grad.astype(F32).T * out.astype(F32), axis=0, keepdims=True)
        stats += [top + jnp.log2(total), delta]
        out = out.astype(F32).T.astype(BF16)
        low = 2 * g * HEAD_SIZE
        o_ref[:, low : low + HEAD_SIZE] = out[:tok]
        o_ref[:, low + HEAD_SIZE : low + 2 * HEAD_SIZE] = out[tok:]
    spare = jnp.zeros((stat_ref.shape[0] - len(stats), 2 * tok), F32)
    stat_ref[...] = jnp.concatenate(stats + [spare], 0)
    half = d_rel.shape[1] // 2
    packed = jnp.concatenate([st[:, :tok] for st in stats] + [st[:, tok:] for st in stats], 0)
    packed = jnp.concatenate([packed, jnp.zeros((PACK - packed.shape[0], tok), F32)], 0)
    second_ref[:tok, :] = d_rel[:, half:]
    for part in range(3):
        rounded = packed.astype(BF16)
        second_ref[tok + part * PACK : tok + (part + 1) * PACK, :] = rounded
        packed = packed - rounded.astype(F32)


def project_kernel(o_ref, w_ref, *part_refs):
    size = part_refs[0].shape[0]
    cols = w_ref.shape[1]
    step = cols // 7 if cols % (7 * HEAD_SIZE) == 0 else cols
    for low in range(0, cols, step):
        part = dot(o_ref[...], w_ref[:, low : low + step], 1, 0).astype(BF16)
        for i, ref in enumerate(part_refs):
            ref[:, low : low + step] = part[i * size : (i + 1) * size]


def near_back_kernel(own_ref, core_ref, w_ref, d_ref):
    rows = jnp.concatenate([own_ref[...], core_ref[...]], 0)
    d_ref[...] = dot(rows, w_ref[...], 1, 1).astype(BF16)


def far_back_kernel(y_ref, yc_ref, w_ref, near_ref, d_ref, first_ref):
    rows = jnp.concatenate([y_ref[...], yc_ref[...]], 0)
    grad = dot(rows, w_ref[...], 1, 1).astype(BF16)
    d_ref[...] = grad
    cols = first_ref.shape[1]
    first_ref[...] = jnp.concatenate([near_ref[:, :cols], grad[:, :cols]], 0)


def across_kernel(q_ref, x1_ref, p_ref, stat_ref, dn_ref, df_ref, tx_ref):
    tok = q_ref.shape[0]
    kv_cols = x1_ref.shape[1] // 2
    q_rel = own_order(q_ref, lax.axis_index("head"))
    d_rel = jnp.concatenate([dn_ref[...], df_ref[...]], 0)
    for g in range(kv_cols // HEAD_SIZE):
        kc, vc = columns(kv_cols, g)
        qg, dg = stacked(q_rel, g), stacked(d_rel, g)
        pb = p_ref[g, 3]
        dp = dot(x1_ref[:, vc], dg, 1, 1)
        ds = (pb.astype(F32) * (dp - stat_ref[2 * g + 1 : 2 * g + 2, :])).astype(BF16)
        tx_ref[:, vc] = dot(pb, dg, 1, 0).astype(BF16)
        tx_ref[:, kc] = (dot(ds, qg, 1, 0) * LOGIT_SCALE).astype(BF16)


def backward_kernel(q_ref, kv_ref, r1_ref, r2_ref, x1_ref, p0_ref, x2_ref, p_ref, stat_ref, dn_ref, df_ref,
                    dq_ref, town_ref, t1_ref, tz_ref):
    seq, head = lax.axis_index("seq"), lax.axis_index("head")
    odd = lax.rem(seq, 2) == 1
    tok = q_ref.shape[0]
    kv_cols = kv_ref.shape[1] // 2
    size = tok // 4
    q_rel = own_order(q_ref, head)
    d_rel = jnp.concatenate([dn_ref[...], df_ref[...]], 0)
    outs = [town_ref, t1_ref, None, None, tz_ref]
    for g in range(kv_cols // HEAD_SIZE):
        kc, vc = columns(kv_cols, g)
        qg, dg = stacked(q_rel, g), stacked(d_rel, g)
        blocks = (kv_ref, r1_ref, r2_ref, x1_ref, p0_ref, x2_ref)
        key_blocks, value_blocks = window(*blocks, odd, kc), window(*blocks, odd, vc)
        delta = stat_ref[2 * g + 1 : 2 * g + 2, :]
        dq = jnp.zeros((HEAD_SIZE, 2 * tok), F32)
        for b in range(5):
            pb = p_ref[g, b]
            dp = dot(value_blocks[b], dg, 1, 1)
            ds = (pb.astype(F32) * (dp - delta)).astype(BF16)
            if outs[b] is not None:
                outs[b][:, vc] = dot(pb, dg, 1, 0).astype(outs[b].dtype)
                outs[b][:, kc] = (dot(ds, qg, 1, 0) * LOGIT_SCALE).astype(outs[b].dtype)
            dq = dq + dot(key_blocks[b], ds, 0, 0)
        dq = (dq * LOGIT_SCALE).T.astype(BF16)
        low = 2 * g * HEAD_SIZE
        for r in range(4):
            rows = group_rows(r, head, size)
            dq_ref[rows, low : low + HEAD_SIZE] = dq[r * size : (r + 1) * size]
            dq_ref[rows, low + HEAD_SIZE : low + 2 * HEAD_SIZE] = dq[tok + r * size : tok + (r + 1) * size]


def unpacked(second_ref, tok, kv_heads):
    parts = [second_ref[tok + i * PACK : tok + (i + 1) * PACK, :tok].astype(F32) for i in range(3)]
    packed = parts[0] + (parts[1] + parts[2])
    count = 2 * kv_heads
    return [jnp.concatenate([packed[i : i + 1], packed[count + i : count + i + 1]], 1) for i in range(count)]


def pair_kernel(t_ref, a_ref, b_ref, out_ref):
    tok, half = a_ref.shape
    odd = lax.rem(lax.axis_index("seq"), 2) == 1
    out_ref[:tok, :] = jnp.where(odd, t_ref[...], jnp.concatenate([a_ref[...], b_ref[:tok, :]], 1))
    out_ref[tok:, :half] = b_ref[tok:, :]
    out_ref[tok:, half:] = jnp.zeros((b_ref.shape[0] - tok, half), BF16)


def far_kernel(kv_ref, qf_ref, af_ref, bf_ref, qx_ref, px_ref, t_ref):
    seq, head = lax.axis_index("seq"), lax.axis_index("head")
    count = lax.axis_size("seq")
    tok = kv_ref.shape[0]
    kv_cols = kv_ref.shape[1] // 2
    kv_heads = kv_cols // HEAD_SIZE
    straight = jnp.logical_and(jnp.logical_not(causal_mask(tok, head)), seq + FAR < count)
    across = jnp.logical_and(lax.rem(seq, 2) == 1, seq + FAR - 1 < count)
    sources = [
        (own_order(qf_ref, head), jnp.concatenate([af_ref[...], bf_ref[:tok, :]], 1), unpacked(bf_ref, tok, kv_heads), straight),
        (own_order(qx_ref, head), px_ref[:tok, :], unpacked(px_ref, tok, kv_heads), across),
    ]
    scale = LOGIT_SCALE * LOG2E
    for g in range(kv_heads):
        kc, vc = columns(kv_cols, g)
        key, value = kv_ref[:, kc], kv_ref[:, vc]
        dk = jnp.zeros((tok, HEAD_SIZE), F32)
        dv = jnp.zeros((tok, HEAD_SIZE), F32)
        for q_rel, d_rel, stats, keep in sources:
            qg, dg = stacked(q_rel, g), stacked(d_rel, g)
            prob = jnp.exp2(dot(key, qg, 1, 1) * scale - stats[2 * g])
            prob = jnp.where(keep, prob, 0.0).astype(BF16)
            dp = dot(value, dg, 1, 1)
            ds = jnp.where(keep, prob.astype(F32) * (dp - stats[2 * g + 1]), 0.0).astype(BF16)
            dv = dv + dot(prob, dg, 1, 0)
            dk = dk + dot(ds, qg, 1, 0)
        t_ref[:, kc] = dk * LOGIT_SCALE
        t_ref[:, vc] = dv


def sum_kernel(*refs):
    total = refs[0][...].astype(F32)
    for ref in refs[1:-1]:
        total = total + ref[...].astype(F32)
    refs[-1][...] = total.astype(refs[-1].dtype)


def closing_kernel(own_ref, far_ref, hop_ref, pair_ref, near_ref, core_ref, y_ref, dk_ref, dv_ref, proj_ref):
    odd = lax.rem(lax.axis_index("seq"), 2) == 1
    proj_ref[...] = (near_ref[...].astype(F32) + core_ref[...].astype(F32) + y_ref[...].astype(F32)).astype(BF16)
    kept = jnp.where(odd, 0.0, pair_ref[: own_ref.shape[0], :].astype(F32))
    total = own_ref[...] + far_ref[...] + hop_ref[...].astype(F32) + kept
    kv_cols = dk_ref.shape[1]
    dk_ref[...] = total[:, :kv_cols].astype(BF16)
    dv_ref[...] = total[:, kv_cols:].astype(BF16)


def per_device(queries, keys, values, out_weight, out_grad):
    tok, q_cols = queries.shape
    kv_cols = keys.shape[1]
    kv_heads = kv_cols // HEAD_SIZE
    size = tok // 4
    rows = jax.ShapeDtypeStruct((size, out_weight.shape[1]), BF16)
    block = jax.ShapeDtypeStruct((tok, 2 * kv_cols), BF16)
    wide_block = jax.ShapeDtypeStruct((tok, 2 * kv_cols), F32)

    def call(kernel, name, outs, scratch, *operands, cost=SMALL):
        return pl.pallas_call(
            kernel,
            out_shape=outs,
            in_specs=[VMEM] * len(operands),
            out_specs=jax.tree.map(lambda _: VMEM, outs),
            scratch_shapes=scratch,
            compiler_params=pltpu.CompilerParams(vmem_limit_bytes=16 << 20),
            cost_estimate=cost,
            name=name,
        )(*operands)

    def gate(value, *others):
        return lax.optimization_barrier((value, *others))[0]

    og_y = swapped(out_grad, "head", 2)
    kv = call(join_kernel, "join", block, [], keys, values)
    far_sent = call(functools.partial(either_kernel, is_lower), "far_sent", block, [], kv, queries)
    r1 = shifted(kv, 2)
    r2, q_far = far_swapped(lambda: kv, lambda: queries) if lax.axis_size("seq") > 2 * FAR else (far_swapped(*[lambda: far_sent] * 2))
    p0 = swapped(kv, "seq", 1)
    og_c = swapped(out_grad, "head", 1)
    half_grad = jax.ShapeDtypeStruct((tok // 2, q_cols), BF16)
    grad_near = call(near_back_kernel, "near_back", half_grad, [], out_grad, og_c, out_weight, cost=LARGE)
    x1 = swapped(gate(r1, p0, grad_near), "seq", 1)
    x2 = swapped(call(functools.partial(either_kernel, is_odd), "pick", block, [], r2, q_far, cost=LARGE), "seq", 1)
    og_yc = swapped(gate(og_y, r2, grad_near), "head", 1)
    first = jax.ShapeDtypeStruct((tok, q_cols // 2), BF16)
    second = jax.ShapeDtypeStruct((tok + 3 * PACK, q_cols // 2), BF16)
    grad_far, sent_first = call(far_back_kernel, "far_back", (half_grad, first), [], gate(og_y, x1), og_yc, out_weight, grad_near,
                                cost=LARGE)

    def down(value):
        return far_swapped(*[lambda: value] * 2)[1]

    far_first = down(sent_first)
    table = jax.ShapeDtypeStruct((8 * pl.cdiv(2 * kv_heads, 8), 2 * tok), F32)
    early = call(
        early_kernel,
        "attend_early",
        (
            jax.ShapeDtypeStruct((kv_heads, 4, tok, 2 * tok), F32),
            table,
            jax.ShapeDtypeStruct((kv_heads, HEAD_SIZE, 2 * tok), F32),
        ),
        [],
        queries, kv, r1, r2, x1,
    )
    attended, probs, stats, sent_second = call(
        forward_kernel,
        "attend",
        (
            jax.ShapeDtypeStruct((tok, q_cols), BF16),
            jax.ShapeDtypeStruct((kv_heads, 5, tok, 2 * tok), BF16),
            table,
            second,
        ),
        [],
        queries, p0, x2, *early, grad_near, grad_far,
    )
    t_x = call(across_kernel, "across_grad", block, [], queries, x1, probs, stats, grad_near, grad_far)
    d1 = swapped(t_x, "seq", 1)
    far_second = down(sent_second)
    near_own, near_core, far_own, far_core = call(
        project_kernel, "project", (rows,) * 4, [], gate(attended, t_x), out_weight
    )
    sent = swapped(gate(far_core, far_first), "head", 1)
    far_sum = call(sum_kernel, "far_sum", rows, [], far_own, sent)
    from_y = swapped(far_sum, "head", 2)

    query_gradient, t_own, t_1, t_z = call(
        backward_kernel,
        "attend_grad",
        (jax.ShapeDtypeStruct((tok, q_cols), BF16), wide_block, block, block),
        [],
        queries, kv, r1, r2, x1, p0, x2, probs, stats, grad_near, gate(grad_far, far_first),
        cost=LARGE,
    )
    e1 = shifted(call(sum_kernel, "hop_sum", block, [], t_1, d1), -2)
    pair = jax.ShapeDtypeStruct((second.shape[0], q_cols), BF16)
    pair = swapped(call(pair_kernel, "pair", pair, [], t_z, far_first, far_second), "seq", 1)
    from_core = swapped(gate(near_core, far_sum), "head", 1)
    t_far = call(far_kernel, "far_grad", wide_block, [],
                 kv, q_far, far_first, far_second, x2, pair, cost=MEDIUM)

    narrow = jax.ShapeDtypeStruct(keys.shape, BF16)
    key_gradient, value_gradient, projected = call(
        closing_kernel, "closing", (narrow, narrow, rows), [], t_own, t_far, e1, pair, near_own, from_core, from_y
    )
    return (projected, query_gradient, key_gradient, value_gradient)


def solution(mesh):
    return jax.shard_map(
        per_device,
        mesh=mesh,
        in_specs=(
            P("seq", "head"),
            P("seq", "head"),
            P("seq", "head"),
            P("head", None),
            P(("seq", "head"), None),
        ),
        out_specs=(P(("seq", "head"), None), P("seq", "head"), P("seq", "head"), P("seq", "head")),
        check_vma=False,
    )
```

```python
import functools

import jax
import jax.numpy as jnp
from jax import lax
from jax.experimental import pallas as pl
from jax.experimental.pallas import tpu as pltpu
from jax.sharding import PartitionSpec as P

HEAD_SIZE = 128
WIN = 1024
LOGIT_SCALE = 168.0 ** (-0.5)
LOG2E = 1.4426950408889634
NEG = -1e30
PACK = 16
FAR = 4
F32 = jnp.float32
BF16 = jnp.bfloat16
SMALL = pl.CostEstimate(flops=1, bytes_accessed=1, transcendentals=0)
MEDIUM = pl.CostEstimate(flops=1 * 10**8, bytes_accessed=1, transcendentals=0)
LARGE = pl.CostEstimate(flops=10**10, bytes_accessed=1, transcendentals=0)
VMEM = pl.BlockSpec(memory_space=pltpu.VMEM)


def dot(a, b, ca, cb):
    return lax.dot_general(a, b, (((ca,), (cb,)), ((), ())), preferred_element_type=F32)


def shifted(value, steps):
    count = lax.axis_size("seq")
    first, last = (max(0, -steps), min(count, count - steps))
    return lax.ppermute(value, "seq", [(i, i + steps) for i in range(first, last)])


def swapped(value, axis, bit):
    count = lax.axis_size(axis)
    return lax.ppermute(value, axis, [(i, i ^ bit) for i in range(count)])


def far_swapped(lower, upper):
    count = lax.axis_size("seq")
    side = lax.rem(lax.div(lax.axis_index("seq"), FAR), 2)
    rounds = []
    for r in range(2):
        pairs = [(i, i + FAR) for i in range(count - FAR) if (i // FAR) % 2 == r]
        if pairs:
            pairs = pairs + [(j, i) for i, j in pairs]
            rounds.append(lax.ppermute(lower() if lower is upper else jnp.where(side == r, lower(), upper()), "seq", pairs))
    if len(rounds) == 1:
        return rounds[0], rounds[0]
    return jnp.where(side == 1, rounds[0], rounds[1]), jnp.where(side == 0, rounds[0], rounds[1])


def group_rows(group, head, size):
    return pl.ds(pl.multiple_of(jnp.bitwise_xor(group, head) * size, size), size)


def own_order(ref, head):
    size = ref.shape[0] // 4
    return jnp.concatenate([ref[group_rows(g, head, size), :] for g in range(4)], 0)


def stacked(mat, kv_head):
    low = 2 * kv_head * HEAD_SIZE
    return jnp.concatenate([mat[:, low : low + HEAD_SIZE], mat[:, low + HEAD_SIZE : low + 2 * HEAD_SIZE]], 0)


def causal_mask(tok, head):
    key_pos = lax.broadcasted_iota(jnp.int32, (tok, 2 * tok), 0)
    lane = lax.broadcasted_iota(jnp.int32, (tok, 2 * tok), 1)
    query_pos = jnp.bitwise_xor(jnp.bitwise_and(lane, tok - 1), head * (tok // 4))
    return query_pos >= key_pos


def columns(kv_cols, kv_head):
    low = kv_head * HEAD_SIZE
    return slice(low, low + HEAD_SIZE), slice(kv_cols + low, kv_cols + low + HEAD_SIZE)


def window(kv_ref, r1_ref, r2_ref, x1_ref, p0_ref, x2_ref, odd, cols):
    return [kv_ref[:, cols], r1_ref[:, cols], r2_ref[:, cols], x1_ref[:, cols], jnp.where(odd, p0_ref[:, cols], x2_ref[:, cols])]


def join_kernel(k_ref, v_ref, kv_ref, sems):
    cols = k_ref.shape[1]
    copies = [
        pltpu.make_async_copy(k_ref, kv_ref.at[:, pl.ds(0, cols)], sems.at[0]),
        pltpu.make_async_copy(v_ref, kv_ref.at[:, pl.ds(cols, cols)], sems.at[1]),
    ]
    for copy in copies:
        copy.start()
    for copy in copies:
        copy.wait()


def either_kernel(first, a_ref, b_ref, out_ref):
    out_ref[...] = jnp.where(first(lax.axis_index("seq")), a_ref[...], b_ref[...])


def far_sent_kernel(kv_ref, q_ref, sent_ref, kept_ref):
    kv = kv_ref[...]
    kept_ref[...] = kv
    sent_ref[...] = jnp.where(is_lower(lax.axis_index("seq")), kv, q_ref[...])


def is_odd(seq):
    return lax.rem(seq, 2) == 1


def is_lower(seq):
    return lax.rem(lax.div(seq, FAR), 2) == 0


def early_kernel(q_ref, kv_ref, r1_ref, r2_ref, x1_ref, e_ref, m_ref, part_ref):
    seq, head = lax.axis_index("seq"), lax.axis_index("head")
    tok = q_ref.shape[0]
    kv_cols = kv_ref.shape[1] // 2
    q_rel = own_order(q_ref, head)
    causal = causal_mask(tok, head)
    near = jnp.where(seq >= 2, 0.0, NEG).astype(F32)
    far = jnp.where(seq >= FAR, 0.0, NEG).astype(F32)
    biases = [None, near, far, near]
    scale = LOGIT_SCALE * LOG2E
    marks = []
    for g in range(kv_cols // HEAD_SIZE):
        kc, vc = columns(kv_cols, g)
        qg = stacked(q_rel, g)
        blocks = (kv_ref, r1_ref, r2_ref, x1_ref)
        scores = [dot(ref[:, kc], qg, 1, 1) for ref in blocks]
        scores[0] = jnp.where(causal, scores[0], NEG)
        scores[2] = jnp.where(causal, NEG, scores[2])
        tops = [jnp.max(sb, axis=0, keepdims=True) for sb in scores]
        tops = [t if b is None else t + b for t, b in zip(tops, biases)]
        top = jnp.maximum(jnp.maximum(tops[0], tops[1]), jnp.maximum(tops[2], tops[3])) * scale
        total = jnp.zeros_like(top)
        part = jnp.zeros((HEAD_SIZE, 2 * tok), F32)
        for b, bias in enumerate(biases):
            eb = jnp.exp2(scores[b] * scale - (top if bias is None else top - bias))
            e_ref[g, b] = eb
            total = total + jnp.sum(eb, axis=0, keepdims=True)
            part = part + dot(blocks[b][:, vc], eb.astype(BF16), 0, 0)
        part_ref[g] = part
        marks += [top, total]
    spare = jnp.zeros((m_ref.shape[0] - len(marks), 2 * tok), F32)
    m_ref[...] = jnp.concatenate(marks + [spare], 0)


def forward_kernel(q_ref, p0_ref, x2_ref, e_ref, m_ref, part_ref, dn_ref, df_ref,
                   o_ref, p_ref, stat_ref, second_ref):
    seq, head = lax.axis_index("seq"), lax.axis_index("head")
    odd = lax.rem(seq, 2) == 1
    tok = q_ref.shape[0]
    kv_cols = p0_ref.shape[1] // 2
    q_rel = own_order(q_ref, head)
    d_rel = jnp.concatenate([dn_ref[...], df_ref[...]], 0)
    bias = jnp.where(jnp.logical_or(odd, seq >= FAR), 0.0, NEG).astype(F32)
    scale = LOGIT_SCALE * LOG2E
    stats = []
    for g in range(kv_cols // HEAD_SIZE):
        kc, vc = columns(kv_cols, g)
        score = dot(jnp.where(odd, p0_ref[:, kc], x2_ref[:, kc]), stacked(q_rel, g), 1, 1)
        top_early = m_ref[2 * g : 2 * g + 1, :]
        top = jnp.maximum(top_early, (jnp.max(score, axis=0, keepdims=True) + bias) * scale)
        last = jnp.exp2(score * scale - (top - bias))
        shrink = jnp.exp2(top_early - top)
        total = m_ref[2 * g + 1 : 2 * g + 2, :] * shrink + jnp.sum(last, axis=0, keepdims=True)
        inv = 1.0 / total
        shrink = shrink * inv
        last = (last * inv).astype(BF16)
        p_ref[g, 4] = last
        out = part_ref[g] * shrink + dot(jnp.where(odd, p0_ref[:, vc], x2_ref[:, vc]), last, 0, 0)
        for b in range(4):
            p_ref[g, b] = (e_ref[g, b] * shrink).astype(BF16)
        out = out.astype(BF16)
        grad = stacked(d_rel, g)
        delta = jnp.sum(grad.astype(F32).T * out.astype(F32), axis=0, keepdims=True)
        stats += [top + jnp.log2(total), delta]
        out = out.astype(F32).T.astype(BF16)
        low = 2 * g * HEAD_SIZE
        o_ref[:, low : low + HEAD_SIZE] = out[:tok]
        o_ref[:, low + HEAD_SIZE : low + 2 * HEAD_SIZE] = out[tok:]
    spare = jnp.zeros((stat_ref.shape[0] - len(stats), 2 * tok), F32)
    stat_ref[...] = jnp.concatenate(stats + [spare], 0)
    half = d_rel.shape[1] // 2
    packed = jnp.concatenate([st[:, :tok] for st in stats] + [st[:, tok:] for st in stats], 0)
    packed = jnp.concatenate([packed, jnp.zeros((PACK - packed.shape[0], tok), F32)], 0)
    second_ref[:tok, :] = d_rel[:, half:]
    for part in range(3):
        rounded = packed.astype(BF16)
        second_ref[tok + part * PACK : tok + (part + 1) * PACK, :] = rounded
        packed = packed - rounded.astype(F32)


def project_kernel(o_ref, w_ref, *part_refs):
    size = part_refs[0].shape[0]
    cols = w_ref.shape[1]
    step = cols // 7 if cols % (7 * HEAD_SIZE) == 0 else cols
    for low in range(0, cols, step):
        part = dot(o_ref[...], w_ref[:, low : low + step], 1, 0).astype(BF16)
        for i, ref in enumerate(part_refs):
            ref[:, low : low + step] = part[i * size : (i + 1) * size]


def near_back_kernel(own_ref, core_ref, w_ref, d_ref):
    rows = jnp.concatenate([own_ref[...], core_ref[...]], 0)
    d_ref[...] = dot(rows, w_ref[...], 1, 1).astype(BF16)


def far_back_kernel(y_ref, yc_ref, w_ref, near_ref, d_ref, first_ref):
    rows = jnp.concatenate([y_ref[...], yc_ref[...]], 0)
    grad = dot(rows, w_ref[...], 1, 1).astype(BF16)
    d_ref[...] = grad
    cols = first_ref.shape[1]
    first_ref[...] = jnp.concatenate([near_ref[:, :cols], grad[:, :cols]], 0)


def across_kernel(q_ref, x1_ref, p_ref, stat_ref, dn_ref, df_ref, tx_ref):
    tok = q_ref.shape[0]
    kv_cols = x1_ref.shape[1] // 2
    q_rel = own_order(q_ref, lax.axis_index("head"))
    d_rel = jnp.concatenate([dn_ref[...], df_ref[...]], 0)
    for g in range(kv_cols // HEAD_SIZE):
        kc, vc = columns(kv_cols, g)
        qg, dg = stacked(q_rel, g), stacked(d_rel, g)
        pb = p_ref[g, 3]
        dp = dot(x1_ref[:, vc], dg, 1, 1)
        ds = (pb.astype(F32) * (dp - stat_ref[2 * g + 1 : 2 * g + 2, :])).astype(BF16)
        tx_ref[:, vc] = dot(pb, dg, 1, 0).astype(BF16)
        tx_ref[:, kc] = (dot(ds, qg, 1, 0) * LOGIT_SCALE).astype(BF16)


def backward_kernel(q_ref, kv_ref, r1_ref, r2_ref, x1_ref, p0_ref, x2_ref, p_ref, stat_ref, dn_ref, df_ref,
                    dq_ref, town_ref, t1_ref, tz_ref):
    seq, head = lax.axis_index("seq"), lax.axis_index("head")
    odd = lax.rem(seq, 2) == 1
    tok = q_ref.shape[0]
    kv_cols = kv_ref.shape[1] // 2
    size = tok // 4
    q_rel = own_order(q_ref, head)
    d_rel = jnp.concatenate([dn_ref[...], df_ref[...]], 0)
    outs = [town_ref, t1_ref, None, None, tz_ref]
    for g in range(kv_cols // HEAD_SIZE):
        kc, vc = columns(kv_cols, g)
        qg, dg = stacked(q_rel, g), stacked(d_rel, g)
        blocks = (kv_ref, r1_ref, r2_ref, x1_ref, p0_ref, x2_ref)
        key_blocks, value_blocks = window(*blocks, odd, kc), window(*blocks, odd, vc)
        delta = stat_ref[2 * g + 1 : 2 * g + 2, :]
        dq = jnp.zeros((HEAD_SIZE, 2 * tok), F32)
        for b in range(5):
            pb = p_ref[g, b]
            dp = dot(value_blocks[b], dg, 1, 1)
            ds = (pb.astype(F32) * (dp - delta)).astype(BF16)
            if outs[b] is not None:
                outs[b][:, vc] = dot(pb, dg, 1, 0).astype(outs[b].dtype)
                outs[b][:, kc] = (dot(ds, qg, 1, 0) * LOGIT_SCALE).astype(outs[b].dtype)
            dq = dq + dot(key_blocks[b], ds, 0, 0)
        dq = (dq * LOGIT_SCALE).T.astype(BF16)
        low = 2 * g * HEAD_SIZE
        for r in range(4):
            rows = group_rows(r, head, size)
            dq_ref[rows, low : low + HEAD_SIZE] = dq[r * size : (r + 1) * size]
            dq_ref[rows, low + HEAD_SIZE : low + 2 * HEAD_SIZE] = dq[tok + r * size : tok + (r + 1) * size]


def unpacked(second_ref, tok, kv_heads):
    parts = [second_ref[tok + i * PACK : tok + (i + 1) * PACK, :tok].astype(F32) for i in range(3)]
    packed = parts[0] + (parts[1] + parts[2])
    count = 2 * kv_heads
    return [jnp.concatenate([packed[i : i + 1], packed[count + i : count + i + 1]], 1) for i in range(count)]


def pair_kernel(t_ref, a_ref, b_ref, out_ref):
    tok, half = a_ref.shape
    odd = lax.rem(lax.axis_index("seq"), 2) == 1
    out_ref[:tok, :] = jnp.where(odd, t_ref[...], jnp.concatenate([a_ref[...], b_ref[:tok, :]], 1))
    out_ref[tok:, :half] = b_ref[tok:, :]
    out_ref[tok:, half:] = jnp.zeros((b_ref.shape[0] - tok, half), BF16)


def far_kernel(kv_ref, qf_ref, af_ref, bf_ref, qx_ref, px_ref, t_ref):
    seq, head = lax.axis_index("seq"), lax.axis_index("head")
    count = lax.axis_size("seq")
    tok = kv_ref.shape[0]
    kv_cols = kv_ref.shape[1] // 2
    kv_heads = kv_cols // HEAD_SIZE
    straight = jnp.logical_and(jnp.logical_not(causal_mask(tok, head)), seq + FAR < count)
    across = jnp.logical_and(lax.rem(seq, 2) == 1, seq + FAR - 1 < count)
    sources = [
        (own_order(qf_ref, head), jnp.concatenate([af_ref[...], bf_ref[:tok, :]], 1), unpacked(bf_ref, tok, kv_heads), straight),
        (own_order(qx_ref, head), px_ref[:tok, :], unpacked(px_ref, tok, kv_heads), across),
    ]
    scale = LOGIT_SCALE * LOG2E
    for g in range(kv_heads):
        kc, vc = columns(kv_cols, g)
        key, value = kv_ref[:, kc], kv_ref[:, vc]
        dk = jnp.zeros((tok, HEAD_SIZE), F32)
        dv = jnp.zeros((tok, HEAD_SIZE), F32)
        for q_rel, d_rel, stats, keep in sources:
            qg, dg = stacked(q_rel, g), stacked(d_rel, g)
            prob = jnp.exp2(dot(key, qg, 1, 1) * scale - stats[2 * g])
            prob = jnp.where(keep, prob, 0.0).astype(BF16)
            dp = dot(value, dg, 1, 1)
            ds = jnp.where(keep, prob.astype(F32) * (dp - stats[2 * g + 1]), 0.0).astype(BF16)
            dv = dv + dot(prob, dg, 1, 0)
            dk = dk + dot(ds, qg, 1, 0)
        t_ref[:, kc] = dk * LOGIT_SCALE
        t_ref[:, vc] = dv


def sum_kernel(*refs):
    total = refs[0][...].astype(F32)
    for ref in refs[1:-1]:
        total = total + ref[...].astype(F32)
    refs[-1][...] = total.astype(refs[-1].dtype)


def closing_kernel(own_ref, far_ref, hop_ref, pair_ref, near_ref, core_ref, y_ref, dk_ref, dv_ref, proj_ref):
    odd = lax.rem(lax.axis_index("seq"), 2) == 1
    proj_ref[...] = (near_ref[...].astype(F32) + core_ref[...].astype(F32) + y_ref[...].astype(F32)).astype(BF16)
    kept = jnp.where(odd, 0.0, pair_ref[: own_ref.shape[0], :].astype(F32))
    total = own_ref[...] + far_ref[...] + hop_ref[...].astype(F32) + kept
    kv_cols = dk_ref.shape[1]
    dk_ref[...] = total[:, :kv_cols].astype(BF16)
    dv_ref[...] = total[:, kv_cols:].astype(BF16)


def per_device(queries, keys, values, out_weight, out_grad):
    tok, q_cols = queries.shape
    kv_cols = keys.shape[1]
    kv_heads = kv_cols // HEAD_SIZE
    size = tok // 4
    rows = jax.ShapeDtypeStruct((size, out_weight.shape[1]), BF16)
    block = jax.ShapeDtypeStruct((tok, 2 * kv_cols), BF16)
    wide_block = jax.ShapeDtypeStruct((tok, 2 * kv_cols), F32)

    def call(kernel, name, outs, scratch, *operands, cost=SMALL):
        return pl.pallas_call(
            kernel,
            out_shape=outs,
            in_specs=[VMEM] * len(operands),
            out_specs=jax.tree.map(lambda _: VMEM, outs),
            scratch_shapes=scratch,
            compiler_params=pltpu.CompilerParams(vmem_limit_bytes=16 << 20),
            cost_estimate=cost,
            name=name,
        )(*operands)

    def gate(value, *others):
        return lax.optimization_barrier((value, *others))[0]

    kv_sent = pl.pallas_call(
        join_kernel,
        out_shape=block,
        in_specs=[pl.BlockSpec(memory_space=pl.ANY)] * 2,
        out_specs=pl.BlockSpec(memory_space=pl.ANY),
        scratch_shapes=[pltpu.SemaphoreType.DMA((2,))],
        compiler_params=pltpu.CompilerParams(vmem_limit_bytes=60 << 20),
        cost_estimate=SMALL,
        name="join",
    )(keys, values)
    far_sent, kv = call(far_sent_kernel, "far_sent", (block, block), [], kv_sent, queries)
    r1 = shifted(kv_sent, 2)
    r2, q_far = far_swapped(lambda: kv, lambda: queries) if lax.axis_size("seq") > 2 * FAR else (far_swapped(*[lambda: far_sent] * 2))
    og_c = swapped(out_grad, "head", 1)
    og_y = swapped(out_grad, "head", 2)
    p0 = swapped(kv, "seq", 1)
    half_grad = jax.ShapeDtypeStruct((tok // 2, q_cols), BF16)
    grad_near = call(near_back_kernel, "near_back", half_grad, [], out_grad, og_c, out_weight, cost=LARGE)
    x1 = swapped(gate(r1, grad_near), "seq", 1)
    x2 = swapped(call(functools.partial(either_kernel, is_odd), "pick", block, [], r2, q_far, cost=LARGE), "seq", 1)
    og_yc = swapped(gate(og_y, r2, grad_near), "head", 1)
    first = jax.ShapeDtypeStruct((tok, q_cols // 2), BF16)
    second = jax.ShapeDtypeStruct((tok + 3 * PACK, q_cols // 2), BF16)
    grad_far, sent_first = call(far_back_kernel, "far_back", (half_grad, first), [], gate(og_y, x1), og_yc, out_weight, grad_near,
                                cost=LARGE)

    def down(value):
        return far_swapped(*[lambda: value] * 2)[1]

    far_first = down(sent_first)
    table = jax.ShapeDtypeStruct((8 * pl.cdiv(2 * kv_heads, 8), 2 * tok), F32)
    early = call(
        early_kernel,
        "attend_early",
        (
            jax.ShapeDtypeStruct((kv_heads, 4, tok, 2 * tok), F32),
            table,
            jax.ShapeDtypeStruct((kv_heads, HEAD_SIZE, 2 * tok), F32),
        ),
        [],
        queries, kv, gate(r1, p0), r2, x1,
    )
    attended, probs, stats, sent_second = call(
        forward_kernel,
        "attend",
        (
            jax.ShapeDtypeStruct((tok, q_cols), BF16),
            jax.ShapeDtypeStruct((kv_heads, 5, tok, 2 * tok), BF16),
            table,
            second,
        ),
        [],
        queries, p0, x2, *early, grad_near, grad_far,
    )
    t_x = call(across_kernel, "across_grad", block, [], queries, x1, probs, stats, grad_near, grad_far)
    d1 = swapped(t_x, "seq", 1)
    far_second = down(sent_second)
    near_own, near_core, far_own, far_core = call(
        project_kernel, "project", (rows,) * 4, [], gate(attended, t_x), out_weight
    )
    sent = swapped(gate(far_core, far_first), "head", 1)
    far_sum = call(sum_kernel, "far_sum", rows, [], far_own, sent)
    from_y = swapped(far_sum, "head", 2)

    query_gradient, t_own, t_1, t_z = call(
        backward_kernel,
        "attend_grad",
        (jax.ShapeDtypeStruct((tok, q_cols), BF16), wide_block, block, block),
        [],
        queries, kv, r1, r2, x1, p0, x2, probs, stats, grad_near, gate(grad_far, far_first),
        cost=LARGE,
    )
    e1 = shifted(call(sum_kernel, "hop_sum", block, [], t_1, d1), -2)
    pair = jax.ShapeDtypeStruct((second.shape[0], q_cols), BF16)
    pair = swapped(call(pair_kernel, "pair", pair, [], t_z, far_first, far_second), "seq", 1)
    from_core = swapped(gate(near_core, far_sum), "head", 1)
    t_far = call(far_kernel, "far_grad", wide_block, [],
                 kv, q_far, far_first, far_second, x2, pair, cost=MEDIUM)

    narrow = jax.ShapeDtypeStruct(keys.shape, BF16)
    key_gradient, value_gradient, projected = call(
        closing_kernel, "closing", (narrow, narrow, rows), [], t_own, t_far, e1, pair, near_own, from_core, from_y
    )
    return (projected, query_gradient, key_gradient, value_gradient)


def solution(mesh):
    return jax.shard_map(
        per_device,
        mesh=mesh,
        in_specs=(
            P("seq", "head"),
            P("seq", "head"),
            P("seq", "head"),
            P("head", None),
            P(("seq", "head"), None),
        ),
        out_specs=(P(("seq", "head"), None), P("seq", "head"), P("seq", "head"), P("seq", "head")),
        check_vma=False,
    )
```

```python
import functools

import jax
import jax.numpy as jnp
from jax import lax
from jax.experimental import pallas as pl
from jax.experimental.pallas import tpu as pltpu
from jax.sharding import PartitionSpec as P

HEAD_SIZE = 128
WIN = 1024
LOGIT_SCALE = 168.0 ** (-0.5)
LOG2E = 1.4426950408889634
NEG = -1e30
PACK = 16
FAR = 4
F32 = jnp.float32
BF16 = jnp.bfloat16
SMALL = pl.CostEstimate(flops=1, bytes_accessed=1, transcendentals=0)
MEDIUM = pl.CostEstimate(flops=1 * 10**8, bytes_accessed=1, transcendentals=0)
LARGE = pl.CostEstimate(flops=10**10, bytes_accessed=1, transcendentals=0)
VMEM = pl.BlockSpec(memory_space=pltpu.VMEM)


def dot(a, b, ca, cb):
    return lax.dot_general(a, b, (((ca,), (cb,)), ((), ())), preferred_element_type=F32)


def shifted(value, steps):
    count = lax.axis_size("seq")
    first, last = (max(0, -steps), min(count, count - steps))
    return lax.ppermute(value, "seq", [(i, i + steps) for i in range(first, last)])


def swapped(value, axis, bit):
    count = lax.axis_size(axis)
    return lax.ppermute(value, axis, [(i, i ^ bit) for i in range(count)])


def far_swapped(lower, upper):
    count = lax.axis_size("seq")
    side = lax.rem(lax.div(lax.axis_index("seq"), FAR), 2)
    rounds = []
    for r in range(2):
        pairs = [(i, i + FAR) for i in range(count - FAR) if (i // FAR) % 2 == r]
        if pairs:
            pairs = pairs + [(j, i) for i, j in pairs]
            rounds.append(lax.ppermute(lower() if lower is upper else jnp.where(side == r, lower(), upper()), "seq", pairs))
    if len(rounds) == 1:
        return rounds[0], rounds[0]
    return jnp.where(side == 1, rounds[0], rounds[1]), jnp.where(side == 0, rounds[0], rounds[1])


def group_rows(group, head, size):
    return pl.ds(pl.multiple_of(jnp.bitwise_xor(group, head) * size, size), size)


def own_order(ref, head):
    size = ref.shape[0] // 4
    return jnp.concatenate([ref[group_rows(g, head, size), :] for g in range(4)], 0)


def stacked(mat, kv_head):
    low = 2 * kv_head * HEAD_SIZE
    return jnp.concatenate([mat[:, low : low + HEAD_SIZE], mat[:, low + HEAD_SIZE : low + 2 * HEAD_SIZE]], 0)


def causal_mask(tok, head):
    key_pos = lax.broadcasted_iota(jnp.int32, (tok, 2 * tok), 0)
    lane = lax.broadcasted_iota(jnp.int32, (tok, 2 * tok), 1)
    query_pos = jnp.bitwise_xor(jnp.bitwise_and(lane, tok - 1), head * (tok // 4))
    return query_pos >= key_pos


def columns(kv_cols, kv_head):
    low = kv_head * HEAD_SIZE
    return slice(low, low + HEAD_SIZE), slice(kv_cols + low, kv_cols + low + HEAD_SIZE)


def window(kv_ref, r1_ref, r2_ref, x1_ref, p0_ref, x2_ref, odd, cols):
    return [kv_ref[:, cols], r1_ref[:, cols], r2_ref[:, cols], x1_ref[:, cols], jnp.where(odd, p0_ref[:, cols], x2_ref[:, cols])]


def join_kernel(k_ref, v_ref, kv_ref):
    cols = k_ref.shape[1]
    kv_ref[:, :cols] = k_ref[...]
    kv_ref[:, cols:] = v_ref[...]


def either_kernel(first, a_ref, b_ref, out_ref):
    out_ref[...] = jnp.where(first(lax.axis_index("seq")), a_ref[...], b_ref[...])


def is_odd(seq):
    return lax.rem(seq, 2) == 1


def is_lower(seq):
    return lax.rem(lax.div(seq, FAR), 2) == 0


def early_kernel(q_ref, kv_ref, r1_ref, r2_ref, x1_ref, e_ref, m_ref, part_ref):
    seq, head = lax.axis_index("seq"), lax.axis_index("head")
    tok = q_ref.shape[0]
    kv_cols = kv_ref.shape[1] // 2
    q_rel = own_order(q_ref, head)
    causal = causal_mask(tok, head)
    near = jnp.where(seq >= 2, 0.0, NEG).astype(F32)
    far = jnp.where(seq >= FAR, 0.0, NEG).astype(F32)
    biases = [None, near, far, near]
    scale = LOGIT_SCALE * LOG2E
    marks = []
    for g in range(kv_cols // HEAD_SIZE):
        kc, vc = columns(kv_cols, g)
        qg = stacked(q_rel, g)
        blocks = (kv_ref, r1_ref, r2_ref, x1_ref)
        scores = [dot(ref[:, kc], qg, 1, 1) for ref in blocks]
        scores[0] = jnp.where(causal, scores[0], NEG)
        scores[2] = jnp.where(causal, NEG, scores[2])
        tops = [jnp.max(sb, axis=0, keepdims=True) for sb in scores]
        tops = [t if b is None else t + b for t, b in zip(tops, biases)]
        top = jnp.maximum(jnp.maximum(tops[0], tops[1]), jnp.maximum(tops[2], tops[3])) * scale
        total = jnp.zeros_like(top)
        part = jnp.zeros((HEAD_SIZE, 2 * tok), F32)
        for b, bias in enumerate(biases):
            eb = jnp.exp2(scores[b] * scale - (top if bias is None else top - bias))
            e_ref[g, b] = eb
            total = total + jnp.sum(eb, axis=0, keepdims=True)
            part = part + dot(blocks[b][:, vc], eb.astype(BF16), 0, 0)
        part_ref[g] = part
        marks += [top, total]
    spare = jnp.zeros((m_ref.shape[0] - len(marks), 2 * tok), F32)
    m_ref[...] = jnp.concatenate(marks + [spare], 0)


def forward_kernel(q_ref, p0_ref, x2_ref, e_ref, m_ref, part_ref, dn_ref, df_ref,
                   o_ref, p_ref, stat_ref, second_ref):
    seq, head = lax.axis_index("seq"), lax.axis_index("head")
    odd = lax.rem(seq, 2) == 1
    tok = q_ref.shape[0]
    kv_cols = p0_ref.shape[1] // 2
    q_rel = own_order(q_ref, head)
    d_rel = jnp.concatenate([dn_ref[...], df_ref[...]], 0)
    bias = jnp.where(jnp.logical_or(odd, seq >= FAR), 0.0, NEG).astype(F32)
    scale = LOGIT_SCALE * LOG2E
    stats = []
    for g in range(kv_cols // HEAD_SIZE):
        kc, vc = columns(kv_cols, g)
        score = dot(jnp.where(odd, p0_ref[:, kc], x2_ref[:, kc]), stacked(q_rel, g), 1, 1)
        top_early = m_ref[2 * g : 2 * g + 1, :]
        top = jnp.maximum(top_early, (jnp.max(score, axis=0, keepdims=True) + bias) * scale)
        last = jnp.exp2(score * scale - (top - bias))
        shrink = jnp.exp2(top_early - top)
        total = m_ref[2 * g + 1 : 2 * g + 2, :] * shrink + jnp.sum(last, axis=0, keepdims=True)
        inv = 1.0 / total
        shrink = shrink * inv
        last = (last * inv).astype(BF16)
        p_ref[g, 4] = last
        out = part_ref[g] * shrink + dot(jnp.where(odd, p0_ref[:, vc], x2_ref[:, vc]), last, 0, 0)
        for b in range(4):
            p_ref[g, b] = (e_ref[g, b] * shrink).astype(BF16)
        out = out.astype(BF16)
        grad = stacked(d_rel, g)
        delta = jnp.sum(grad.astype(F32).T * out.astype(F32), axis=0, keepdims=True)
        stats += [top + jnp.log2(total), delta]
        out = out.astype(F32).T.astype(BF16)
        low = 2 * g * HEAD_SIZE
        o_ref[:, low : low + HEAD_SIZE] = out[:tok]
        o_ref[:, low + HEAD_SIZE : low + 2 * HEAD_SIZE] = out[tok:]
    spare = jnp.zeros((stat_ref.shape[0] - len(stats), 2 * tok), F32)
    stat_ref[...] = jnp.concatenate(stats + [spare], 0)
    half = d_rel.shape[1] // 2
    packed = jnp.concatenate([st[:, :tok] for st in stats] + [st[:, tok:] for st in stats], 0)
    packed = jnp.concatenate([packed, jnp.zeros((PACK - packed.shape[0], tok), F32)], 0)
    second_ref[:tok, :] = d_rel[:, half:]
    for part in range(3):
        rounded = packed.astype(BF16)
        second_ref[tok + part * PACK : tok + (part + 1) * PACK, :] = rounded
        packed = packed - rounded.astype(F32)


def project_kernel(o_ref, w_ref, *part_refs):
    size = part_refs[0].shape[0]
    cols = w_ref.shape[1]
    step = cols // 7 if cols % (7 * HEAD_SIZE) == 0 else cols
    for low in range(0, cols, step):
        part = dot(o_ref[...], w_ref[:, low : low + step], 1, 0).astype(BF16)
        for i, ref in enumerate(part_refs):
            ref[:, low : low + step] = part[i * size : (i + 1) * size]


def near_back_kernel(own_ref, core_ref, w_ref, d_ref):
    rows = jnp.concatenate([own_ref[...], core_ref[...]], 0)
    d_ref[...] = dot(rows, w_ref[...], 1, 1).astype(BF16)


def far_back_kernel(y_ref, yc_ref, w_ref, near_ref, d_ref, first_ref):
    rows = jnp.concatenate([y_ref[...], yc_ref[...]], 0)
    grad = dot(rows, w_ref[...], 1, 1).astype(BF16)
    d_ref[...] = grad
    cols = first_ref.shape[1]
    first_ref[...] = jnp.concatenate([near_ref[:, :cols], grad[:, :cols]], 0)


def across_kernel(q_ref, x1_ref, p_ref, stat_ref, dn_ref, df_ref, tx_ref):
    tok = q_ref.shape[0]
    kv_cols = x1_ref.shape[1] // 2
    q_rel = own_order(q_ref, lax.axis_index("head"))
    d_rel = jnp.concatenate([dn_ref[...], df_ref[...]], 0)
    for g in range(kv_cols // HEAD_SIZE):
        kc, vc = columns(kv_cols, g)
        qg, dg = stacked(q_rel, g), stacked(d_rel, g)
        pb = p_ref[g, 3]
        dp = dot(x1_ref[:, vc], dg, 1, 1)
        ds = (pb.astype(F32) * (dp - stat_ref[2 * g + 1 : 2 * g + 2, :])).astype(BF16)
        tx_ref[:, vc] = dot(pb, dg, 1, 0).astype(BF16)
        tx_ref[:, kc] = (dot(ds, qg, 1, 0) * LOGIT_SCALE).astype(BF16)


def backward_kernel(q_ref, kv_ref, r1_ref, r2_ref, x1_ref, p0_ref, x2_ref, p_ref, stat_ref, dn_ref, df_ref,
                    dq_ref, town_ref, t1_ref, tz_ref):
    seq, head = lax.axis_index("seq"), lax.axis_index("head")
    odd = lax.rem(seq, 2) == 1
    tok = q_ref.shape[0]
    kv_cols = kv_ref.shape[1] // 2
    size = tok // 4
    q_rel = own_order(q_ref, head)
    d_rel = jnp.concatenate([dn_ref[...], df_ref[...]], 0)
    outs = [town_ref, t1_ref, None, None, tz_ref]
    for g in range(kv_cols // HEAD_SIZE):
        kc, vc = columns(kv_cols, g)
        qg, dg = stacked(q_rel, g), stacked(d_rel, g)
        blocks = (kv_ref, r1_ref, r2_ref, x1_ref, p0_ref, x2_ref)
        key_blocks, value_blocks = window(*blocks, odd, kc), window(*blocks, odd, vc)
        delta = stat_ref[2 * g + 1 : 2 * g + 2, :]
        dq = jnp.zeros((HEAD_SIZE, 2 * tok), F32)
        for b in range(5):
            pb = p_ref[g, b]
            dp = dot(value_blocks[b], dg, 1, 1)
            ds = (pb.astype(F32) * (dp - delta)).astype(BF16)
            if outs[b] is not None:
                outs[b][:, vc] = dot(pb, dg, 1, 0).astype(outs[b].dtype)
                outs[b][:, kc] = (dot(ds, qg, 1, 0) * LOGIT_SCALE).astype(outs[b].dtype)
            dq = dq + dot(key_blocks[b], ds, 0, 0)
        dq = (dq * LOGIT_SCALE).T.astype(BF16)
        low = 2 * g * HEAD_SIZE
        for r in range(4):
            rows = group_rows(r, head, size)
            dq_ref[rows, low : low + HEAD_SIZE] = dq[r * size : (r + 1) * size]
            dq_ref[rows, low + HEAD_SIZE : low + 2 * HEAD_SIZE] = dq[tok + r * size : tok + (r + 1) * size]


def unpacked(second_ref, tok, kv_heads):
    parts = [second_ref[tok + i * PACK : tok + (i + 1) * PACK, :tok].astype(F32) for i in range(3)]
    packed = parts[0] + (parts[1] + parts[2])
    count = 2 * kv_heads
    return [jnp.concatenate([packed[i : i + 1], packed[count + i : count + i + 1]], 1) for i in range(count)]


def pair_kernel(t_ref, a_ref, b_ref, out_ref):
    tok, half = a_ref.shape
    odd = lax.rem(lax.axis_index("seq"), 2) == 1
    out_ref[:tok, :] = jnp.where(odd, t_ref[...], jnp.concatenate([a_ref[...], b_ref[:tok, :]], 1))
    out_ref[tok:, :half] = b_ref[tok:, :]
    out_ref[tok:, half:] = jnp.zeros((b_ref.shape[0] - tok, half), BF16)


def far_kernel(kv_ref, qf_ref, af_ref, bf_ref, qx_ref, px_ref, t_ref):
    seq, head = lax.axis_index("seq"), lax.axis_index("head")
    count = lax.axis_size("seq")
    tok = kv_ref.shape[0]
    kv_cols = kv_ref.shape[1] // 2
    kv_heads = kv_cols // HEAD_SIZE
    straight = jnp.logical_and(jnp.logical_not(causal_mask(tok, head)), seq + FAR < count)
    across = jnp.logical_and(lax.rem(seq, 2) == 1, seq + FAR - 1 < count)
    sources = [
        (own_order(qf_ref, head), jnp.concatenate([af_ref[...], bf_ref[:tok, :]], 1), unpacked(bf_ref, tok, kv_heads), straight),
        (own_order(qx_ref, head), px_ref[:tok, :], unpacked(px_ref, tok, kv_heads), across),
    ]
    scale = LOGIT_SCALE * LOG2E
    for g in range(kv_heads):
        kc, vc = columns(kv_cols, g)
        key, value = kv_ref[:, kc], kv_ref[:, vc]
        dk = jnp.zeros((tok, HEAD_SIZE), F32)
        dv = jnp.zeros((tok, HEAD_SIZE), F32)
        for q_rel, d_rel, stats, keep in sources:
            qg, dg = stacked(q_rel, g), stacked(d_rel, g)
            prob = jnp.exp2(dot(key, qg, 1, 1) * scale - stats[2 * g])
            prob = jnp.where(keep, prob, 0.0).astype(BF16)
            dp = dot(value, dg, 1, 1)
            ds = jnp.where(keep, prob.astype(F32) * (dp - stats[2 * g + 1]), 0.0).astype(BF16)
            dv = dv + dot(prob, dg, 1, 0)
            dk = dk + dot(ds, qg, 1, 0)
        t_ref[:, kc] = dk * LOGIT_SCALE
        t_ref[:, vc] = dv


def sum_kernel(*refs):
    total = refs[0][...].astype(F32)
    for ref in refs[1:-1]:
        total = total + ref[...].astype(F32)
    refs[-1][...] = total.astype(refs[-1].dtype)


def closing_kernel(own_ref, far_ref, hop_ref, pair_ref, near_ref, core_ref, y_ref, dk_ref, dv_ref, proj_ref):
    odd = lax.rem(lax.axis_index("seq"), 2) == 1
    proj_ref[...] = (near_ref[...].astype(F32) + core_ref[...].astype(F32) + y_ref[...].astype(F32)).astype(BF16)
    kept = jnp.where(odd, 0.0, pair_ref[: own_ref.shape[0], :].astype(F32))
    total = own_ref[...] + far_ref[...] + hop_ref[...].astype(F32) + kept
    kv_cols = dk_ref.shape[1]
    dk_ref[...] = total[:, :kv_cols].astype(BF16)
    dv_ref[...] = total[:, kv_cols:].astype(BF16)


def per_device(queries, keys, values, out_weight, out_grad):
    tok, q_cols = queries.shape
    kv_cols = keys.shape[1]
    kv_heads = kv_cols // HEAD_SIZE
    size = tok // 4
    rows = jax.ShapeDtypeStruct((size, out_weight.shape[1]), BF16)
    block = jax.ShapeDtypeStruct((tok, 2 * kv_cols), BF16)
    wide_block = jax.ShapeDtypeStruct((tok, 2 * kv_cols), F32)

    def call(kernel, name, outs, scratch, *operands, cost=SMALL):
        return pl.pallas_call(
            kernel,
            out_shape=outs,
            in_specs=[VMEM] * len(operands),
            out_specs=jax.tree.map(lambda _: VMEM, outs),
            scratch_shapes=scratch,
            compiler_params=pltpu.CompilerParams(vmem_limit_bytes=16 << 20),
            cost_estimate=cost,
            name=name,
        )(*operands)

    def gate(value, *others):
        return lax.optimization_barrier((value, *others))[0]

    kv = call(join_kernel, "join", block, [], keys, values)
    far_sent = call(functools.partial(either_kernel, is_lower), "far_sent", block, [], kv, queries)
    r1 = shifted(kv, 2)
    r2, q_far = far_swapped(lambda: kv, lambda: queries) if lax.axis_size("seq") > 2 * FAR else (far_swapped(*[lambda: far_sent] * 2))
    og_c = swapped(out_grad, "head", 1)
    og_y = swapped(out_grad, "head", 2)
    p0 = swapped(gate(kv, far_sent), "seq", 1)
    half_grad = jax.ShapeDtypeStruct((tok // 2, q_cols), BF16)
    grad_near = call(near_back_kernel, "near_back", half_grad, [], out_grad, og_c, out_weight, cost=LARGE)
    x1 = swapped(gate(r1, grad_near), "seq", 1)
    x2 = swapped(call(functools.partial(either_kernel, is_odd), "pick", block, [], r2, q_far, cost=LARGE), "seq", 1)
    og_yc = swapped(gate(og_y, r2, grad_near), "head", 1)
    first = jax.ShapeDtypeStruct((tok, q_cols // 2), BF16)
    second = jax.ShapeDtypeStruct((tok + 3 * PACK, q_cols // 2), BF16)
    grad_far, sent_first = call(far_back_kernel, "far_back", (half_grad, first), [], gate(og_y, x1), og_yc, out_weight, grad_near,
                                cost=LARGE)

    def down(value):
        return far_swapped(*[lambda: value] * 2)[1]

    far_first = down(sent_first)
    table = jax.ShapeDtypeStruct((8 * pl.cdiv(2 * kv_heads, 8), 2 * tok), F32)
    early = call(
        early_kernel,
        "attend_early",
        (
            jax.ShapeDtypeStruct((kv_heads, 4, tok, 2 * tok), F32),
            table,
            jax.ShapeDtypeStruct((kv_heads, HEAD_SIZE, 2 * tok), F32),
        ),
        [],
        queries, kv, gate(r1, p0), r2, x1,
    )
    attended, probs, stats, sent_second = call(
        forward_kernel,
        "attend",
        (
            jax.ShapeDtypeStruct((tok, q_cols), BF16),
            jax.ShapeDtypeStruct((kv_heads, 5, tok, 2 * tok), BF16),
            table,
            second,
        ),
        [],
        queries, p0, x2, *early, grad_near, grad_far,
    )
    far_second = down(sent_second)
    near_own, near_core, far_own, far_core = call(
        project_kernel, "project", (rows,) * 4, [], attended, out_weight
    )
    sent = swapped(gate(far_core, far_first), "head", 1)
    t_x = call(across_kernel, "across_grad", block, [], queries, x1, probs, stats, grad_near, gate(grad_far, far_core))
    d1 = swapped(t_x, "seq", 1)
    far_sum = call(sum_kernel, "far_sum", rows, [], far_own, sent)
    from_y = swapped(far_sum, "head", 2)

    query_gradient, t_own, t_1, t_z = call(
        backward_kernel,
        "attend_grad",
        (jax.ShapeDtypeStruct((tok, q_cols), BF16), wide_block, block, block),
        [],
        queries, kv, r1, r2, x1, p0, x2, probs, stats, grad_near, gate(grad_far, far_first),
        cost=LARGE,
    )
    e1 = shifted(call(sum_kernel, "hop_sum", block, [], t_1, d1), -2)
    pair = jax.ShapeDtypeStruct((second.shape[0], q_cols), BF16)
    pair = swapped(call(pair_kernel, "pair", pair, [], t_z, far_first, far_second), "seq", 1)
    from_core = swapped(gate(near_core, far_sum), "head", 1)
    t_far = call(far_kernel, "far_grad", wide_block, [],
                 kv, q_far, far_first, far_second, x2, pair, cost=MEDIUM)

    narrow = jax.ShapeDtypeStruct(keys.shape, BF16)
    key_gradient, value_gradient, projected = call(
        closing_kernel, "closing", (narrow, narrow, rows), [], t_own, t_far, e1, pair, near_own, from_core, from_y
    )
    return (projected, query_gradient, key_gradient, value_gradient)


def solution(mesh):
    return jax.shard_map(
        per_device,
        mesh=mesh,
        in_specs=(
            P("seq", "head"),
            P("seq", "head"),
            P("seq", "head"),
            P("head", None),
            P(("seq", "head"), None),
        ),
        out_specs=(P(("seq", "head"), None), P("seq", "head"), P("seq", "head"), P("seq", "head")),
        check_vma=False,
    )
```

```python
import functools

import jax
import jax.numpy as jnp
from jax import lax
from jax.experimental import pallas as pl
from jax.experimental.pallas import tpu as pltpu
from jax.sharding import PartitionSpec as P

HEAD_SIZE = 128
WIN = 1024
LOGIT_SCALE = 168.0 ** (-0.5)
LOG2E = 1.4426950408889634
NEG = -1e30
PACK = 16
FAR = 4
F32 = jnp.float32
BF16 = jnp.bfloat16
SMALL = pl.CostEstimate(flops=1, bytes_accessed=1, transcendentals=0)
MEDIUM = pl.CostEstimate(flops=1 * 10**8, bytes_accessed=1, transcendentals=0)
LARGE = pl.CostEstimate(flops=10**10, bytes_accessed=1, transcendentals=0)
VMEM = pl.BlockSpec(memory_space=pltpu.VMEM)


def dot(a, b, ca, cb):
    return lax.dot_general(a, b, (((ca,), (cb,)), ((), ())), preferred_element_type=F32)


def shifted(value, steps):
    count = lax.axis_size("seq")
    first, last = (max(0, -steps), min(count, count - steps))
    return lax.ppermute(value, "seq", [(i, i + steps) for i in range(first, last)])


def swapped(value, axis, bit):
    count = lax.axis_size(axis)
    return lax.ppermute(value, axis, [(i, i ^ bit) for i in range(count)])


def far_swapped(lower, upper):
    count = lax.axis_size("seq")
    side = lax.rem(lax.div(lax.axis_index("seq"), FAR), 2)
    rounds = []
    for r in range(2):
        pairs = [(i, i + FAR) for i in range(count - FAR) if (i // FAR) % 2 == r]
        if pairs:
            pairs = pairs + [(j, i) for i, j in pairs]
            rounds.append(lax.ppermute(lower() if lower is upper else jnp.where(side == r, lower(), upper()), "seq", pairs))
    if len(rounds) == 1:
        return rounds[0], rounds[0]
    return jnp.where(side == 1, rounds[0], rounds[1]), jnp.where(side == 0, rounds[0], rounds[1])


def group_rows(group, head, size):
    return pl.ds(pl.multiple_of(jnp.bitwise_xor(group, head) * size, size), size)


def own_order(ref, head):
    size = ref.shape[0] // 4
    return jnp.concatenate([ref[group_rows(g, head, size), :] for g in range(4)], 0)


def stacked(mat, kv_head):
    low = 2 * kv_head * HEAD_SIZE
    return jnp.concatenate([mat[:, low : low + HEAD_SIZE], mat[:, low + HEAD_SIZE : low + 2 * HEAD_SIZE]], 0)


def causal_mask(tok, head):
    key_pos = lax.broadcasted_iota(jnp.int32, (tok, 2 * tok), 0)
    lane = lax.broadcasted_iota(jnp.int32, (tok, 2 * tok), 1)
    query_pos = jnp.bitwise_xor(jnp.bitwise_and(lane, tok - 1), head * (tok // 4))
    return query_pos >= key_pos


def columns(kv_cols, kv_head):
    low = kv_head * HEAD_SIZE
    return slice(low, low + HEAD_SIZE), slice(kv_cols + low, kv_cols + low + HEAD_SIZE)


def window(kv_ref, r1_ref, r2_ref, x1_ref, p0_ref, x2_ref, odd, cols):
    return [kv_ref[:, cols], r1_ref[:, cols], r2_ref[:, cols], x1_ref[:, cols], jnp.where(odd, p0_ref[:, cols], x2_ref[:, cols])]


def join_kernel(k_ref, v_ref, kv_ref):
    cols = k_ref.shape[1]
    kv_ref[:, :cols] = k_ref[...]
    kv_ref[:, cols:] = v_ref[...]


def either_kernel(first, a_ref, b_ref, out_ref):
    out_ref[...] = jnp.where(first(lax.axis_index("seq")), a_ref[...], b_ref[...])


def is_odd(seq):
    return lax.rem(seq, 2) == 1


def is_lower(seq):
    return lax.rem(lax.div(seq, FAR), 2) == 0


def early_kernel(q_ref, kv_ref, r1_ref, r2_ref, x1_ref, e_ref, m_ref, part_ref):
    seq, head = lax.axis_index("seq"), lax.axis_index("head")
    tok = q_ref.shape[0]
    kv_cols = kv_ref.shape[1] // 2
    q_rel = own_order(q_ref, head)
    causal = causal_mask(tok, head)
    near = jnp.where(seq >= 2, 0.0, NEG).astype(F32)
    far = jnp.where(seq >= FAR, 0.0, NEG).astype(F32)
    biases = [None, near, far, near]
    scale = LOGIT_SCALE * LOG2E
    marks = []
    for g in range(kv_cols // HEAD_SIZE):
        kc, vc = columns(kv_cols, g)
        qg = stacked(q_rel, g)
        blocks = (kv_ref, r1_ref, r2_ref, x1_ref)
        scores = [dot(ref[:, kc], qg, 1, 1) for ref in blocks]
        scores[0] = jnp.where(causal, scores[0], NEG)
        scores[2] = jnp.where(causal, NEG, scores[2])
        tops = [jnp.max(sb, axis=0, keepdims=True) for sb in scores]
        tops = [t if b is None else t + b for t, b in zip(tops, biases)]
        top = jnp.maximum(jnp.maximum(tops[0], tops[1]), jnp.maximum(tops[2], tops[3])) * scale
        total = jnp.zeros_like(top)
        part = jnp.zeros((HEAD_SIZE, 2 * tok), F32)
        for b, bias in enumerate(biases):
            eb = jnp.exp2(scores[b] * scale - (top if bias is None else top - bias))
            e_ref[g, b] = eb
            total = total + jnp.sum(eb, axis=0, keepdims=True)
            part = part + dot(blocks[b][:, vc], eb.astype(BF16), 0, 0)
        part_ref[g] = part
        marks += [top, total]
    spare = jnp.zeros((m_ref.shape[0] - len(marks), 2 * tok), F32)
    m_ref[...] = jnp.concatenate(marks + [spare], 0)


def forward_kernel(q_ref, p0_ref, x2_ref, e_ref, m_ref, part_ref, dn_ref, df_ref,
                   o_ref, p_ref, stat_ref, second_ref):
    seq, head = lax.axis_index("seq"), lax.axis_index("head")
    odd = lax.rem(seq, 2) == 1
    tok = q_ref.shape[0]
    kv_cols = p0_ref.shape[1] // 2
    q_rel = own_order(q_ref, head)
    d_rel = jnp.concatenate([dn_ref[...], df_ref[...]], 0)
    bias = jnp.where(jnp.logical_or(odd, seq >= FAR), 0.0, NEG).astype(F32)
    scale = LOGIT_SCALE * LOG2E
    stats = []
    for g in range(kv_cols // HEAD_SIZE):
        kc, vc = columns(kv_cols, g)
        score = dot(jnp.where(odd, p0_ref[:, kc], x2_ref[:, kc]), stacked(q_rel, g), 1, 1)
        top_early = m_ref[2 * g : 2 * g + 1, :]
        top = jnp.maximum(top_early, (jnp.max(score, axis=0, keepdims=True) + bias) * scale)
        last = jnp.exp2(score * scale - (top - bias))
        shrink = jnp.exp2(top_early - top)
        total = m_ref[2 * g + 1 : 2 * g + 2, :] * shrink + jnp.sum(last, axis=0, keepdims=True)
        inv = 1.0 / total
        shrink = shrink * inv
        last = (last * inv).astype(BF16)
        p_ref[g, 4] = last
        out = part_ref[g] * shrink + dot(jnp.where(odd, p0_ref[:, vc], x2_ref[:, vc]), last, 0, 0)
        for b in range(4):
            p_ref[g, b] = (e_ref[g, b] * shrink).astype(BF16)
        out = out.astype(BF16)
        grad = stacked(d_rel, g)
        delta = jnp.sum(grad.astype(F32).T * out.astype(F32), axis=0, keepdims=True)
        stats += [top + jnp.log2(total), delta]
        out = out.astype(F32).T.astype(BF16)
        low = 2 * g * HEAD_SIZE
        o_ref[:, low : low + HEAD_SIZE] = out[:tok]
        o_ref[:, low + HEAD_SIZE : low + 2 * HEAD_SIZE] = out[tok:]
    spare = jnp.zeros((stat_ref.shape[0] - len(stats), 2 * tok), F32)
    stat_ref[...] = jnp.concatenate(stats + [spare], 0)
    half = d_rel.shape[1] // 2
    packed = jnp.concatenate([st[:, :tok] for st in stats] + [st[:, tok:] for st in stats], 0)
    packed = jnp.concatenate([packed, jnp.zeros((PACK - packed.shape[0], tok), F32)], 0)
    second_ref[:tok, :] = d_rel[:, half:]
    for part in range(3):
        rounded = packed.astype(BF16)
        second_ref[tok + part * PACK : tok + (part + 1) * PACK, :] = rounded
        packed = packed - rounded.astype(F32)


def project_kernel(o_ref, w_ref, *part_refs):
    size = part_refs[0].shape[0]
    cols = w_ref.shape[1]
    step = cols // 7 if cols % (7 * HEAD_SIZE) == 0 else cols
    for low in range(0, cols, step):
        part = dot(o_ref[...], w_ref[:, low : low + step], 1, 0).astype(BF16)
        for i, ref in enumerate(part_refs):
            ref[:, low : low + step] = part[i * size : (i + 1) * size]


def near_back_kernel(own_ref, core_ref, w_ref, d_ref):
    rows = jnp.concatenate([own_ref[...], core_ref[...]], 0)
    d_ref[...] = dot(rows, w_ref[...], 1, 1).astype(BF16)


def far_back_kernel(y_ref, yc_ref, w_ref, near_ref, d_ref, first_ref):
    rows = jnp.concatenate([y_ref[...], yc_ref[...]], 0)
    grad = dot(rows, w_ref[...], 1, 1).astype(BF16)
    d_ref[...] = grad
    cols = first_ref.shape[1]
    first_ref[...] = jnp.concatenate([near_ref[:, :cols], grad[:, :cols]], 0)


def across_kernel(q_ref, x1_ref, p_ref, stat_ref, dn_ref, df_ref, tx_ref):
    tok = q_ref.shape[0]
    kv_cols = x1_ref.shape[1] // 2
    q_rel = own_order(q_ref, lax.axis_index("head"))
    d_rel = jnp.concatenate([dn_ref[...], df_ref[...]], 0)
    for g in range(kv_cols // HEAD_SIZE):
        kc, vc = columns(kv_cols, g)
        qg, dg = stacked(q_rel, g), stacked(d_rel, g)
        pb = p_ref[g, 3]
        dp = dot(x1_ref[:, vc], dg, 1, 1)
        ds = (pb.astype(F32) * (dp - stat_ref[2 * g + 1 : 2 * g + 2, :])).astype(BF16)
        tx_ref[:, vc] = dot(pb, dg, 1, 0).astype(BF16)
        tx_ref[:, kc] = (dot(ds, qg, 1, 0) * LOGIT_SCALE).astype(BF16)


def backward_kernel(q_ref, kv_ref, r1_ref, r2_ref, x1_ref, p0_ref, x2_ref, p_ref, stat_ref, dn_ref, df_ref,
                    dq_ref, town_ref, t1_ref, tz_ref):
    seq, head = lax.axis_index("seq"), lax.axis_index("head")
    odd = lax.rem(seq, 2) == 1
    tok = q_ref.shape[0]
    kv_cols = kv_ref.shape[1] // 2
    size = tok // 4
    q_rel = own_order(q_ref, head)
    d_rel = jnp.concatenate([dn_ref[...], df_ref[...]], 0)
    outs = [town_ref, t1_ref, None, None, tz_ref]
    for g in range(kv_cols // HEAD_SIZE):
        kc, vc = columns(kv_cols, g)
        qg, dg = stacked(q_rel, g), stacked(d_rel, g)
        blocks = (kv_ref, r1_ref, r2_ref, x1_ref, p0_ref, x2_ref)
        key_blocks, value_blocks = window(*blocks, odd, kc), window(*blocks, odd, vc)
        delta = stat_ref[2 * g + 1 : 2 * g + 2, :]
        dq = jnp.zeros((HEAD_SIZE, 2 * tok), F32)
        for b in range(5):
            pb = p_ref[g, b]
            dp = dot(value_blocks[b], dg, 1, 1)
            ds = (pb.astype(F32) * (dp - delta)).astype(BF16)
            if outs[b] is not None:
                outs[b][:, vc] = dot(pb, dg, 1, 0).astype(outs[b].dtype)
                outs[b][:, kc] = (dot(ds, qg, 1, 0) * LOGIT_SCALE).astype(outs[b].dtype)
            dq = dq + dot(key_blocks[b], ds, 0, 0)
        dq = (dq * LOGIT_SCALE).T.astype(BF16)
        low = 2 * g * HEAD_SIZE
        for r in range(4):
            rows = group_rows(r, head, size)
            dq_ref[rows, low : low + HEAD_SIZE] = dq[r * size : (r + 1) * size]
            dq_ref[rows, low + HEAD_SIZE : low + 2 * HEAD_SIZE] = dq[tok + r * size : tok + (r + 1) * size]


def unpacked(second_ref, tok, kv_heads):
    parts = [second_ref[tok + i * PACK : tok + (i + 1) * PACK, :tok].astype(F32) for i in range(3)]
    packed = parts[0] + (parts[1] + parts[2])
    count = 2 * kv_heads
    return [jnp.concatenate([packed[i : i + 1], packed[count + i : count + i + 1]], 1) for i in range(count)]


def pair_kernel(t_ref, a_ref, b_ref, out_ref):
    tok, half = a_ref.shape
    odd = lax.rem(lax.axis_index("seq"), 2) == 1
    out_ref[:tok, :] = jnp.where(odd, t_ref[...], jnp.concatenate([a_ref[...], b_ref[:tok, :]], 1))
    out_ref[tok:, :half] = b_ref[tok:, :]
    out_ref[tok:, half:] = jnp.zeros((b_ref.shape[0] - tok, half), BF16)


def far_kernel(kv_ref, qf_ref, af_ref, bf_ref, qx_ref, px_ref, t_ref):
    seq, head = lax.axis_index("seq"), lax.axis_index("head")
    count = lax.axis_size("seq")
    tok = kv_ref.shape[0]
    kv_cols = kv_ref.shape[1] // 2
    kv_heads = kv_cols // HEAD_SIZE
    straight = jnp.logical_and(jnp.logical_not(causal_mask(tok, head)), seq + FAR < count)
    across = jnp.logical_and(lax.rem(seq, 2) == 1, seq + FAR - 1 < count)
    sources = [
        (own_order(qf_ref, head), jnp.concatenate([af_ref[...], bf_ref[:tok, :]], 1), unpacked(bf_ref, tok, kv_heads), straight),
        (own_order(qx_ref, head), px_ref[:tok, :], unpacked(px_ref, tok, kv_heads), across),
    ]
    scale = LOGIT_SCALE * LOG2E
    for g in range(kv_heads):
        kc, vc = columns(kv_cols, g)
        key, value = kv_ref[:, kc], kv_ref[:, vc]
        dk = jnp.zeros((tok, HEAD_SIZE), F32)
        dv = jnp.zeros((tok, HEAD_SIZE), F32)
        for q_rel, d_rel, stats, keep in sources:
            qg, dg = stacked(q_rel, g), stacked(d_rel, g)
            prob = jnp.exp2(dot(key, qg, 1, 1) * scale - stats[2 * g])
            prob = jnp.where(keep, prob, 0.0).astype(BF16)
            dp = dot(value, dg, 1, 1)
            ds = jnp.where(keep, prob.astype(F32) * (dp - stats[2 * g + 1]), 0.0).astype(BF16)
            dv = dv + dot(prob, dg, 1, 0)
            dk = dk + dot(ds, qg, 1, 0)
        t_ref[:, kc] = dk * LOGIT_SCALE
        t_ref[:, vc] = dv


def sum_kernel(*refs):
    total = refs[0][...].astype(F32)
    for ref in refs[1:-1]:
        total = total + ref[...].astype(F32)
    refs[-1][...] = total.astype(refs[-1].dtype)


def closing_kernel(own_ref, far_ref, hop_ref, pair_ref, near_ref, core_ref, y_ref, dk_ref, dv_ref, proj_ref):
    odd = lax.rem(lax.axis_index("seq"), 2) == 1
    proj_ref[...] = (near_ref[...].astype(F32) + core_ref[...].astype(F32) + y_ref[...].astype(F32)).astype(BF16)
    kept = jnp.where(odd, 0.0, pair_ref[: own_ref.shape[0], :].astype(F32))
    total = own_ref[...] + far_ref[...] + hop_ref[...].astype(F32) + kept
    kv_cols = dk_ref.shape[1]
    dk_ref[...] = total[:, :kv_cols].astype(BF16)
    dv_ref[...] = total[:, kv_cols:].astype(BF16)


def per_device(queries, keys, values, out_weight, out_grad):
    tok, q_cols = queries.shape
    kv_cols = keys.shape[1]
    kv_heads = kv_cols // HEAD_SIZE
    size = tok // 4
    rows = jax.ShapeDtypeStruct((size, out_weight.shape[1]), BF16)
    block = jax.ShapeDtypeStruct((tok, 2 * kv_cols), BF16)
    wide_block = jax.ShapeDtypeStruct((tok, 2 * kv_cols), F32)

    def call(kernel, name, outs, scratch, *operands, cost=SMALL):
        return pl.pallas_call(
            kernel,
            out_shape=outs,
            in_specs=[VMEM] * len(operands),
            out_specs=jax.tree.map(lambda _: VMEM, outs),
            scratch_shapes=scratch,
            compiler_params=pltpu.CompilerParams(vmem_limit_bytes=16 << 20),
            cost_estimate=cost,
            name=name,
        )(*operands)

    def gate(value, *others):
        return lax.optimization_barrier((value, *others))[0]

    kv = call(join_kernel, "join", block, [], keys, values)
    far_sent = call(functools.partial(either_kernel, is_lower), "far_sent", block, [], kv, queries)
    r1 = shifted(kv, 2)
    r2, q_far = far_swapped(lambda: kv, lambda: queries) if lax.axis_size("seq") > 2 * FAR else (far_swapped(*[lambda: far_sent] * 2))
    og_c = swapped(out_grad, "head", 1)
    og_y = swapped(out_grad, "head", 2)
    p0 = swapped(gate(kv, far_sent), "seq", 1)
    half_grad = jax.ShapeDtypeStruct((tok // 2, q_cols), BF16)
    grad_near = call(near_back_kernel, "near_back", half_grad, [], out_grad, og_c, out_weight, cost=LARGE)
    x1 = swapped(gate(r1, grad_near), "seq", 1)
    x2 = swapped(call(functools.partial(either_kernel, is_odd), "pick", block, [], r2, q_far, cost=LARGE), "seq", 1)
    og_yc = swapped(gate(og_y, r2, grad_near), "head", 1)
    first = jax.ShapeDtypeStruct((tok, q_cols // 2), BF16)
    second = jax.ShapeDtypeStruct((tok + 3 * PACK, q_cols // 2), BF16)
    grad_far, sent_first = call(far_back_kernel, "far_back", (half_grad, first), [], og_y, og_yc, out_weight, grad_near,
                                cost=SMALL)

    def down(value):
        return far_swapped(*[lambda: value] * 2)[1]

    far_first = down(sent_first)
    table = jax.ShapeDtypeStruct((8 * pl.cdiv(2 * kv_heads, 8), 2 * tok), F32)
    early = call(
        early_kernel,
        "attend_early",
        (
            jax.ShapeDtypeStruct((kv_heads, 4, tok, 2 * tok), F32),
            table,
            jax.ShapeDtypeStruct((kv_heads, HEAD_SIZE, 2 * tok), F32),
        ),
        [],
        queries, kv, gate(r1, p0), r2, x1,
        cost=SMALL,
    )
    attended, probs, stats, sent_second = call(
        forward_kernel,
        "attend",
        (
            jax.ShapeDtypeStruct((tok, q_cols), BF16),
            jax.ShapeDtypeStruct((kv_heads, 5, tok, 2 * tok), BF16),
            table,
            second,
        ),
        [],
        queries, p0, x2, *early, grad_near, grad_far,
    )
    t_x = call(across_kernel, "across_grad", block, [], queries, x1, probs, stats, grad_near, grad_far)
    d1 = swapped(t_x, "seq", 1)
    far_second = down(sent_second)
    near_own, near_core, far_own, far_core = call(
        project_kernel, "project", (rows,) * 4, [], gate(attended, t_x), out_weight
    )
    sent = swapped(gate(far_core, far_first), "head", 1)
    far_sum = call(sum_kernel, "far_sum", rows, [], far_own, sent)
    from_y = swapped(far_sum, "head", 2)

    query_gradient, t_own, t_1, t_z = call(
        backward_kernel,
        "attend_grad",
        (jax.ShapeDtypeStruct((tok, q_cols), BF16), wide_block, block, block),
        [],
        queries, kv, r1, r2, x1, p0, x2, probs, stats, grad_near, gate(grad_far, far_first),
        cost=LARGE,
    )
    e1 = shifted(call(sum_kernel, "hop_sum", block, [], t_1, d1), -2)
    pair = jax.ShapeDtypeStruct((second.shape[0], q_cols), BF16)
    pair = swapped(call(pair_kernel, "pair", pair, [], t_z, far_first, far_second), "seq", 1)
    from_core = swapped(gate(near_core, far_sum), "head", 1)
    t_far = call(far_kernel, "far_grad", wide_block, [],
                 kv, q_far, far_first, far_second, x2, pair, cost=MEDIUM)

    narrow = jax.ShapeDtypeStruct(keys.shape, BF16)
    key_gradient, value_gradient, projected = call(
        closing_kernel, "closing", (narrow, narrow, rows), [], t_own, t_far, e1, pair, near_own, from_core, from_y
    )
    return (projected, query_gradient, key_gradient, value_gradient)


def solution(mesh):
    return jax.shard_map(
        per_device,
        mesh=mesh,
        in_specs=(
            P("seq", "head"),
            P("seq", "head"),
            P("seq", "head"),
            P("head", None),
            P(("seq", "head"), None),
        ),
        out_specs=(P(("seq", "head"), None), P("seq", "head"), P("seq", "head"), P("seq", "head")),
        check_vma=False,
    )
```

```python
import functools

import jax
import jax.numpy as jnp
from jax import lax
from jax.experimental import pallas as pl
from jax.experimental.pallas import tpu as pltpu
from jax.sharding import PartitionSpec as P

HEAD_SIZE = 128
WIN = 1024
LOGIT_SCALE = 168.0 ** (-0.5)
LOG2E = 1.4426950408889634
NEG = -1e30
PACK = 16
FAR = 4
F32 = jnp.float32
BF16 = jnp.bfloat16
SMALL = pl.CostEstimate(flops=1, bytes_accessed=1, transcendentals=0)
MEDIUM = pl.CostEstimate(flops=1 * 10**8, bytes_accessed=1, transcendentals=0)
LARGE = pl.CostEstimate(flops=10**10, bytes_accessed=1, transcendentals=0)
VMEM = pl.BlockSpec(memory_space=pltpu.VMEM)


def dot(a, b, ca, cb):
    return lax.dot_general(a, b, (((ca,), (cb,)), ((), ())), preferred_element_type=F32)


def shifted(value, steps):
    count = lax.axis_size("seq")
    first, last = (max(0, -steps), min(count, count - steps))
    return lax.ppermute(value, "seq", [(i, i + steps) for i in range(first, last)])


def swapped(value, axis, bit):
    count = lax.axis_size(axis)
    return lax.ppermute(value, axis, [(i, i ^ bit) for i in range(count)])


def far_swapped(lower, upper):
    count = lax.axis_size("seq")
    side = lax.rem(lax.div(lax.axis_index("seq"), FAR), 2)
    rounds = []
    for r in range(2):
        pairs = [(i, i + FAR) for i in range(count - FAR) if (i // FAR) % 2 == r]
        if pairs:
            pairs = pairs + [(j, i) for i, j in pairs]
            rounds.append(lax.ppermute(lower() if lower is upper else jnp.where(side == r, lower(), upper()), "seq", pairs))
    if len(rounds) == 1:
        return rounds[0], rounds[0]
    return jnp.where(side == 1, rounds[0], rounds[1]), jnp.where(side == 0, rounds[0], rounds[1])


def group_rows(group, head, size):
    return pl.ds(pl.multiple_of(jnp.bitwise_xor(group, head) * size, size), size)


def own_order(ref, head):
    size = ref.shape[0] // 4
    return jnp.concatenate([ref[group_rows(g, head, size), :] for g in range(4)], 0)


def stacked(mat, kv_head):
    low = 2 * kv_head * HEAD_SIZE
    return jnp.concatenate([mat[:, low : low + HEAD_SIZE], mat[:, low + HEAD_SIZE : low + 2 * HEAD_SIZE]], 0)


def causal_mask(tok, head):
    key_pos = lax.broadcasted_iota(jnp.int32, (tok, 2 * tok), 0)
    lane = lax.broadcasted_iota(jnp.int32, (tok, 2 * tok), 1)
    query_pos = jnp.bitwise_xor(jnp.bitwise_and(lane, tok - 1), head * (tok // 4))
    return query_pos >= key_pos


def columns(kv_cols, kv_head):
    low = kv_head * HEAD_SIZE
    return slice(low, low + HEAD_SIZE), slice(kv_cols + low, kv_cols + low + HEAD_SIZE)


def window(kv_ref, r1_ref, r2_ref, x1_ref, p0_ref, x2_ref, odd, cols):
    return [kv_ref[:, cols], r1_ref[:, cols], r2_ref[:, cols], x1_ref[:, cols], jnp.where(odd, p0_ref[:, cols], x2_ref[:, cols])]


def join_kernel(k_ref, v_ref, kv_ref):
    cols = k_ref.shape[1]
    kv_ref[:, :cols] = k_ref[...]
    kv_ref[:, cols:] = v_ref[...]


def either_kernel(first, a_ref, b_ref, out_ref):
    out_ref[...] = jnp.where(first(lax.axis_index("seq")), a_ref[...], b_ref[...])


def is_odd(seq):
    return lax.rem(seq, 2) == 1


def is_lower(seq):
    return lax.rem(lax.div(seq, FAR), 2) == 0


def early_kernel(q_ref, kv_ref, r1_ref, r2_ref, x1_ref, e_ref, m_ref, part_ref):
    seq, head = lax.axis_index("seq"), lax.axis_index("head")
    tok = q_ref.shape[0]
    kv_cols = kv_ref.shape[1] // 2
    q_rel = own_order(q_ref, head)
    causal = causal_mask(tok, head)
    near = jnp.where(seq >= 2, 0.0, NEG).astype(F32)
    far = jnp.where(seq >= FAR, 0.0, NEG).astype(F32)
    biases = [None, near, far, near]
    scale = LOGIT_SCALE * LOG2E
    marks = []
    for g in range(kv_cols // HEAD_SIZE):
        kc, vc = columns(kv_cols, g)
        qg = stacked(q_rel, g)
        blocks = (kv_ref, r1_ref, r2_ref, x1_ref)
        scores = [dot(ref[:, kc], qg, 1, 1) for ref in blocks]
        scores[0] = jnp.where(causal, scores[0], NEG)
        scores[2] = jnp.where(causal, NEG, scores[2])
        tops = [jnp.max(sb, axis=0, keepdims=True) for sb in scores]
        tops = [t if b is None else t + b for t, b in zip(tops, biases)]
        top = jnp.maximum(jnp.maximum(tops[0], tops[1]), jnp.maximum(tops[2], tops[3])) * scale
        total = jnp.zeros_like(top)
        part = jnp.zeros((HEAD_SIZE, 2 * tok), F32)
        for b, bias in enumerate(biases):
            eb = jnp.exp2(scores[b] * scale - (top if bias is None else top - bias))
            e_ref[g, b] = eb
            total = total + jnp.sum(eb, axis=0, keepdims=True)
            part = part + dot(blocks[b][:, vc], eb.astype(BF16), 0, 0)
        part_ref[g] = part
        marks += [top, total]
    spare = jnp.zeros((m_ref.shape[0] - len(marks), 2 * tok), F32)
    m_ref[...] = jnp.concatenate(marks + [spare], 0)


def forward_kernel(q_ref, p0_ref, x2_ref, e_ref, m_ref, part_ref, dn_ref, df_ref,
                   o_ref, p_ref, stat_ref, second_ref):
    seq, head = lax.axis_index("seq"), lax.axis_index("head")
    odd = lax.rem(seq, 2) == 1
    tok = q_ref.shape[0]
    kv_cols = p0_ref.shape[1] // 2
    q_rel = own_order(q_ref, head)
    d_rel = jnp.concatenate([dn_ref[...], df_ref[...]], 0)
    bias = jnp.where(jnp.logical_or(odd, seq >= FAR), 0.0, NEG).astype(F32)
    scale = LOGIT_SCALE * LOG2E
    stats = []
    for g in range(kv_cols // HEAD_SIZE):
        kc, vc = columns(kv_cols, g)
        score = dot(jnp.where(odd, p0_ref[:, kc], x2_ref[:, kc]), stacked(q_rel, g), 1, 1)
        top_early = m_ref[2 * g : 2 * g + 1, :]
        top = jnp.maximum(top_early, (jnp.max(score, axis=0, keepdims=True) + bias) * scale)
        last = jnp.exp2(score * scale - (top - bias))
        shrink = jnp.exp2(top_early - top)
        total = m_ref[2 * g + 1 : 2 * g + 2, :] * shrink + jnp.sum(last, axis=0, keepdims=True)
        inv = 1.0 / total
        shrink = shrink * inv
        last = (last * inv).astype(BF16)
        p_ref[g, 4] = last
        out = part_ref[g] * shrink + dot(jnp.where(odd, p0_ref[:, vc], x2_ref[:, vc]), last, 0, 0)
        for b in range(4):
            p_ref[g, b] = (e_ref[g, b] * shrink).astype(BF16)
        out = out.astype(BF16)
        grad = stacked(d_rel, g)
        delta = jnp.sum(grad.astype(F32).T * out.astype(F32), axis=0, keepdims=True)
        stats += [top + jnp.log2(total), delta]
        out = out.astype(F32).T.astype(BF16)
        low = 2 * g * HEAD_SIZE
        o_ref[:, low : low + HEAD_SIZE] = out[:tok]
        o_ref[:, low + HEAD_SIZE : low + 2 * HEAD_SIZE] = out[tok:]
    spare = jnp.zeros((stat_ref.shape[0] - len(stats), 2 * tok), F32)
    stat_ref[...] = jnp.concatenate(stats + [spare], 0)
    width = second_ref.shape[1]
    packed = jnp.concatenate([st[:, :tok] for st in stats] + [st[:, tok:] for st in stats], 0)
    packed = jnp.concatenate([packed, jnp.zeros((PACK - packed.shape[0], tok), F32)], 0)
    second_ref[:tok, :] = d_rel[:, d_rel.shape[1] - width :]
    for part in range(3):
        rounded = packed.astype(BF16)
        for c, rows in enumerate(part_rows(part, tok, width)):
            second_ref[rows, :] = rounded[:, c * width : (c + 1) * width]
        packed = packed - rounded.astype(F32)


def part_rows(part, tok, width):
    pieces = tok // width
    return [slice(tok + (part * pieces + c) * PACK, tok + (part * pieces + c + 1) * PACK) for c in range(pieces)]


def project_kernel(o_ref, w_ref, *part_refs):
    size = part_refs[0].shape[0]
    cols = w_ref.shape[1]
    step = cols // 7 if cols % (7 * HEAD_SIZE) == 0 else cols
    for low in range(0, cols, step):
        part = dot(o_ref[...], w_ref[:, low : low + step], 1, 0).astype(BF16)
        for i, ref in enumerate(part_refs):
            ref[:, low : low + step] = part[i * size : (i + 1) * size]


def near_back_kernel(own_ref, core_ref, w_ref, d_ref):
    rows = jnp.concatenate([own_ref[...], core_ref[...]], 0)
    d_ref[...] = dot(rows, w_ref[...], 1, 1).astype(BF16)


def far_back_kernel(y_ref, yc_ref, w_ref, near_ref, d_ref, first_ref):
    rows = jnp.concatenate([y_ref[...], yc_ref[...]], 0)
    grad = dot(rows, w_ref[...], 1, 1).astype(BF16)
    d_ref[...] = grad
    cols = first_ref.shape[1]
    first_ref[...] = jnp.concatenate([near_ref[:, :cols], grad[:, :cols]], 0)


def across_kernel(q_ref, x1_ref, p_ref, stat_ref, dn_ref, df_ref, tx_ref):
    tok = q_ref.shape[0]
    kv_cols = x1_ref.shape[1] // 2
    q_rel = own_order(q_ref, lax.axis_index("head"))
    d_rel = jnp.concatenate([dn_ref[...], df_ref[...]], 0)
    for g in range(kv_cols // HEAD_SIZE):
        kc, vc = columns(kv_cols, g)
        qg, dg = stacked(q_rel, g), stacked(d_rel, g)
        pb = p_ref[g, 3]
        dp = dot(x1_ref[:, vc], dg, 1, 1)
        ds = (pb.astype(F32) * (dp - stat_ref[2 * g + 1 : 2 * g + 2, :])).astype(BF16)
        tx_ref[:, vc] = dot(pb, dg, 1, 0).astype(BF16)
        tx_ref[:, kc] = (dot(ds, qg, 1, 0) * LOGIT_SCALE).astype(BF16)


def backward_kernel(q_ref, kv_ref, r1_ref, r2_ref, x1_ref, p0_ref, x2_ref, p_ref, stat_ref, dn_ref, df_ref,
                    dq_ref, town_ref, t1_ref, tz_ref):
    seq, head = lax.axis_index("seq"), lax.axis_index("head")
    odd = lax.rem(seq, 2) == 1
    tok = q_ref.shape[0]
    kv_cols = kv_ref.shape[1] // 2
    size = tok // 4
    q_rel = own_order(q_ref, head)
    d_rel = jnp.concatenate([dn_ref[...], df_ref[...]], 0)
    outs = [town_ref, t1_ref, None, None, tz_ref]
    for g in range(kv_cols // HEAD_SIZE):
        kc, vc = columns(kv_cols, g)
        qg, dg = stacked(q_rel, g), stacked(d_rel, g)
        blocks = (kv_ref, r1_ref, r2_ref, x1_ref, p0_ref, x2_ref)
        key_blocks, value_blocks = window(*blocks, odd, kc), window(*blocks, odd, vc)
        delta = stat_ref[2 * g + 1 : 2 * g + 2, :]
        dq = jnp.zeros((HEAD_SIZE, 2 * tok), F32)
        for b in range(5):
            pb = p_ref[g, b]
            dp = dot(value_blocks[b], dg, 1, 1)
            ds = (pb.astype(F32) * (dp - delta)).astype(BF16)
            if outs[b] is not None:
                outs[b][:, vc] = dot(pb, dg, 1, 0).astype(outs[b].dtype)
                outs[b][:, kc] = (dot(ds, qg, 1, 0) * LOGIT_SCALE).astype(outs[b].dtype)
            dq = dq + dot(key_blocks[b], ds, 0, 0)
        dq = (dq * LOGIT_SCALE).T.astype(BF16)
        low = 2 * g * HEAD_SIZE
        for r in range(4):
            rows = group_rows(r, head, size)
            dq_ref[rows, low : low + HEAD_SIZE] = dq[r * size : (r + 1) * size]
            dq_ref[rows, low + HEAD_SIZE : low + 2 * HEAD_SIZE] = dq[tok + r * size : tok + (r + 1) * size]


def unpacked(ref, tok, width, kv_heads):
    parts = [
        jnp.concatenate([ref[rows, :width] for rows in part_rows(part, tok, width)], 1).astype(F32) for part in range(3)
    ]
    packed = parts[0] + (parts[1] + parts[2])
    count = 2 * kv_heads
    return [jnp.concatenate([packed[i : i + 1], packed[count + i : count + i + 1]], 1) for i in range(count)]


def pair_kernel(t_ref, a_ref, b_ref, out_ref):
    tok, width = a_ref.shape[0], b_ref.shape[1]
    odd = lax.rem(lax.axis_index("seq"), 2) == 1
    out_ref[:tok, :] = jnp.where(odd, t_ref[...], jnp.concatenate([a_ref[...], b_ref[:tok, :]], 1))
    for part in range(3):
        (into,) = part_rows(part, tok, tok)
        out_ref[into, :tok] = jnp.concatenate([b_ref[rows, :] for rows in part_rows(part, tok, width)], 1)
    out_ref[tok:, tok:] = jnp.zeros((out_ref.shape[0] - tok, out_ref.shape[1] - tok), BF16)


def far_kernel(kv_ref, qf_ref, af_ref, bf_ref, qx_ref, px_ref, t_ref):
    seq, head = lax.axis_index("seq"), lax.axis_index("head")
    count = lax.axis_size("seq")
    tok = kv_ref.shape[0]
    kv_cols = kv_ref.shape[1] // 2
    kv_heads = kv_cols // HEAD_SIZE
    straight = jnp.logical_and(jnp.logical_not(causal_mask(tok, head)), seq + FAR < count)
    across = jnp.logical_and(lax.rem(seq, 2) == 1, seq + FAR - 1 < count)
    sources = [
        (own_order(qf_ref, head), jnp.concatenate([af_ref[...], bf_ref[:tok, :]], 1), unpacked(bf_ref, tok, bf_ref.shape[1], kv_heads), straight),
        (own_order(qx_ref, head), px_ref[:tok, :], unpacked(px_ref, tok, tok, kv_heads), across),
    ]
    scale = LOGIT_SCALE * LOG2E
    for g in range(kv_heads):
        kc, vc = columns(kv_cols, g)
        key, value = kv_ref[:, kc], kv_ref[:, vc]
        dk = jnp.zeros((tok, HEAD_SIZE), F32)
        dv = jnp.zeros((tok, HEAD_SIZE), F32)
        for q_rel, d_rel, stats, keep in sources:
            qg, dg = stacked(q_rel, g), stacked(d_rel, g)
            prob = jnp.exp2(dot(key, qg, 1, 1) * scale - stats[2 * g])
            prob = jnp.where(keep, prob, 0.0).astype(BF16)
            dp = dot(value, dg, 1, 1)
            ds = jnp.where(keep, prob.astype(F32) * (dp - stats[2 * g + 1]), 0.0).astype(BF16)
            dv = dv + dot(prob, dg, 1, 0)
            dk = dk + dot(ds, qg, 1, 0)
        t_ref[:, kc] = dk * LOGIT_SCALE
        t_ref[:, vc] = dv


def sum_kernel(*refs):
    total = refs[0][...].astype(F32)
    for ref in refs[1:-1]:
        total = total + ref[...].astype(F32)
    refs[-1][...] = total.astype(refs[-1].dtype)


def closing_kernel(own_ref, far_ref, hop_ref, pair_ref, near_ref, core_ref, y_ref, dk_ref, dv_ref, proj_ref):
    odd = lax.rem(lax.axis_index("seq"), 2) == 1
    proj_ref[...] = (near_ref[...].astype(F32) + core_ref[...].astype(F32) + y_ref[...].astype(F32)).astype(BF16)
    kept = jnp.where(odd, 0.0, pair_ref[: own_ref.shape[0], :].astype(F32))
    total = own_ref[...] + far_ref[...] + hop_ref[...].astype(F32) + kept
    kv_cols = dk_ref.shape[1]
    dk_ref[...] = total[:, :kv_cols].astype(BF16)
    dv_ref[...] = total[:, kv_cols:].astype(BF16)


def per_device(queries, keys, values, out_weight, out_grad):
    tok, q_cols = queries.shape
    kv_cols = keys.shape[1]
    kv_heads = kv_cols // HEAD_SIZE
    size = tok // 4
    rows = jax.ShapeDtypeStruct((size, out_weight.shape[1]), BF16)
    block = jax.ShapeDtypeStruct((tok, 2 * kv_cols), BF16)
    wide_block = jax.ShapeDtypeStruct((tok, 2 * kv_cols), F32)

    def call(kernel, name, outs, scratch, *operands, cost=SMALL):
        return pl.pallas_call(
            kernel,
            out_shape=outs,
            in_specs=[VMEM] * len(operands),
            out_specs=jax.tree.map(lambda _: VMEM, outs),
            scratch_shapes=scratch,
            compiler_params=pltpu.CompilerParams(vmem_limit_bytes=16 << 20),
            cost_estimate=cost,
            name=name,
        )(*operands)

    def gate(value, *others):
        return lax.optimization_barrier((value, *others))[0]

    kv = call(join_kernel, "join", block, [], keys, values)
    far_sent = call(functools.partial(either_kernel, is_lower), "far_sent", block, [], kv, queries)
    r1 = shifted(kv, 2)
    r2, q_far = far_swapped(lambda: kv, lambda: queries) if lax.axis_size("seq") > 2 * FAR else (far_swapped(*[lambda: far_sent] * 2))
    og_c = swapped(out_grad, "head", 1)
    og_y = swapped(out_grad, "head", 2)
    p0 = swapped(gate(kv, far_sent), "seq", 1)
    half_grad = jax.ShapeDtypeStruct((tok // 2, q_cols), BF16)
    grad_near = call(near_back_kernel, "near_back", half_grad, [], out_grad, og_c, out_weight, cost=LARGE)
    x1 = swapped(gate(r1, grad_near), "seq", 1)
    x2 = swapped(call(functools.partial(either_kernel, is_odd), "pick", block, [], r2, q_far, cost=LARGE), "seq", 1)
    og_yc = swapped(gate(og_y, r2, grad_near), "head", 1)
    rest = q_cols // 4
    first = jax.ShapeDtypeStruct((tok, q_cols - rest), BF16)
    second = jax.ShapeDtypeStruct((tok + 3 * PACK * (tok // rest), rest), BF16)
    grad_far, sent_first = call(far_back_kernel, "far_back", (half_grad, first), [], og_y, og_yc, out_weight, grad_near,
                                cost=SMALL)

    def down(value):
        return far_swapped(*[lambda: value] * 2)[1]

    far_first = down(sent_first)
    table = jax.ShapeDtypeStruct((8 * pl.cdiv(2 * kv_heads, 8), 2 * tok), F32)
    early = call(
        early_kernel,
        "attend_early",
        (
            jax.ShapeDtypeStruct((kv_heads, 4, tok, 2 * tok), F32),
            table,
            jax.ShapeDtypeStruct((kv_heads, HEAD_SIZE, 2 * tok), F32),
        ),
        [],
        queries, kv, gate(r1, p0), r2, x1,
        cost=SMALL,
    )
    attended, probs, stats, sent_second = call(
        forward_kernel,
        "attend",
        (
            jax.ShapeDtypeStruct((tok, q_cols), BF16),
            jax.ShapeDtypeStruct((kv_heads, 5, tok, 2 * tok), BF16),
            table,
            second,
        ),
        [],
        queries, p0, x2, *early, grad_near, grad_far,
    )
    t_x = call(across_kernel, "across_grad", block, [], queries, x1, probs, stats, grad_near, grad_far)
    d1 = swapped(t_x, "seq", 1)
    near_own, near_core, far_own, far_core = call(
        project_kernel, "project", (rows,) * 4, [], gate(attended, t_x), out_weight
    )
    sent = swapped(gate(far_core, far_first), "head", 1)
    far_sum = call(sum_kernel, "far_sum", rows, [], far_own, sent)
    from_y = swapped(far_sum, "head", 2)
    far_second = down(gate(sent_second, far_sum))

    query_gradient, t_own, t_1, t_z = call(
        backward_kernel,
        "attend_grad",
        (jax.ShapeDtypeStruct((tok, q_cols), BF16), wide_block, block, block),
        [],
        queries, kv, r1, r2, x1, p0, x2, probs, stats, grad_near, gate(grad_far, far_first),
        cost=LARGE,
    )
    e1 = shifted(call(sum_kernel, "hop_sum", block, [], t_1, d1), -2)
    pair = jax.ShapeDtypeStruct((tok + 3 * PACK, q_cols), BF16)
    pair = swapped(call(pair_kernel, "pair", pair, [], t_z, far_first, far_second), "seq", 1)
    from_core = swapped(gate(near_core, far_sum), "head", 1)
    t_far = call(far_kernel, "far_grad", wide_block, [],
                 kv, q_far, far_first, far_second, x2, pair, cost=MEDIUM)

    narrow = jax.ShapeDtypeStruct(keys.shape, BF16)
    key_gradient, value_gradient, projected = call(
        closing_kernel, "closing", (narrow, narrow, rows), [], t_own, t_far, e1, pair, near_own, from_core, from_y
    )
    return (projected, query_gradient, key_gradient, value_gradient)


def solution(mesh):
    return jax.shard_map(
        per_device,
        mesh=mesh,
        in_specs=(
            P("seq", "head"),
            P("seq", "head"),
            P("seq", "head"),
            P("head", None),
            P(("seq", "head"), None),
        ),
        out_specs=(P(("seq", "head"), None), P("seq", "head"), P("seq", "head"), P("seq", "head")),
        check_vma=False,
    )
```

```python
import functools

import jax
import jax.numpy as jnp
from jax import lax
from jax.experimental import pallas as pl
from jax.experimental.pallas import tpu as pltpu
from jax.sharding import PartitionSpec as P

HEAD_SIZE = 128
WIN = 1024
LOGIT_SCALE = 168.0 ** (-0.5)
LOG2E = 1.4426950408889634
NEG = -1e30
PACK = 16
FAR = 4
F32 = jnp.float32
BF16 = jnp.bfloat16
SMALL = pl.CostEstimate(flops=1, bytes_accessed=1, transcendentals=0)
MEDIUM = pl.CostEstimate(flops=1 * 10**8, bytes_accessed=1, transcendentals=0)
LARGE = pl.CostEstimate(flops=10**10, bytes_accessed=1, transcendentals=0)
VMEM = pl.BlockSpec(memory_space=pltpu.VMEM)


def dot(a, b, ca, cb):
    return lax.dot_general(a, b, (((ca,), (cb,)), ((), ())), preferred_element_type=F32)


def shifted(value, steps):
    count = lax.axis_size("seq")
    first, last = (max(0, -steps), min(count, count - steps))
    return lax.ppermute(value, "seq", [(i, i + steps) for i in range(first, last)])


def swapped(value, axis, bit):
    count = lax.axis_size(axis)
    return lax.ppermute(value, axis, [(i, i ^ bit) for i in range(count)])


def far_swapped(lower, upper):
    count = lax.axis_size("seq")
    side = lax.rem(lax.div(lax.axis_index("seq"), FAR), 2)
    rounds = []
    for r in range(2):
        pairs = [(i, i + FAR) for i in range(count - FAR) if (i // FAR) % 2 == r]
        if pairs:
            pairs = pairs + [(j, i) for i, j in pairs]
            rounds.append(lax.ppermute(lower() if lower is upper else jnp.where(side == r, lower(), upper()), "seq", pairs))
    if len(rounds) == 1:
        return rounds[0], rounds[0]
    return jnp.where(side == 1, rounds[0], rounds[1]), jnp.where(side == 0, rounds[0], rounds[1])


def group_rows(group, head, size):
    return pl.ds(pl.multiple_of(jnp.bitwise_xor(group, head) * size, size), size)


def own_order(ref, head):
    size = ref.shape[0] // 4
    return jnp.concatenate([ref[group_rows(g, head, size), :] for g in range(4)], 0)


def stacked(mat, kv_head):
    low = 2 * kv_head * HEAD_SIZE
    return jnp.concatenate([mat[:, low : low + HEAD_SIZE], mat[:, low + HEAD_SIZE : low + 2 * HEAD_SIZE]], 0)


def causal_mask(tok, head):
    key_pos = lax.broadcasted_iota(jnp.int32, (tok, 2 * tok), 0)
    lane = lax.broadcasted_iota(jnp.int32, (tok, 2 * tok), 1)
    query_pos = jnp.bitwise_xor(jnp.bitwise_and(lane, tok - 1), head * (tok // 4))
    return query_pos >= key_pos


def columns(kv_cols, kv_head):
    low = kv_head * HEAD_SIZE
    return slice(low, low + HEAD_SIZE), slice(kv_cols + low, kv_cols + low + HEAD_SIZE)


def window(kv_ref, r1_ref, r2_ref, x1_ref, p0_ref, x2_ref, odd, cols):
    return [kv_ref[:, cols], r1_ref[:, cols], r2_ref[:, cols], x1_ref[:, cols], jnp.where(odd, p0_ref[:, cols], x2_ref[:, cols])]


def join_kernel(k_ref, v_ref, kv_ref):
    cols = k_ref.shape[1]
    kv_ref[:, :cols] = k_ref[...]
    kv_ref[:, cols:] = v_ref[...]


def either_kernel(first, a_ref, b_ref, out_ref):
    out_ref[...] = jnp.where(first(lax.axis_index("seq")), a_ref[...], b_ref[...])


def is_odd(seq):
    return lax.rem(seq, 2) == 1


def is_lower(seq):
    return lax.rem(lax.div(seq, FAR), 2) == 0


def early_kernel(q_ref, kv_ref, r1_ref, r2_ref, x1_ref, e_ref, m_ref, part_ref):
    seq, head = lax.axis_index("seq"), lax.axis_index("head")
    tok = q_ref.shape[0]
    kv_cols = kv_ref.shape[1] // 2
    q_rel = own_order(q_ref, head)
    causal = causal_mask(tok, head)
    near = jnp.where(seq >= 2, 0.0, NEG).astype(F32)
    far = jnp.where(seq >= FAR, 0.0, NEG).astype(F32)
    biases = [None, near, far, near]
    scale = LOGIT_SCALE * LOG2E
    marks = []
    for g in range(kv_cols // HEAD_SIZE):
        kc, vc = columns(kv_cols, g)
        qg = stacked(q_rel, g)
        blocks = (kv_ref, r1_ref, r2_ref, x1_ref)
        scores = [dot(ref[:, kc], qg, 1, 1) for ref in blocks]
        scores[0] = jnp.where(causal, scores[0], NEG)
        scores[2] = jnp.where(causal, NEG, scores[2])
        tops = [jnp.max(sb, axis=0, keepdims=True) for sb in scores]
        tops = [t if b is None else t + b for t, b in zip(tops, biases)]
        top = jnp.maximum(jnp.maximum(tops[0], tops[1]), jnp.maximum(tops[2], tops[3])) * scale
        total = jnp.zeros_like(top)
        part = jnp.zeros((HEAD_SIZE, 2 * tok), F32)
        for b, bias in enumerate(biases):
            eb = jnp.exp2(scores[b] * scale - (top if bias is None else top - bias))
            e_ref[g, b] = eb
            total = total + jnp.sum(eb, axis=0, keepdims=True)
            part = part + dot(blocks[b][:, vc], eb.astype(BF16), 0, 0)
        part_ref[g] = part
        marks += [top, total]
    spare = jnp.zeros((m_ref.shape[0] - len(marks), 2 * tok), F32)
    m_ref[...] = jnp.concatenate(marks + [spare], 0)


def forward_kernel(q_ref, p0_ref, x2_ref, e_ref, m_ref, part_ref, dn_ref, df_ref,
                   o_ref, p_ref, stat_ref, second_ref):
    seq, head = lax.axis_index("seq"), lax.axis_index("head")
    odd = lax.rem(seq, 2) == 1
    tok = q_ref.shape[0]
    kv_cols = p0_ref.shape[1] // 2
    q_rel = own_order(q_ref, head)
    d_rel = jnp.concatenate([dn_ref[...], df_ref[...]], 0)
    bias = jnp.where(jnp.logical_or(odd, seq >= FAR), 0.0, NEG).astype(F32)
    scale = LOGIT_SCALE * LOG2E
    stats = []
    for g in range(kv_cols // HEAD_SIZE):
        kc, vc = columns(kv_cols, g)
        score = dot(jnp.where(odd, p0_ref[:, kc], x2_ref[:, kc]), stacked(q_rel, g), 1, 1)
        top_early = m_ref[2 * g : 2 * g + 1, :]
        top = jnp.maximum(top_early, (jnp.max(score, axis=0, keepdims=True) + bias) * scale)
        last = jnp.exp2(score * scale - (top - bias))
        shrink = jnp.exp2(top_early - top)
        total = m_ref[2 * g + 1 : 2 * g + 2, :] * shrink + jnp.sum(last, axis=0, keepdims=True)
        inv = 1.0 / total
        shrink = shrink * inv
        last = (last * inv).astype(BF16)
        p_ref[g, 4] = last
        out = part_ref[g] * shrink + dot(jnp.where(odd, p0_ref[:, vc], x2_ref[:, vc]), last, 0, 0)
        for b in range(4):
            p_ref[g, b] = (e_ref[g, b] * shrink).astype(BF16)
        out = out.astype(BF16)
        grad = stacked(d_rel, g)
        delta = jnp.sum(grad.astype(F32).T * out.astype(F32), axis=0, keepdims=True)
        stats += [top + jnp.log2(total), delta]
        out = out.astype(F32).T.astype(BF16)
        low = 2 * g * HEAD_SIZE
        o_ref[:, low : low + HEAD_SIZE] = out[:tok]
        o_ref[:, low + HEAD_SIZE : low + 2 * HEAD_SIZE] = out[tok:]
    spare = jnp.zeros((stat_ref.shape[0] - len(stats), 2 * tok), F32)
    stat_ref[...] = jnp.concatenate(stats + [spare], 0)
    half = d_rel.shape[1] // 2
    packed = jnp.concatenate([st[:, :tok] for st in stats] + [st[:, tok:] for st in stats], 0)
    packed = jnp.concatenate([packed, jnp.zeros((PACK - packed.shape[0], tok), F32)], 0)
    second_ref[:tok, :] = d_rel[:, half:]
    for part in range(3):
        rounded = packed.astype(BF16)
        second_ref[tok + part * PACK : tok + (part + 1) * PACK, :] = rounded
        packed = packed - rounded.astype(F32)


def project_kernel(o_ref, w_ref, *part_refs):
    size = part_refs[0].shape[0]
    cols = w_ref.shape[1]
    step = cols // 7 if cols % (7 * HEAD_SIZE) == 0 else cols
    for low in range(0, cols, step):
        part = dot(o_ref[...], w_ref[:, low : low + step], 1, 0).astype(BF16)
        for i, ref in enumerate(part_refs):
            ref[:, low : low + step] = part[i * size : (i + 1) * size]


def near_back_kernel(own_ref, core_ref, w_ref, d_ref):
    rows = jnp.concatenate([own_ref[...], core_ref[...]], 0)
    d_ref[...] = dot(rows, w_ref[...], 1, 1).astype(BF16)


def far_back_kernel(y_ref, yc_ref, w_ref, near_ref, d_ref, first_ref):
    rows = jnp.concatenate([y_ref[...], yc_ref[...]], 0)
    grad = dot(rows, w_ref[...], 1, 1).astype(BF16)
    d_ref[...] = grad
    cols = first_ref.shape[1]
    first_ref[...] = jnp.concatenate([near_ref[:, :cols], grad[:, :cols]], 0)


def across_kernel(q_ref, x1_ref, p_ref, stat_ref, dn_ref, df_ref, tx_ref):
    tok = q_ref.shape[0]
    kv_cols = x1_ref.shape[1] // 2
    q_rel = own_order(q_ref, lax.axis_index("head"))
    d_rel = jnp.concatenate([dn_ref[...], df_ref[...]], 0)
    for g in range(kv_cols // HEAD_SIZE):
        kc, vc = columns(kv_cols, g)
        qg, dg = stacked(q_rel, g), stacked(d_rel, g)
        pb = p_ref[g, 3]
        dp = dot(x1_ref[:, vc], dg, 1, 1)
        ds = (pb.astype(F32) * (dp - stat_ref[2 * g + 1 : 2 * g + 2, :])).astype(BF16)
        tx_ref[:, vc] = dot(pb, dg, 1, 0).astype(BF16)
        tx_ref[:, kc] = (dot(ds, qg, 1, 0) * LOGIT_SCALE).astype(BF16)


def backward_kernel(q_ref, kv_ref, r1_ref, r2_ref, x1_ref, p0_ref, x2_ref, p_ref, stat_ref, dn_ref, df_ref,
                    dq_ref, town_ref, t1_ref, tz_ref):
    seq, head = lax.axis_index("seq"), lax.axis_index("head")
    odd = lax.rem(seq, 2) == 1
    tok = q_ref.shape[0]
    kv_cols = kv_ref.shape[1] // 2
    size = tok // 4
    q_rel = own_order(q_ref, head)
    d_rel = jnp.concatenate([dn_ref[...], df_ref[...]], 0)
    outs = [town_ref, t1_ref, None, None, tz_ref]
    for g in range(kv_cols // HEAD_SIZE):
        kc, vc = columns(kv_cols, g)
        qg, dg = stacked(q_rel, g), stacked(d_rel, g)
        blocks = (kv_ref, r1_ref, r2_ref, x1_ref, p0_ref, x2_ref)
        key_blocks, value_blocks = window(*blocks, odd, kc), window(*blocks, odd, vc)
        delta = stat_ref[2 * g + 1 : 2 * g + 2, :]
        dq = jnp.zeros((HEAD_SIZE, 2 * tok), F32)
        for b in range(5):
            pb = p_ref[g, b]
            dp = dot(value_blocks[b], dg, 1, 1)
            ds = (pb.astype(F32) * (dp - delta)).astype(BF16)
            if outs[b] is not None:
                outs[b][:, vc] = dot(pb, dg, 1, 0).astype(outs[b].dtype)
                outs[b][:, kc] = (dot(ds, qg, 1, 0) * LOGIT_SCALE).astype(outs[b].dtype)
            dq = dq + dot(key_blocks[b], ds, 0, 0)
        dq = (dq * LOGIT_SCALE).T.astype(BF16)
        low = 2 * g * HEAD_SIZE
        for r in range(4):
            rows = group_rows(r, head, size)
            dq_ref[rows, low : low + HEAD_SIZE] = dq[r * size : (r + 1) * size]
            dq_ref[rows, low + HEAD_SIZE : low + 2 * HEAD_SIZE] = dq[tok + r * size : tok + (r + 1) * size]


def unpacked(second_ref, tok, kv_heads):
    parts = [second_ref[tok + i * PACK : tok + (i + 1) * PACK, :tok].astype(F32) for i in range(3)]
    packed = parts[0] + (parts[1] + parts[2])
    count = 2 * kv_heads
    return [jnp.concatenate([packed[i : i + 1], packed[count + i : count + i + 1]], 1) for i in range(count)]


def pair_kernel(t_ref, a_ref, b_ref, out_ref):
    tok, half = a_ref.shape
    odd = lax.rem(lax.axis_index("seq"), 2) == 1
    out_ref[:tok, :] = jnp.where(odd, t_ref[...], jnp.concatenate([a_ref[...], b_ref[:tok, :]], 1))
    out_ref[tok:, :half] = b_ref[tok:, :]
    out_ref[tok:, half:] = jnp.zeros((b_ref.shape[0] - tok, half), BF16)


def far_kernel(kv_ref, qf_ref, af_ref, bf_ref, qx_ref, px_ref, t_ref):
    seq, head = lax.axis_index("seq"), lax.axis_index("head")
    count = lax.axis_size("seq")
    tok = kv_ref.shape[0]
    kv_cols = kv_ref.shape[1] // 2
    kv_heads = kv_cols // HEAD_SIZE
    straight = jnp.logical_and(jnp.logical_not(causal_mask(tok, head)), seq + FAR < count)
    across = jnp.logical_and(lax.rem(seq, 2) == 1, seq + FAR - 1 < count)
    sources = [
        (own_order(qf_ref, head), jnp.concatenate([af_ref[...], bf_ref[:tok, :]], 1), unpacked(bf_ref, tok, kv_heads), straight),
        (own_order(qx_ref, head), px_ref[:tok, :], unpacked(px_ref, tok, kv_heads), across),
    ]
    scale = LOGIT_SCALE * LOG2E
    for g in range(kv_heads):
        kc, vc = columns(kv_cols, g)
        key, value = kv_ref[:, kc], kv_ref[:, vc]
        dk = jnp.zeros((tok, HEAD_SIZE), F32)
        dv = jnp.zeros((tok, HEAD_SIZE), F32)
        for q_rel, d_rel, stats, keep in sources:
            qg, dg = stacked(q_rel, g), stacked(d_rel, g)
            prob = jnp.exp2(dot(key, qg, 1, 1) * scale - stats[2 * g])
            prob = jnp.where(keep, prob, 0.0).astype(BF16)
            dp = dot(value, dg, 1, 1)
            ds = jnp.where(keep, prob.astype(F32) * (dp - stats[2 * g + 1]), 0.0).astype(BF16)
            dv = dv + dot(prob, dg, 1, 0)
            dk = dk + dot(ds, qg, 1, 0)
        t_ref[:, kc] = dk * LOGIT_SCALE
        t_ref[:, vc] = dv


def sum_kernel(*refs):
    total = refs[0][...].astype(F32)
    for ref in refs[1:-1]:
        total = total + ref[...].astype(F32)
    refs[-1][...] = total.astype(refs[-1].dtype)


def closing_kernel(own_ref, far_ref, hop_ref, pair_ref, near_ref, core_ref, y_ref, dk_ref, dv_ref, proj_ref):
    odd = lax.rem(lax.axis_index("seq"), 2) == 1
    proj_ref[...] = (near_ref[...].astype(F32) + core_ref[...].astype(F32) + y_ref[...].astype(F32)).astype(BF16)
    kept = jnp.where(odd, 0.0, pair_ref[: own_ref.shape[0], :].astype(F32))
    total = own_ref[...] + far_ref[...] + hop_ref[...].astype(F32) + kept
    kv_cols = dk_ref.shape[1]
    dk_ref[...] = total[:, :kv_cols].astype(BF16)
    dv_ref[...] = total[:, kv_cols:].astype(BF16)


def per_device(queries, keys, values, out_weight, out_grad):
    tok, q_cols = queries.shape
    kv_cols = keys.shape[1]
    kv_heads = kv_cols // HEAD_SIZE
    size = tok // 4
    rows = jax.ShapeDtypeStruct((size, out_weight.shape[1]), BF16)
    block = jax.ShapeDtypeStruct((tok, 2 * kv_cols), BF16)
    wide_block = jax.ShapeDtypeStruct((tok, 2 * kv_cols), F32)

    def call(kernel, name, outs, scratch, *operands, cost=SMALL):
        return pl.pallas_call(
            kernel,
            out_shape=outs,
            in_specs=[VMEM] * len(operands),
            out_specs=jax.tree.map(lambda _: VMEM, outs),
            scratch_shapes=scratch,
            compiler_params=pltpu.CompilerParams(vmem_limit_bytes=16 << 20),
            cost_estimate=cost,
            name=name,
        )(*operands)

    def gate(value, *others):
        return lax.optimization_barrier((value, *others))[0]

    kv = call(join_kernel, "join", block, [], keys, values)
    far_sent = call(functools.partial(either_kernel, is_lower), "far_sent", block, [], kv, queries)
    r1 = shifted(kv, 2)
    r2, q_far = far_swapped(lambda: kv, lambda: queries) if lax.axis_size("seq") > 2 * FAR else (far_swapped(*[lambda: far_sent] * 2))
    og_c = swapped(out_grad, "head", 1)
    og_y = swapped(out_grad, "head", 2)
    p0 = swapped(gate(kv, far_sent), "seq", 1)
    half_grad = jax.ShapeDtypeStruct((tok // 2, q_cols), BF16)
    grad_near = call(near_back_kernel, "near_back", half_grad, [], out_grad, og_c, out_weight, cost=LARGE)
    x1 = swapped(gate(r1, grad_near), "seq", 1)
    x2 = swapped(call(functools.partial(either_kernel, is_odd), "pick", block, [], r2, q_far, cost=LARGE), "seq", 1)
    og_yc = swapped(gate(og_y, r2, grad_near), "head", 1)
    first = jax.ShapeDtypeStruct((tok, q_cols // 2), BF16)
    second = jax.ShapeDtypeStruct((tok + 3 * PACK, q_cols // 2), BF16)
    grad_far, sent_first = call(far_back_kernel, "far_back", (half_grad, first), [], og_y, og_yc, out_weight, grad_near,
                                cost=SMALL)

    def down(value):
        return far_swapped(*[lambda: value] * 2)[1]

    far_first = down(sent_first)
    table = jax.ShapeDtypeStruct((8 * pl.cdiv(2 * kv_heads, 8), 2 * tok), F32)
    early = call(
        early_kernel,
        "attend_early",
        (
            jax.ShapeDtypeStruct((kv_heads, 4, tok, 2 * tok), F32),
            table,
            jax.ShapeDtypeStruct((kv_heads, HEAD_SIZE, 2 * tok), F32),
        ),
        [],
        queries, kv, gate(r1, p0), r2, x1,
        cost=SMALL,
    )
    attended, probs, stats, sent_second = call(
        forward_kernel,
        "attend",
        (
            jax.ShapeDtypeStruct((tok, q_cols), BF16),
            jax.ShapeDtypeStruct((kv_heads, 5, tok, 2 * tok), BF16),
            table,
            second,
        ),
        [],
        queries, p0, x2, *early, grad_near, grad_far,
    )
    t_x = call(across_kernel, "across_grad", block, [], queries, x1, probs, stats, grad_near, grad_far)
    d1 = swapped(t_x, "seq", 1)
    near_own, near_core, far_own, far_core = call(
        project_kernel, "project", (rows,) * 4, [], gate(attended, t_x), out_weight
    )
    sent = swapped(gate(far_core, far_first), "head", 1)
    far_sum = call(sum_kernel, "far_sum", rows, [], far_own, sent)
    from_y = swapped(far_sum, "head", 2)
    far_second = down(gate(sent_second, far_sum))

    query_gradient, t_own, t_1, t_z = call(
        backward_kernel,
        "attend_grad",
        (jax.ShapeDtypeStruct((tok, q_cols), BF16), wide_block, block, block),
        [],
        queries, kv, r1, r2, x1, p0, x2, probs, stats, grad_near, gate(grad_far, far_first),
        cost=LARGE,
    )
    e1 = shifted(call(sum_kernel, "hop_sum", block, [], t_1, d1), -2)
    pair = jax.ShapeDtypeStruct((second.shape[0], q_cols), BF16)
    pair = swapped(call(pair_kernel, "pair", pair, [], t_z, far_first, far_second), "seq", 1)
    from_core = swapped(gate(near_core, far_sum), "head", 1)
    t_far = call(far_kernel, "far_grad", wide_block, [],
                 kv, q_far, far_first, far_second, x2, pair, cost=MEDIUM)

    narrow = jax.ShapeDtypeStruct(keys.shape, BF16)
    key_gradient, value_gradient, projected = call(
        closing_kernel, "closing", (narrow, narrow, rows), [], t_own, t_far, e1, pair, near_own, from_core, from_y
    )
    return (projected, query_gradient, key_gradient, value_gradient)


def solution(mesh):
    return jax.shard_map(
        per_device,
        mesh=mesh,
        in_specs=(
            P("seq", "head"),
            P("seq", "head"),
            P("seq", "head"),
            P("head", None),
            P(("seq", "head"), None),
        ),
        out_specs=(P(("seq", "head"), None), P("seq", "head"), P("seq", "head"), P("seq", "head")),
        check_vma=False,
    )
```

```python
import functools

import jax
import jax.numpy as jnp
from jax import lax
from jax.experimental import pallas as pl
from jax.experimental.pallas import tpu as pltpu
from jax.sharding import PartitionSpec as P

HEAD_SIZE = 128
WIN = 1024
LOGIT_SCALE = 168.0 ** (-0.5)
LOG2E = 1.4426950408889634
NEG = -1e30
PACK = 16
FAR = 4
F32 = jnp.float32
BF16 = jnp.bfloat16
SMALL = pl.CostEstimate(flops=1, bytes_accessed=1, transcendentals=0)
MEDIUM = pl.CostEstimate(flops=1 * 10**8, bytes_accessed=1, transcendentals=0)
LARGE = pl.CostEstimate(flops=10**10, bytes_accessed=1, transcendentals=0)
VMEM = pl.BlockSpec(memory_space=pltpu.VMEM)


def dot(a, b, ca, cb):
    return lax.dot_general(a, b, (((ca,), (cb,)), ((), ())), preferred_element_type=F32)


def shifted(value, steps):
    count = lax.axis_size("seq")
    first, last = (max(0, -steps), min(count, count - steps))
    return lax.ppermute(value, "seq", [(i, i + steps) for i in range(first, last)])


def swapped(value, axis, bit):
    count = lax.axis_size(axis)
    return lax.ppermute(value, axis, [(i, i ^ bit) for i in range(count)])


def far_swapped(lower, upper):
    count = lax.axis_size("seq")
    side = lax.rem(lax.div(lax.axis_index("seq"), FAR), 2)
    rounds = []
    for r in range(2):
        pairs = [(i, i + FAR) for i in range(count - FAR) if (i // FAR) % 2 == r]
        if pairs:
            pairs = pairs + [(j, i) for i, j in pairs]
            rounds.append(lax.ppermute(lower() if lower is upper else jnp.where(side == r, lower(), upper()), "seq", pairs))
    if len(rounds) == 1:
        return rounds[0], rounds[0]
    return jnp.where(side == 1, rounds[0], rounds[1]), jnp.where(side == 0, rounds[0], rounds[1])


def group_rows(group, head, size):
    return pl.ds(pl.multiple_of(jnp.bitwise_xor(group, head) * size, size), size)


def own_order(ref, head):
    size = ref.shape[0] // 4
    return jnp.concatenate([ref[group_rows(g, head, size), :] for g in range(4)], 0)


def stacked(mat, kv_head):
    low = 2 * kv_head * HEAD_SIZE
    return jnp.concatenate([mat[:, low : low + HEAD_SIZE], mat[:, low + HEAD_SIZE : low + 2 * HEAD_SIZE]], 0)


def causal_mask(tok, head):
    key_pos = lax.broadcasted_iota(jnp.int32, (tok, 2 * tok), 0)
    lane = lax.broadcasted_iota(jnp.int32, (tok, 2 * tok), 1)
    query_pos = jnp.bitwise_xor(jnp.bitwise_and(lane, tok - 1), head * (tok // 4))
    return query_pos >= key_pos


def columns(kv_cols, kv_head):
    low = kv_head * HEAD_SIZE
    return slice(low, low + HEAD_SIZE), slice(kv_cols + low, kv_cols + low + HEAD_SIZE)


def window(kv_ref, r1_ref, r2_ref, x1_ref, p0_ref, x2_ref, odd, cols):
    return [kv_ref[:, cols], r1_ref[:, cols], r2_ref[:, cols], x1_ref[:, cols], jnp.where(odd, p0_ref[:, cols], x2_ref[:, cols])]


def join_kernel(k_ref, v_ref, kv_ref):
    cols = k_ref.shape[1]
    kv_ref[:, :cols] = k_ref[...]
    kv_ref[:, cols:] = v_ref[...]


def either_kernel(first, a_ref, b_ref, out_ref):
    out_ref[...] = jnp.where(first(lax.axis_index("seq")), a_ref[...], b_ref[...])


def is_odd(seq):
    return lax.rem(seq, 2) == 1


def is_lower(seq):
    return lax.rem(lax.div(seq, FAR), 2) == 0


def early_kernel(q_ref, kv_ref, r1_ref, r2_ref, x1_ref, e_ref, m_ref, part_ref):
    seq, head = lax.axis_index("seq"), lax.axis_index("head")
    tok = q_ref.shape[0]
    kv_cols = kv_ref.shape[1] // 2
    q_rel = own_order(q_ref, head)
    causal = causal_mask(tok, head)
    near = jnp.where(seq >= 2, 0.0, NEG).astype(F32)
    far = jnp.where(seq >= FAR, 0.0, NEG).astype(F32)
    biases = [None, near, far, near]
    scale = LOGIT_SCALE * LOG2E
    marks = []
    for g in range(kv_cols // HEAD_SIZE):
        kc, vc = columns(kv_cols, g)
        qg = stacked(q_rel, g)
        blocks = (kv_ref, r1_ref, r2_ref, x1_ref)
        scores = [dot(ref[:, kc], qg, 1, 1) for ref in blocks]
        scores[0] = jnp.where(causal, scores[0], NEG)
        scores[2] = jnp.where(causal, NEG, scores[2])
        tops = [jnp.max(sb, axis=0, keepdims=True) for sb in scores]
        tops = [t if b is None else t + b for t, b in zip(tops, biases)]
        top = jnp.maximum(jnp.maximum(tops[0], tops[1]), jnp.maximum(tops[2], tops[3])) * scale
        total = jnp.zeros_like(top)
        part = jnp.zeros((HEAD_SIZE, 2 * tok), F32)
        for b, bias in enumerate(biases):
            eb = jnp.exp2(scores[b] * scale - (top if bias is None else top - bias))
            e_ref[g, b] = eb
            total = total + jnp.sum(eb, axis=0, keepdims=True)
            part = part + dot(blocks[b][:, vc], eb.astype(BF16), 0, 0)
        part_ref[g] = part
        marks += [top, total]
    spare = jnp.zeros((m_ref.shape[0] - len(marks), 2 * tok), F32)
    m_ref[...] = jnp.concatenate(marks + [spare], 0)


def forward_kernel(q_ref, p0_ref, x2_ref, e_ref, m_ref, part_ref, dn_ref, df_ref,
                   o_ref, p_ref, stat_ref, second_ref):
    seq, head = lax.axis_index("seq"), lax.axis_index("head")
    odd = lax.rem(seq, 2) == 1
    tok = q_ref.shape[0]
    kv_cols = p0_ref.shape[1] // 2
    q_rel = own_order(q_ref, head)
    d_rel = jnp.concatenate([dn_ref[...], df_ref[...]], 0)
    bias = jnp.where(jnp.logical_or(odd, seq >= FAR), 0.0, NEG).astype(F32)
    scale = LOGIT_SCALE * LOG2E
    stats = []
    for g in range(kv_cols // HEAD_SIZE):
        kc, vc = columns(kv_cols, g)
        score = dot(jnp.where(odd, p0_ref[:, kc], x2_ref[:, kc]), stacked(q_rel, g), 1, 1)
        top_early = m_ref[2 * g : 2 * g + 1, :]
        top = jnp.maximum(top_early, (jnp.max(score, axis=0, keepdims=True) + bias) * scale)
        last = jnp.exp2(score * scale - (top - bias))
        shrink = jnp.exp2(top_early - top)
        total = m_ref[2 * g + 1 : 2 * g + 2, :] * shrink + jnp.sum(last, axis=0, keepdims=True)
        inv = 1.0 / total
        shrink = shrink * inv
        last = (last * inv).astype(BF16)
        p_ref[g, 4] = last
        out = part_ref[g] * shrink + dot(jnp.where(odd, p0_ref[:, vc], x2_ref[:, vc]), last, 0, 0)
        for b in range(4):
            p_ref[g, b] = (e_ref[g, b] * shrink).astype(BF16)
        out = out.astype(BF16)
        grad = stacked(d_rel, g)
        delta = jnp.sum(grad.astype(F32).T * out.astype(F32), axis=0, keepdims=True)
        stats += [top + jnp.log2(total), delta]
        out = out.astype(F32).T.astype(BF16)
        low = 2 * g * HEAD_SIZE
        o_ref[:, low : low + HEAD_SIZE] = out[:tok]
        o_ref[:, low + HEAD_SIZE : low + 2 * HEAD_SIZE] = out[tok:]
    spare = jnp.zeros((stat_ref.shape[0] - len(stats), 2 * tok), F32)
    stat_ref[...] = jnp.concatenate(stats + [spare], 0)
    half = d_rel.shape[1] // 2
    packed = jnp.concatenate([st[:, :tok] for st in stats] + [st[:, tok:] for st in stats], 0)
    packed = jnp.concatenate([packed, jnp.zeros((PACK - packed.shape[0], tok), F32)], 0)
    second_ref[:tok, :] = d_rel[:, half:]
    for part in range(3):
        rounded = packed.astype(BF16)
        second_ref[tok + part * PACK : tok + (part + 1) * PACK, :] = rounded
        packed = packed - rounded.astype(F32)


def project_kernel(o_ref, w_ref, *part_refs):
    size = part_refs[0].shape[0]
    cols = w_ref.shape[1]
    step = cols // 7 if cols % (7 * HEAD_SIZE) == 0 else cols
    for low in range(0, cols, step):
        part = dot(o_ref[...], w_ref[:, low : low + step], 1, 0).astype(BF16)
        for i, ref in enumerate(part_refs):
            ref[:, low : low + step] = part[i * size : (i + 1) * size]


def near_back_kernel(own_ref, core_ref, w_ref, d_ref):
    rows = jnp.concatenate([own_ref[...], core_ref[...]], 0)
    d_ref[...] = dot(rows, w_ref[...], 1, 1).astype(BF16)


def far_back_kernel(y_ref, yc_ref, w_ref, near_ref, d_ref, first_ref):
    rows = jnp.concatenate([y_ref[...], yc_ref[...]], 0)
    grad = dot(rows, w_ref[...], 1, 1).astype(BF16)
    d_ref[...] = grad
    cols = first_ref.shape[1]
    first_ref[...] = jnp.concatenate([near_ref[:, :cols], grad[:, :cols]], 0)


def across_kernel(q_ref, x1_ref, p_ref, stat_ref, dn_ref, df_ref, tx_ref):
    tok = q_ref.shape[0]
    kv_cols = x1_ref.shape[1] // 2
    q_rel = own_order(q_ref, lax.axis_index("head"))
    d_rel = jnp.concatenate([dn_ref[...], df_ref[...]], 0)
    for g in range(kv_cols // HEAD_SIZE):
        kc, vc = columns(kv_cols, g)
        qg, dg = stacked(q_rel, g), stacked(d_rel, g)
        pb = p_ref[g, 3]
        dp = dot(x1_ref[:, vc], dg, 1, 1)
        ds = (pb.astype(F32) * (dp - stat_ref[2 * g + 1 : 2 * g + 2, :])).astype(BF16)
        tx_ref[:, vc] = dot(pb, dg, 1, 0).astype(BF16)
        tx_ref[:, kc] = (dot(ds, qg, 1, 0) * LOGIT_SCALE).astype(BF16)


def backward_kernel(q_ref, kv_ref, r1_ref, r2_ref, x1_ref, p0_ref, x2_ref, p_ref, stat_ref, dn_ref, df_ref,
                    dq_ref, town_ref, t1_ref, tz_ref):
    seq, head = lax.axis_index("seq"), lax.axis_index("head")
    odd = lax.rem(seq, 2) == 1
    tok = q_ref.shape[0]
    kv_cols = kv_ref.shape[1] // 2
    size = tok // 4
    q_rel = own_order(q_ref, head)
    d_rel = jnp.concatenate([dn_ref[...], df_ref[...]], 0)
    outs = [town_ref, t1_ref, None, None, tz_ref]
    for g in range(kv_cols // HEAD_SIZE):
        kc, vc = columns(kv_cols, g)
        qg, dg = stacked(q_rel, g), stacked(d_rel, g)
        blocks = (kv_ref, r1_ref, r2_ref, x1_ref, p0_ref, x2_ref)
        key_blocks, value_blocks = window(*blocks, odd, kc), window(*blocks, odd, vc)
        delta = stat_ref[2 * g + 1 : 2 * g + 2, :]
        dq = jnp.zeros((HEAD_SIZE, 2 * tok), F32)
        for b in range(5):
            pb = p_ref[g, b]
            dp = dot(value_blocks[b], dg, 1, 1)
            ds = (pb.astype(F32) * (dp - delta)).astype(BF16)
            if outs[b] is not None:
                outs[b][:, vc] = dot(pb, dg, 1, 0).astype(outs[b].dtype)
                outs[b][:, kc] = (dot(ds, qg, 1, 0) * LOGIT_SCALE).astype(outs[b].dtype)
            dq = dq + dot(key_blocks[b], ds, 0, 0)
        dq = (dq * LOGIT_SCALE).T.astype(BF16)
        low = 2 * g * HEAD_SIZE
        for r in range(4):
            rows = group_rows(r, head, size)
            dq_ref[rows, low : low + HEAD_SIZE] = dq[r * size : (r + 1) * size]
            dq_ref[rows, low + HEAD_SIZE : low + 2 * HEAD_SIZE] = dq[tok + r * size : tok + (r + 1) * size]


def unpacked(second_ref, tok, kv_heads):
    parts = [second_ref[tok + i * PACK : tok + (i + 1) * PACK, :tok].astype(F32) for i in range(3)]
    packed = parts[0] + (parts[1] + parts[2])
    count = 2 * kv_heads
    return [jnp.concatenate([packed[i : i + 1], packed[count + i : count + i + 1]], 1) for i in range(count)]


def pair_kernel(t_ref, a_ref, b_ref, out_ref):
    tok, half = a_ref.shape
    odd = lax.rem(lax.axis_index("seq"), 2) == 1
    out_ref[:tok, :] = jnp.where(odd, t_ref[...], jnp.concatenate([a_ref[...], b_ref[:tok, :]], 1))
    out_ref[tok:, :half] = b_ref[tok:, :]
    out_ref[tok:, half:] = jnp.zeros((b_ref.shape[0] - tok, half), BF16)


def far_kernel(kv_ref, qf_ref, af_ref, bf_ref, qx_ref, px_ref, t_ref):
    seq, head = lax.axis_index("seq"), lax.axis_index("head")
    count = lax.axis_size("seq")
    tok = kv_ref.shape[0]
    kv_cols = kv_ref.shape[1] // 2
    kv_heads = kv_cols // HEAD_SIZE
    straight = jnp.logical_and(jnp.logical_not(causal_mask(tok, head)), seq + FAR < count)
    across = jnp.logical_and(lax.rem(seq, 2) == 1, seq + FAR - 1 < count)
    sources = [
        (own_order(qf_ref, head), jnp.concatenate([af_ref[...], bf_ref[:tok, :]], 1), unpacked(bf_ref, tok, kv_heads), straight),
        (own_order(qx_ref, head), px_ref[:tok, :], unpacked(px_ref, tok, kv_heads), across),
    ]
    scale = LOGIT_SCALE * LOG2E
    for g in range(kv_heads):
        kc, vc = columns(kv_cols, g)
        key, value = kv_ref[:, kc], kv_ref[:, vc]
        dk = jnp.zeros((tok, HEAD_SIZE), F32)
        dv = jnp.zeros((tok, HEAD_SIZE), F32)
        for q_rel, d_rel, stats, keep in sources:
            qg, dg = stacked(q_rel, g), stacked(d_rel, g)
            prob = jnp.exp2(dot(key, qg, 1, 1) * scale - stats[2 * g])
            prob = jnp.where(keep, prob, 0.0).astype(BF16)
            dp = dot(value, dg, 1, 1)
            ds = jnp.where(keep, prob.astype(F32) * (dp - stats[2 * g + 1]), 0.0).astype(BF16)
            dv = dv + dot(prob, dg, 1, 0)
            dk = dk + dot(ds, qg, 1, 0)
        t_ref[:, kc] = dk * LOGIT_SCALE
        t_ref[:, vc] = dv


def sum_kernel(*refs):
    total = refs[0][...].astype(F32)
    for ref in refs[1:-1]:
        total = total + ref[...].astype(F32)
    refs[-1][...] = total.astype(refs[-1].dtype)


def closing_kernel(own_ref, far_ref, hop_ref, pair_ref, near_ref, core_ref, y_ref, dk_ref, dv_ref, proj_ref):
    odd = lax.rem(lax.axis_index("seq"), 2) == 1
    proj_ref[...] = (near_ref[...].astype(F32) + core_ref[...].astype(F32) + y_ref[...].astype(F32)).astype(BF16)
    kept = jnp.where(odd, 0.0, pair_ref[: own_ref.shape[0], :].astype(F32))
    total = own_ref[...] + far_ref[...] + hop_ref[...].astype(F32) + kept
    kv_cols = dk_ref.shape[1]
    dk_ref[...] = total[:, :kv_cols].astype(BF16)
    dv_ref[...] = total[:, kv_cols:].astype(BF16)


def per_device(queries, keys, values, out_weight, out_grad):
    tok, q_cols = queries.shape
    kv_cols = keys.shape[1]
    kv_heads = kv_cols // HEAD_SIZE
    size = tok // 4
    rows = jax.ShapeDtypeStruct((size, out_weight.shape[1]), BF16)
    block = jax.ShapeDtypeStruct((tok, 2 * kv_cols), BF16)
    wide_block = jax.ShapeDtypeStruct((tok, 2 * kv_cols), F32)

    def call(kernel, name, outs, scratch, *operands, cost=SMALL):
        return pl.pallas_call(
            kernel,
            out_shape=outs,
            in_specs=[VMEM] * len(operands),
            out_specs=jax.tree.map(lambda _: VMEM, outs),
            scratch_shapes=scratch,
            compiler_params=pltpu.CompilerParams(vmem_limit_bytes=16 << 20),
            cost_estimate=cost,
            name=name,
        )(*operands)

    def gate(value, *others):
        return lax.optimization_barrier((value, *others))[0]

    kv = call(join_kernel, "join", block, [], keys, values)
    far_sent = call(functools.partial(either_kernel, is_lower), "far_sent", block, [], kv, queries)
    r1 = shifted(kv, 2)
    r2, q_far = far_swapped(lambda: kv, lambda: queries) if lax.axis_size("seq") > 2 * FAR else (far_swapped(*[lambda: far_sent] * 2))
    og_c = swapped(out_grad, "head", 1)
    og_y = swapped(out_grad, "head", 2)
    p0 = swapped(gate(kv, far_sent), "seq", 1)
    half_grad = jax.ShapeDtypeStruct((tok // 2, q_cols), BF16)
    grad_near = call(near_back_kernel, "near_back", half_grad, [], out_grad, og_c, out_weight, cost=LARGE)
    x1 = swapped(gate(r1, grad_near), "seq", 1)
    x2 = swapped(call(functools.partial(either_kernel, is_odd), "pick", block, [], r2, q_far, cost=LARGE), "seq", 1)
    og_yc = swapped(gate(og_y, r2, grad_near), "head", 1)
    first = jax.ShapeDtypeStruct((tok, q_cols // 2), BF16)
    second = jax.ShapeDtypeStruct((tok + 3 * PACK, q_cols // 2), BF16)
    grad_far, sent_first = call(far_back_kernel, "far_back", (half_grad, first), [], og_y, og_yc, out_weight, grad_near,
                                cost=SMALL)

    def down(value):
        return far_swapped(*[lambda: value] * 2)[1]

    far_first = down(sent_first)
    table = jax.ShapeDtypeStruct((8 * pl.cdiv(2 * kv_heads, 8), 2 * tok), F32)
    early = call(
        early_kernel,
        "attend_early",
        (
            jax.ShapeDtypeStruct((kv_heads, 4, tok, 2 * tok), F32),
            table,
            jax.ShapeDtypeStruct((kv_heads, HEAD_SIZE, 2 * tok), F32),
        ),
        [],
        queries, kv, gate(r1, p0), r2, x1,
        cost=SMALL,
    )
    attended, probs, stats, sent_second = call(
        forward_kernel,
        "attend",
        (
            jax.ShapeDtypeStruct((tok, q_cols), BF16),
            jax.ShapeDtypeStruct((kv_heads, 5, tok, 2 * tok), BF16),
            table,
            second,
        ),
        [],
        queries, p0, x2, *early, grad_near, grad_far,
    )
    far_second = down(sent_second)
    near_own, near_core, far_own, far_core = call(
        project_kernel, "project", (rows,) * 4, [], attended, out_weight
    )
    sent = swapped(gate(far_core, far_first), "head", 1)
    t_x = call(across_kernel, "across_grad", block, [], queries, x1, probs, stats, grad_near, gate(grad_far, far_core))
    d1 = swapped(t_x, "seq", 1)
    far_sum = call(sum_kernel, "far_sum", rows, [], far_own, sent)
    from_y = swapped(far_sum, "head", 2)

    query_gradient, t_own, t_1, t_z = call(
        backward_kernel,
        "attend_grad",
        (jax.ShapeDtypeStruct((tok, q_cols), BF16), wide_block, block, block),
        [],
        queries, kv, r1, r2, x1, p0, x2, probs, stats, grad_near, gate(grad_far, far_first),
        cost=LARGE,
    )
    e1 = shifted(call(sum_kernel, "hop_sum", block, [], t_1, d1), -2)
    pair = jax.ShapeDtypeStruct((second.shape[0], q_cols), BF16)
    pair = swapped(call(pair_kernel, "pair", pair, [], t_z, far_first, far_second), "seq", 1)
    from_core = swapped(gate(near_core, far_sum), "head", 1)
    t_far = call(far_kernel, "far_grad", wide_block, [],
                 kv, q_far, far_first, far_second, x2, pair, cost=MEDIUM)

    narrow = jax.ShapeDtypeStruct(keys.shape, BF16)
    key_gradient, value_gradient, projected = call(
        closing_kernel, "closing", (narrow, narrow, rows), [], t_own, t_far, e1, pair, near_own, from_core, from_y
    )
    return (projected, query_gradient, key_gradient, value_gradient)


def solution(mesh):
    return jax.shard_map(
        per_device,
        mesh=mesh,
        in_specs=(
            P("seq", "head"),
            P("seq", "head"),
            P("seq", "head"),
            P("head", None),
            P(("seq", "head"), None),
        ),
        out_specs=(P(("seq", "head"), None), P("seq", "head"), P("seq", "head"), P("seq", "head")),
        check_vma=False,
    )
```

```python
import functools

import jax
import jax.numpy as jnp
from jax import lax
from jax.experimental import pallas as pl
from jax.experimental.pallas import tpu as pltpu
from jax.sharding import PartitionSpec as P

HEAD_SIZE = 128
WIN = 1024
LOGIT_SCALE = 168.0 ** (-0.5)
LOG2E = 1.4426950408889634
NEG = -1e30
PACK = 8
FAR = 4
F32 = jnp.float32
BF16 = jnp.bfloat16
SMALL = pl.CostEstimate(flops=1, bytes_accessed=1, transcendentals=0)
MEDIUM = pl.CostEstimate(flops=1 * 10**8, bytes_accessed=1, transcendentals=0)
LARGE = pl.CostEstimate(flops=10**10, bytes_accessed=1, transcendentals=0)
VMEM = pl.BlockSpec(memory_space=pltpu.VMEM)


def dot(a, b, ca, cb):
    return lax.dot_general(a, b, (((ca,), (cb,)), ((), ())), preferred_element_type=F32)


def shifted(value, steps):
    count = lax.axis_size("seq")
    first, last = (max(0, -steps), min(count, count - steps))
    return lax.ppermute(value, "seq", [(i, i + steps) for i in range(first, last)])


def swapped(value, axis, bit):
    count = lax.axis_size(axis)
    return lax.ppermute(value, axis, [(i, i ^ bit) for i in range(count)])


def far_swapped(lower, upper):
    count = lax.axis_size("seq")
    side = lax.rem(lax.div(lax.axis_index("seq"), FAR), 2)
    rounds = []
    for r in range(2):
        pairs = [(i, i + FAR) for i in range(count - FAR) if (i // FAR) % 2 == r]
        if pairs:
            pairs = pairs + [(j, i) for i, j in pairs]
            rounds.append(lax.ppermute(lower() if lower is upper else jnp.where(side == r, lower(), upper()), "seq", pairs))
    if len(rounds) == 1:
        return rounds[0], rounds[0]
    return jnp.where(side == 1, rounds[0], rounds[1]), jnp.where(side == 0, rounds[0], rounds[1])


def group_rows(group, head, size):
    return pl.ds(pl.multiple_of(jnp.bitwise_xor(group, head) * size, size), size)


def own_order(ref, head):
    size = ref.shape[0] // 4
    return jnp.concatenate([ref[group_rows(g, head, size), :] for g in range(4)], 0)


def stacked(mat, kv_head):
    low = 2 * kv_head * HEAD_SIZE
    return jnp.concatenate([mat[:, low : low + HEAD_SIZE], mat[:, low + HEAD_SIZE : low + 2 * HEAD_SIZE]], 0)


def causal_mask(tok, head):
    key_pos = lax.broadcasted_iota(jnp.int32, (tok, 2 * tok), 0)
    lane = lax.broadcasted_iota(jnp.int32, (tok, 2 * tok), 1)
    query_pos = jnp.bitwise_xor(jnp.bitwise_and(lane, tok - 1), head * (tok // 4))
    return query_pos >= key_pos


def columns(kv_cols, kv_head):
    low = kv_head * HEAD_SIZE
    return slice(low, low + HEAD_SIZE), slice(kv_cols + low, kv_cols + low + HEAD_SIZE)


def window(kv_ref, r1_ref, r2_ref, x1_ref, p0_ref, x2_ref, odd, cols):
    return [kv_ref[:, cols], r1_ref[:, cols], r2_ref[:, cols], x1_ref[:, cols], jnp.where(odd, p0_ref[:, cols], x2_ref[:, cols])]


def join_kernel(k_ref, v_ref, kv_ref):
    cols = k_ref.shape[1]
    kv_ref[:, :cols] = k_ref[...]
    kv_ref[:, cols:] = v_ref[...]


def either_kernel(first, a_ref, b_ref, out_ref):
    out_ref[...] = jnp.where(first(lax.axis_index("seq")), a_ref[...], b_ref[...])


def is_odd(seq):
    return lax.rem(seq, 2) == 1


def is_lower(seq):
    return lax.rem(lax.div(seq, FAR), 2) == 0


def early_kernel(q_ref, kv_ref, r1_ref, r2_ref, x1_ref, e_ref, m_ref, part_ref):
    seq, head = lax.axis_index("seq"), lax.axis_index("head")
    tok = q_ref.shape[0]
    kv_cols = kv_ref.shape[1] // 2
    q_rel = own_order(q_ref, head)
    causal = causal_mask(tok, head)
    near = jnp.where(seq >= 2, 0.0, NEG).astype(F32)
    far = jnp.where(seq >= FAR, 0.0, NEG).astype(F32)
    biases = [None, near, far, near]
    scale = LOGIT_SCALE * LOG2E
    marks = []
    for g in range(kv_cols // HEAD_SIZE):
        kc, vc = columns(kv_cols, g)
        qg = stacked(q_rel, g)
        blocks = (kv_ref, r1_ref, r2_ref, x1_ref)
        scores = [dot(ref[:, kc], qg, 1, 1) for ref in blocks]
        scores[0] = jnp.where(causal, scores[0], NEG)
        scores[2] = jnp.where(causal, NEG, scores[2])
        tops = [jnp.max(sb, axis=0, keepdims=True) for sb in scores]
        tops = [t if b is None else t + b for t, b in zip(tops, biases)]
        top = jnp.maximum(jnp.maximum(tops[0], tops[1]), jnp.maximum(tops[2], tops[3])) * scale
        total = jnp.zeros_like(top)
        part = jnp.zeros((HEAD_SIZE, 2 * tok), F32)
        for b, bias in enumerate(biases):
            eb = jnp.exp2(scores[b] * scale - (top if bias is None else top - bias))
            e_ref[g, b] = eb
            total = total + jnp.sum(eb, axis=0, keepdims=True)
            part = part + dot(blocks[b][:, vc], eb.astype(BF16), 0, 0)
        part_ref[g] = part
        marks += [top, total]
    spare = jnp.zeros((m_ref.shape[0] - len(marks), 2 * tok), F32)
    m_ref[...] = jnp.concatenate(marks + [spare], 0)


def forward_kernel(q_ref, p0_ref, x2_ref, e_ref, m_ref, part_ref, dn_ref, df_ref,
                   o_ref, p_ref, stat_ref, second_ref):
    seq, head = lax.axis_index("seq"), lax.axis_index("head")
    odd = lax.rem(seq, 2) == 1
    tok = q_ref.shape[0]
    kv_cols = p0_ref.shape[1] // 2
    q_rel = own_order(q_ref, head)
    d_rel = jnp.concatenate([dn_ref[...], df_ref[...]], 0)
    bias = jnp.where(jnp.logical_or(odd, seq >= FAR), 0.0, NEG).astype(F32)
    scale = LOGIT_SCALE * LOG2E
    stats = []
    for g in range(kv_cols // HEAD_SIZE):
        kc, vc = columns(kv_cols, g)
        score = dot(jnp.where(odd, p0_ref[:, kc], x2_ref[:, kc]), stacked(q_rel, g), 1, 1)
        top_early = m_ref[2 * g : 2 * g + 1, :]
        top = jnp.maximum(top_early, (jnp.max(score, axis=0, keepdims=True) + bias) * scale)
        last = jnp.exp2(score * scale - (top - bias))
        shrink = jnp.exp2(top_early - top)
        total = m_ref[2 * g + 1 : 2 * g + 2, :] * shrink + jnp.sum(last, axis=0, keepdims=True)
        inv = 1.0 / total
        shrink = shrink * inv
        last = (last * inv).astype(BF16)
        p_ref[g, 4] = last
        out = part_ref[g] * shrink + dot(jnp.where(odd, p0_ref[:, vc], x2_ref[:, vc]), last, 0, 0)
        for b in range(4):
            p_ref[g, b] = (e_ref[g, b] * shrink).astype(BF16)
        out = out.astype(BF16)
        grad = stacked(d_rel, g)
        delta = jnp.sum(grad.astype(F32).T * out.astype(F32), axis=0, keepdims=True)
        stats += [top + jnp.log2(total), delta]
        out = out.astype(F32).T.astype(BF16)
        low = 2 * g * HEAD_SIZE
        o_ref[:, low : low + HEAD_SIZE] = out[:tok]
        o_ref[:, low + HEAD_SIZE : low + 2 * HEAD_SIZE] = out[tok:]
    spare = jnp.zeros((stat_ref.shape[0] - len(stats), 2 * tok), F32)
    stat_ref[...] = jnp.concatenate(stats + [spare], 0)
    half = d_rel.shape[1] // 2
    packed = jnp.concatenate([st[:, :tok] for st in stats] + [st[:, tok:] for st in stats], 0)
    second_ref[:tok, :] = d_rel[:, half:]
    for part in range(3):
        rounded = packed.astype(BF16)
        second_ref[tok + part * PACK : tok + (part + 1) * PACK, :] = rounded
        packed = packed - rounded.astype(F32)


def project_kernel(o_ref, w_ref, *part_refs):
    size = part_refs[0].shape[0]
    cols = w_ref.shape[1]
    step = cols // 7 if cols % (7 * HEAD_SIZE) == 0 else cols
    for low in range(0, cols, step):
        part = dot(o_ref[...], w_ref[:, low : low + step], 1, 0).astype(BF16)
        for i, ref in enumerate(part_refs):
            ref[:, low : low + step] = part[i * size : (i + 1) * size]


def near_back_kernel(own_ref, core_ref, w_ref, d_ref):
    rows = jnp.concatenate([own_ref[...], core_ref[...]], 0)
    d_ref[...] = dot(rows, w_ref[...], 1, 1).astype(BF16)


def far_back_kernel(y_ref, yc_ref, w_ref, near_ref, d_ref, first_ref):
    rows = jnp.concatenate([y_ref[...], yc_ref[...]], 0)
    grad = dot(rows, w_ref[...], 1, 1).astype(BF16)
    d_ref[...] = grad
    cols = first_ref.shape[1]
    first_ref[...] = jnp.concatenate([near_ref[:, :cols], grad[:, :cols]], 0)


def across_kernel(q_ref, x1_ref, p_ref, stat_ref, dn_ref, df_ref, tx_ref):
    tok = q_ref.shape[0]
    kv_cols = x1_ref.shape[1] // 2
    q_rel = own_order(q_ref, lax.axis_index("head"))
    d_rel = jnp.concatenate([dn_ref[...], df_ref[...]], 0)
    for g in range(kv_cols // HEAD_SIZE):
        kc, vc = columns(kv_cols, g)
        qg, dg = stacked(q_rel, g), stacked(d_rel, g)
        pb = p_ref[g, 3]
        dp = dot(x1_ref[:, vc], dg, 1, 1)
        ds = (pb.astype(F32) * (dp - stat_ref[2 * g + 1 : 2 * g + 2, :])).astype(BF16)
        tx_ref[:, vc] = dot(pb, dg, 1, 0).astype(BF16)
        tx_ref[:, kc] = (dot(ds, qg, 1, 0) * LOGIT_SCALE).astype(BF16)


def backward_kernel(q_ref, kv_ref, r1_ref, r2_ref, x1_ref, p0_ref, x2_ref, p_ref, stat_ref, dn_ref, df_ref,
                    dq_ref, town_ref, t1_ref, tz_ref):
    seq, head = lax.axis_index("seq"), lax.axis_index("head")
    odd = lax.rem(seq, 2) == 1
    tok = q_ref.shape[0]
    kv_cols = kv_ref.shape[1] // 2
    size = tok // 4
    q_rel = own_order(q_ref, head)
    d_rel = jnp.concatenate([dn_ref[...], df_ref[...]], 0)
    outs = [town_ref, t1_ref, None, None, tz_ref]
    for g in range(kv_cols // HEAD_SIZE):
        kc, vc = columns(kv_cols, g)
        qg, dg = stacked(q_rel, g), stacked(d_rel, g)
        blocks = (kv_ref, r1_ref, r2_ref, x1_ref, p0_ref, x2_ref)
        key_blocks, value_blocks = window(*blocks, odd, kc), window(*blocks, odd, vc)
        delta = stat_ref[2 * g + 1 : 2 * g + 2, :]
        dq = jnp.zeros((HEAD_SIZE, 2 * tok), F32)
        for b in range(5):
            pb = p_ref[g, b]
            dp = dot(value_blocks[b], dg, 1, 1)
            ds = (pb.astype(F32) * (dp - delta)).astype(BF16)
            if outs[b] is not None:
                outs[b][:, vc] = dot(pb, dg, 1, 0).astype(outs[b].dtype)
                outs[b][:, kc] = (dot(ds, qg, 1, 0) * LOGIT_SCALE).astype(outs[b].dtype)
            dq = dq + dot(key_blocks[b], ds, 0, 0)
        dq = (dq * LOGIT_SCALE).T.astype(BF16)
        low = 2 * g * HEAD_SIZE
        for r in range(4):
            rows = group_rows(r, head, size)
            dq_ref[rows, low : low + HEAD_SIZE] = dq[r * size : (r + 1) * size]
            dq_ref[rows, low + HEAD_SIZE : low + 2 * HEAD_SIZE] = dq[tok + r * size : tok + (r + 1) * size]


def unpacked(second_ref, tok, kv_heads):
    parts = [second_ref[tok + i * PACK : tok + (i + 1) * PACK, :tok].astype(F32) for i in range(3)]
    packed = parts[0] + (parts[1] + parts[2])
    count = 2 * kv_heads
    return [jnp.concatenate([packed[i : i + 1], packed[count + i : count + i + 1]], 1) for i in range(count)]


def pair_kernel(t_ref, a_ref, b_ref, out_ref):
    tok, half = a_ref.shape
    odd = lax.rem(lax.axis_index("seq"), 2) == 1
    out_ref[:tok, :] = jnp.where(odd, t_ref[...], jnp.concatenate([a_ref[...], b_ref[:tok, :]], 1))
    out_ref[tok:, :half] = b_ref[tok:, :]
    out_ref[tok:, half:] = jnp.zeros((b_ref.shape[0] - tok, half), BF16)


def far_kernel(kv_ref, qf_ref, af_ref, bf_ref, qx_ref, px_ref, t_ref):
    seq, head = lax.axis_index("seq"), lax.axis_index("head")
    count = lax.axis_size("seq")
    tok = kv_ref.shape[0]
    kv_cols = kv_ref.shape[1] // 2
    kv_heads = kv_cols // HEAD_SIZE
    straight = jnp.logical_and(jnp.logical_not(causal_mask(tok, head)), seq + FAR < count)
    across = jnp.logical_and(lax.rem(seq, 2) == 1, seq + FAR - 1 < count)
    sources = [
        (own_order(qf_ref, head), jnp.concatenate([af_ref[...], bf_ref[:tok, :]], 1), unpacked(bf_ref, tok, kv_heads), straight),
        (own_order(qx_ref, head), px_ref[:tok, :], unpacked(px_ref, tok, kv_heads), across),
    ]
    scale = LOGIT_SCALE * LOG2E
    for g in range(kv_heads):
        kc, vc = columns(kv_cols, g)
        key, value = kv_ref[:, kc], kv_ref[:, vc]
        dk = jnp.zeros((tok, HEAD_SIZE), F32)
        dv = jnp.zeros((tok, HEAD_SIZE), F32)
        for q_rel, d_rel, stats, keep in sources:
            qg, dg = stacked(q_rel, g), stacked(d_rel, g)
            prob = jnp.exp2(dot(key, qg, 1, 1) * scale - stats[2 * g])
            prob = jnp.where(keep, prob, 0.0).astype(BF16)
            dp = dot(value, dg, 1, 1)
            ds = jnp.where(keep, prob.astype(F32) * (dp - stats[2 * g + 1]), 0.0).astype(BF16)
            dv = dv + dot(prob, dg, 1, 0)
            dk = dk + dot(ds, qg, 1, 0)
        t_ref[:, kc] = dk * LOGIT_SCALE
        t_ref[:, vc] = dv


def sum_kernel(*refs):
    total = refs[0][...].astype(F32)
    for ref in refs[1:-1]:
        total = total + ref[...].astype(F32)
    refs[-1][...] = total.astype(refs[-1].dtype)


def closing_kernel(own_ref, far_ref, hop_ref, pair_ref, near_ref, core_ref, y_ref, dk_ref, dv_ref, proj_ref):
    odd = lax.rem(lax.axis_index("seq"), 2) == 1
    proj_ref[...] = (near_ref[...].astype(F32) + core_ref[...].astype(F32) + y_ref[...].astype(F32)).astype(BF16)
    kept = jnp.where(odd, 0.0, pair_ref[: own_ref.shape[0], :].astype(F32))
    total = own_ref[...] + far_ref[...] + hop_ref[...].astype(F32) + kept
    kv_cols = dk_ref.shape[1]
    dk_ref[...] = total[:, :kv_cols].astype(BF16)
    dv_ref[...] = total[:, kv_cols:].astype(BF16)


def per_device(queries, keys, values, out_weight, out_grad):
    tok, q_cols = queries.shape
    kv_cols = keys.shape[1]
    kv_heads = kv_cols // HEAD_SIZE
    size = tok // 4
    rows = jax.ShapeDtypeStruct((size, out_weight.shape[1]), BF16)
    block = jax.ShapeDtypeStruct((tok, 2 * kv_cols), BF16)
    wide_block = jax.ShapeDtypeStruct((tok, 2 * kv_cols), F32)

    def call(kernel, name, outs, scratch, *operands, cost=SMALL):
        return pl.pallas_call(
            kernel,
            out_shape=outs,
            in_specs=[VMEM] * len(operands),
            out_specs=jax.tree.map(lambda _: VMEM, outs),
            scratch_shapes=scratch,
            compiler_params=pltpu.CompilerParams(vmem_limit_bytes=16 << 20),
            cost_estimate=cost,
            name=name,
        )(*operands)

    def gate(value, *others):
        return lax.optimization_barrier((value, *others))[0]

    kv = call(join_kernel, "join", block, [], keys, values)
    far_sent = call(functools.partial(either_kernel, is_lower), "far_sent", block, [], kv, queries)
    r1 = shifted(kv, 2)
    r2, q_far = far_swapped(lambda: kv, lambda: queries) if lax.axis_size("seq") > 2 * FAR else (far_swapped(*[lambda: far_sent] * 2))
    og_c = swapped(out_grad, "head", 1)
    og_y = swapped(out_grad, "head", 2)
    p0 = swapped(gate(kv, far_sent), "seq", 1)
    half_grad = jax.ShapeDtypeStruct((tok // 2, q_cols), BF16)
    grad_near = call(near_back_kernel, "near_back", half_grad, [], out_grad, og_c, out_weight, cost=LARGE)
    x1 = swapped(gate(r1, grad_near), "seq", 1)
    x2 = swapped(call(functools.partial(either_kernel, is_odd), "pick", block, [], r2, q_far, cost=LARGE), "seq", 1)
    og_yc = swapped(gate(og_y, r2, grad_near), "head", 1)
    first = jax.ShapeDtypeStruct((tok, q_cols // 2), BF16)
    second = jax.ShapeDtypeStruct((tok + 3 * PACK, q_cols // 2), BF16)
    grad_far, sent_first = call(far_back_kernel, "far_back", (half_grad, first), [], og_y, og_yc, out_weight, grad_near,
                                cost=SMALL)

    def down(value):
        return far_swapped(*[lambda: value] * 2)[1]

    far_first = down(sent_first)
    table = jax.ShapeDtypeStruct((8 * pl.cdiv(2 * kv_heads, 8), 2 * tok), F32)
    early = call(
        early_kernel,
        "attend_early",
        (
            jax.ShapeDtypeStruct((kv_heads, 4, tok, 2 * tok), F32),
            table,
            jax.ShapeDtypeStruct((kv_heads, HEAD_SIZE, 2 * tok), F32),
        ),
        [],
        queries, kv, gate(r1, p0), r2, x1,
        cost=SMALL,
    )
    attended, probs, stats, sent_second = call(
        forward_kernel,
        "attend",
        (
            jax.ShapeDtypeStruct((tok, q_cols), BF16),
            jax.ShapeDtypeStruct((kv_heads, 5, tok, 2 * tok), BF16),
            table,
            second,
        ),
        [],
        queries, p0, x2, *early, grad_near, grad_far,
    )
    far_second = down(sent_second)
    near_own, near_core, far_own, far_core = call(
        project_kernel, "project", (rows,) * 4, [], attended, out_weight
    )
    sent = swapped(gate(far_core, far_first), "head", 1)
    t_x = call(across_kernel, "across_grad", block, [], queries, x1, probs, stats, grad_near, gate(grad_far, far_core))
    d1 = swapped(t_x, "seq", 1)
    far_sum = call(sum_kernel, "far_sum", rows, [], far_own, sent)
    from_y = swapped(far_sum, "head", 2)

    query_gradient, t_own, t_1, t_z = call(
        backward_kernel,
        "attend_grad",
        (jax.ShapeDtypeStruct((tok, q_cols), BF16), wide_block, block, block),
        [],
        queries, kv, r1, r2, x1, p0, x2, probs, stats, grad_near, gate(grad_far, far_first),
        cost=LARGE,
    )
    e1 = shifted(call(sum_kernel, "hop_sum", block, [], t_1, d1), -2)
    pair = jax.ShapeDtypeStruct((second.shape[0], q_cols), BF16)
    pair = swapped(call(pair_kernel, "pair", pair, [], t_z, far_first, far_second), "seq", 1)
    from_core = swapped(gate(near_core, far_sum), "head", 1)
    t_far = call(far_kernel, "far_grad", wide_block, [],
                 kv, q_far, far_first, far_second, x2, pair, cost=MEDIUM)

    narrow = jax.ShapeDtypeStruct(keys.shape, BF16)
    key_gradient, value_gradient, projected = call(
        closing_kernel, "closing", (narrow, narrow, rows), [], t_own, t_far, e1, pair, near_own, from_core, from_y
    )
    return (projected, query_gradient, key_gradient, value_gradient)


def solution(mesh):
    return jax.shard_map(
        per_device,
        mesh=mesh,
        in_specs=(
            P("seq", "head"),
            P("seq", "head"),
            P("seq", "head"),
            P("head", None),
            P(("seq", "head"), None),
        ),
        out_specs=(P(("seq", "head"), None), P("seq", "head"), P("seq", "head"), P("seq", "head")),
        check_vma=False,
    )
```
